32 devices in a mesh: gx: 8 (over z, y), gy: 4 (over x, core).
Axes of the slice: x: 2, y: 2, z: 4, core: 2. Of those that a mesh axis runs over, the one named last changes fastest.
Arguments:
- right_side: float32 [128, 512, 128], P('gx', 'gy'), may hold values from -21 to 21
- conductivity: float32 [128, 512, 128], P('gx', 'gy'), may hold values from 0.1 to 10
Outputs:
- pressure: float32 [128, 512, 128], P('gx', 'gy')
- residual: float32 [128, 512, 128], P('gx', 'gy')
The draws below stay inside these ranges and needn't reach their ends.
All inputs are finite; a program needn't handle non-finite values.
Results may differ from the reference program's by a relative error of at most 0.00035.
Values sent between devices are 32-bit elements; how exact they have to be, the bound alone decides.
No kernel may reach another device: no remote copies, remote signals or barrier semaphores. Data moves between devices by JAX's collectives and lax.ppermute only.
A program may use at most 64 MiB of HBM per device.

```python
import math
import jax
import jax.numpy as jnp

CX = 16
CY = 128
NZ = 128
NX = 128
NY = 512
N_GX = 8
N_GY = 4


def draw_right_side(key, part):
    fraction_x = jnp.arange(NX, dtype=jnp.float32) / max(NX - 1, 1)
    scale = jnp.exp(math.log(3.0) * fraction_x)[:, None, None]
    values = jnp.clip(jax.random.normal(key, (NX, NY, NZ), jnp.float32), -7.0, 7.0) * scale
    return values


def level_of(rng, shape, split, smallest, largest):
    factor_of = 1.0
    for dim, parts in split:
        draws = jax.random.uniform(jax.random.fold_in(jax.random.fold_in(rng, 6), dim), (parts,), jnp.float32, smallest / len(split), largest / len(split))
        factor_of = factor_of * jnp.repeat(jnp.exp(draws), shape[dim] // parts).reshape((-1,) + (1,) * (len(shape) - 1 - dim))
    return factor_of


def setup_inputs(seed: int = 0) -> dict:
    splits = jax.random.split(jax.random.key(seed), 3)
    return {
        "right_side": draw_right_side(jax.random.fold_in(splits[2], 71), 0),
        "conductivity": jnp.clip(jnp.exp(math.log(10.0) - 4.6051702 * jax.random.uniform(splits[1], (NX, NY, NZ), jnp.float32) ** level_of(splits[1], (NX, NY, NZ), ((0, 8), (1, 4)), -0.2, 0.2)), 0.1, 10.0),
    }


def face_coeffs(cond_grown):
    middle = cond_grown[1:-1, 1:-1]
    along_z = jnp.pad(middle, ((0, 0), (0, 0), (1, 1)))
    to_west = 0.5 * (middle + cond_grown[:-2, 1:-1])
    to_east = 0.5 * (middle + cond_grown[2:, 1:-1])
    to_south = 0.5 * (middle + cond_grown[1:-1, :-2])
    to_north = 0.5 * (middle + cond_grown[1:-1, 2:])
    to_below = 0.5 * (middle + along_z[:, :, :-2])
    to_above = 0.5 * (middle + along_z[:, :, 2:])
    return (to_west, to_east, to_south, to_north, to_below, to_above)


def neighbour_sum(coeffs, grown):
    padded = jnp.pad(grown, ((0, 0), (0, 0), (1, 1)))
    to_west, to_east, to_south, to_north, to_below, to_above = coeffs
    summed = to_west * padded[:-2, 1:-1, 1:-1] + to_east * padded[2:, 1:-1, 1:-1]
    summed = summed + to_south * padded[1:-1, :-2, 1:-1] + to_north * padded[1:-1, 2:, 1:-1]
    summed = summed + to_below * padded[1:-1, 1:-1, :-2] + to_above * padded[1:-1, 1:-1, 2:]
    return summed


def pad_plane(values):
    return jnp.pad(values, ((1, 1), (1, 1), (0, 0)))


def box_count(lower_idx, upper_idx, cell_len, devices):
    counted = jnp.zeros(lower_idx.shape, jnp.float32)
    for offset_q in (-1, 0, 1):
        owner = jnp.floor_divide(jnp.maximum(lower_idx, 0), cell_len) + offset_q
        inside = (owner >= 0) & (owner < devices)
        inside = inside & (owner * cell_len - 2 <= lower_idx) & (upper_idx <= owner * cell_len + cell_len + 1)
        counted = counted + inside.astype(jnp.float32)
    return counted


def reference(right_side, conductivity):
    coeffs = face_coeffs(pad_plane(conductivity))
    to_west, to_east, to_south, to_north, to_below, to_above = coeffs
    diagonal = to_west + to_east + to_south + to_north + to_below + to_above
    initial = right_side / diagonal
    index_x = jnp.arange(NX, dtype=jnp.int32)
    index_y = jnp.arange(NY, dtype=jnp.int32)
    own_x = box_count(index_x, index_x, CX, N_GX)[:, None, None]
    west_x = box_count(index_x - 1, index_x, CX, N_GX)[:, None, None]
    east_x = box_count(index_x, index_x + 1, CX, N_GX)[:, None, None]
    own_y = box_count(index_y, index_y, CY, N_GY)[None, :, None]
    south_y = box_count(index_y - 1, index_y, CY, N_GY)[None, :, None]
    north_y = box_count(index_y, index_y + 1, CY, N_GY)[None, :, None]
    own_count = own_x * own_y
    padded = jnp.pad(initial, 1)
    summed = own_count * right_side
    summed = summed + west_x * own_y * to_west * padded[:-2, 1:-1, 1:-1]
    summed = summed + east_x * own_y * to_east * padded[2:, 1:-1, 1:-1]
    summed = summed + own_x * south_y * to_south * padded[1:-1, :-2, 1:-1]
    summed = summed + own_x * north_y * to_north * padded[1:-1, 2:, 1:-1]
    summed = summed + own_count * (to_below * padded[1:-1, 1:-1, :-2] + to_above * padded[1:-1, 1:-1, 2:])
    precond = summed / diagonal
    image = diagonal * precond - neighbour_sum(coeffs, pad_plane(precond))
    inner_rz = jnp.sum(right_side * precond)
    inner_pq = jnp.sum(precond * image)
    alpha = inner_rz / inner_pq
    return alpha * precond, right_side - alpha * image
```

```python
import jax
import jax.numpy as jnp
from jax import lax
from jax.experimental import pallas as pl
from jax.experimental.pallas import tpu as pltpu
from jax.sharding import PartitionSpec as P

F32 = jnp.float32
HALO = 8
LOW = 2 * HALO
TINY = 1e-30
ANY = pl.BlockSpec(memory_space=pl.ANY)
VMEM = pl.BlockSpec(memory_space=pltpu.VMEM)


def params():
    return pltpu.CompilerParams(vmem_limit_bytes=48 << 20)


def shape(*dims):
    return jax.ShapeDtypeStruct(dims, F32)


def ordered(first_pair_partner, count):
    return [(i, first_pair_partner(i) % count) for i in range(count)]


def swap_even(value, axis):
    count = lax.axis_size(axis)
    return lax.ppermute(value, axis, ordered(lambda i: i ^ 1, count))


def swap_odd(value, axis):
    count = lax.axis_size(axis)
    return lax.ppermute(value, axis, ordered(lambda i: ((i + 1) ^ 1) - 1, count))


def place(axis):
    index, count = lax.axis_index(axis), lax.axis_size(axis)
    odd = lax.rem(index, 2) == 1
    has_low = (index > 0).astype(F32)
    has_high = (index < count - 1).astype(F32)
    return odd, has_low, has_high


def z_sum(value):
    lane = lax.broadcasted_iota(jnp.int32, value.shape, 1)
    last = value.shape[1] - 1
    below = jnp.where(lane > 0, pltpu.roll(value, 1, 1), 0.0)
    above = jnp.where(lane < last, pltpu.roll(value, last, 1), 0.0)
    return below + above


def pack_kernel(cond, resid, x_even, x_odd, y_even, y_odd, sem):
    layers, rows, _ = cond.shape
    copies = []
    for axis, outs in (("gx", (x_even, x_odd)), ("gy", (y_even, y_odd))):
        odd = lax.rem(lax.axis_index(axis), 2)
        for out, high in zip(outs, (1 - odd, odd)):
            if axis == "gx":
                two = pl.ds(high * (layers - 2), 2)
                one = pl.ds(high * (layers - 1), 1)
                copies.append((cond.at[two], out.at[pl.ds(0, 2)]))
                copies.append((resid.at[one], out.at[pl.ds(2, 1)]))
            else:
                tile = pl.ds(pl.multiple_of(high * (rows - HALO), HALO), HALO)
                copies.append((cond.at[:, tile], out.at[:, pl.ds(0, HALO)]))
                copies.append((resid.at[:, tile], out.at[:, pl.ds(HALO, HALO)]))
    started = [
        pltpu.make_async_copy(source, target, sem.at[i])
        for i, (source, target) in enumerate(copies)
    ]
    for copy in started:
        copy.start()
    for copy in started:
        copy.wait()


def pack(cond, resid):
    layers, rows, lanes = cond.shape
    x_out, y_out = shape(3, rows, lanes), shape(layers, 2 * HALO, lanes)
    return pl.pallas_call(
        pack_kernel,
        out_shape=(x_out, x_out, y_out, y_out),
        in_specs=[ANY, ANY],
        out_specs=(ANY, ANY, ANY, ANY),
        scratch_shapes=[pltpu.SemaphoreType.DMA((8,))],
        compiler_params=params(),
        name="pack",
    )(cond, resid)


def y_tiles(y_even, y_odd, layer, part):
    odd, has_low, has_high = place("gy")
    rows = pl.ds(part * HALO, HALO)
    first, second = y_even[layer, rows], y_odd[layer, rows]
    south = jnp.where(odd, first, second) * has_low
    north = jnp.where(odd, second, first) * has_high
    return south, north


def edge_kernel(u_low, u_high, r_low, r_high, y_even, y_odd, t_even, t_odd, grown):
    layers, rows = y_even.shape[0], u_low.shape[1]
    odd = place("gx")[0]
    end = HALO + rows
    sends = []
    for side in range(2):
        u_side, r_side = ((u_low, r_low), (u_high, r_high))[side]
        locals_ = ((0, 1, 2), (3, 2, 1))[side]
        layer_of = ((0, 1, 2), (layers - 1, layers - 2, layers - 3))[side]
        south, north = y_tiles(y_even, y_odd, layer_of[1], 0)
        grown[side, 0:HALO] = south
        grown[side, HALO:end] = u_side[locals_[1]]
        grown[side, end : end + HALO] = north
        middle = u_side[locals_[1]]
        edge = u_side[locals_[0]]
        total = 6.0 * middle + edge + u_side[locals_[2]] + z_sum(middle)
        total = total + grown[side, HALO - 1 : end - 1] + grown[side, HALO + 1 : end + 1]
        term = (edge + middle) * (2.0 * r_side[0] / total)
        edge_south, edge_north = y_tiles(y_even, y_odd, layer_of[0], 0)
        r_south, r_north = y_tiles(y_even, y_odd, layer_of[0], 1)
        corner = jnp.concatenate(
            [
                edge_south[HALO - 1 : HALO],
                edge_south[HALO - 2 : HALO - 1],
                south[HALO - 1 : HALO],
                r_south[HALO - 1 : HALO],
                edge_north[0:1],
                edge_north[1:2],
                north[0:1],
                r_north[0:1],
            ],
            axis=0,
        )
        sends.append((term, corner))
    (t_low, c_low), (t_high, c_high) = sends
    t_even[0:rows] = jnp.where(odd, t_low, t_high)
    t_even[rows : rows + 8] = jnp.where(odd, c_low, c_high)
    t_odd[0:rows] = jnp.where(odd, t_high, t_low)
    t_odd[rows : rows + 8] = jnp.where(odd, c_high, c_low)


def edge_terms(cond, resid, y_even, y_odd):
    layers, rows, lanes = cond.shape
    four, one = (4, rows, lanes), (1, rows, lanes)
    whole = pl.BlockSpec(y_even.shape, lambda i: (0, 0, 0))
    out = pl.BlockSpec((rows + 8, lanes), lambda i: (0, 0))
    return pl.pallas_call(
        edge_kernel,
        grid=(1,),
        out_shape=(shape(rows + 8, lanes), shape(rows + 8, lanes)),
        in_specs=[
            pl.BlockSpec(four, lambda i: (0, 0, 0)),
            pl.BlockSpec(four, lambda i: (layers // 4 - 1, 0, 0)),
            pl.BlockSpec(one, lambda i: (1, 0, 0)),
            pl.BlockSpec(one, lambda i: (layers - 2, 0, 0)),
            whole,
            whole,
        ],
        out_specs=(out, out),
        scratch_shapes=[pltpu.VMEM((2, rows + 2 * HALO, lanes), F32)],
        compiler_params=params(),
        name="edge_terms",
    )(cond, cond, resid, resid, y_even, y_odd)


def row_chunks(rows):
    total = rows + 2 * HALO
    step = total // 3 if total % 24 == 0 else total
    return [(HALO + i * step, step) for i in range(total // step)]


def own_chunks(rows):
    step = 32 if rows % 32 == 0 else rows
    return [(LOW + i * step, step) for i in range(rows // step)]


def fill_rows(masks, rows):
    _, has_low, has_high = place("gy")
    row = lax.broadcasted_iota(jnp.int32, masks.shape[1:], 0) - LOW
    inside = jnp.where(row < 0, has_low, jnp.where(row >= rows, has_high, 1.0))
    near_low, near_high = row < 2, row >= rows - 2
    count = jnp.where(near_low, 1.0 + has_low, jnp.where(near_high, 1.0 + has_high, 1.0))
    masks[0] = inside
    masks[1] = count
    masks[2] = jnp.where(row == rows - 2, 1.0 / (1.0 + has_high), 1.0)
    masks[3] = jnp.where(row == 1, 1.0 / (1.0 + has_low), 1.0)


def is_plain(start, size, rows):
    return start >= LOW + 2 and start + size <= LOW + rows - 2


def eight(value):
    return jnp.sum(value.reshape(value.shape[0] // 8, 8, value.shape[1]), axis=0)


def inner_kernel(
    cond, resid, y_even, y_odd,
    p_out, i_out, e_u, e_r, e_v, e_i, e_d, e_p, sums,
    u, r, inv, v, w, d, p, q, masks, sem,
):
    layers, rows = cond.shape[0], cond.shape[1]
    own = pl.ds(LOW, rows)
    loads = [
        pltpu.make_async_copy(cond, u.at[:, own], sem.at[0]),
        pltpu.make_async_copy(resid, r.at[:, own], sem.at[1]),
    ]
    for copy in loads:
        copy.start()
    fill_rows(masks, rows)

    def halo(k, carry):
        for part, target in enumerate((u, r)):
            south, north = y_tiles(y_even, y_odd, k, part)
            target[k, HALO:LOW] = south
            target[k, LOW + rows : LOW + rows + HALO] = north
        return carry

    lax.fori_loop(0, layers, halo, 0)
    for copy in loads:
        copy.wait()
    chunks = row_chunks(rows)

    def first(k, carry):
        for start, size in chunks:
            here = slice(start, start + size)
            down, up = slice(start - 1, start + size - 1), slice(start + 1, start + size + 1)
            mid = u[k, here]
            total = 6.0 * mid + u[k - 1, here] + u[k + 1, here]
            total = total + u[k, down] + u[k, up] + z_sum(mid)
            inverse = 1.0 / jnp.maximum(total, TINY)
            if not is_plain(start, size, rows):
                inverse = inverse * masks[0, here]
            value = 2.0 * r[k, here] * inverse
            d[k, here] = total
            inv[k, here] = inverse
            v[k, here] = value
            w[k, here] = mid * value
        return carry

    lax.fori_loop(1, layers - 1, first, 0)

    def second(k, carry):
        for start, size in chunks:
            here = slice(start, start + size)
            down, up = slice(start - 1, start + size - 1), slice(start + 1, start + size + 1)
            mid = u[k, here]
            total = 2.0 * r[k, here]
            total = total + mid * (v[k - 1, here] + v[k + 1, here] + z_sum(v[k, here]))
            total = total + (w[k - 1, here] + w[k + 1, here] + z_sum(w[k, here]))
            south = mid * v[k, down] + w[k, down]
            north = mid * v[k, up] + w[k, up]
            if is_plain(start, size, rows):
                value = inv[k, here] * (total + south + north)
            else:
                total = total + masks[2, here] * south + masks[3, here] * north
                value = masks[1, here] * inv[k, here] * total
            p[k, here] = value
            q[k, here] = mid * value
        return carry

    lax.fori_loop(2, layers - 2, second, 0)

    def third(k, carry):
        rz, pq = carry
        for start, size in own_chunks(rows):
            here = slice(start, start + size)
            down, up = slice(start - 1, start + size - 1), slice(start + 1, start + size + 1)
            mid = p[k, here]
            around = p[k - 1, here] + p[k + 1, here] + p[k, down] + p[k, up] + z_sum(mid)
            scaled = q[k - 1, here] + q[k + 1, here] + q[k, down] + q[k, up]
            scaled = scaled + z_sum(q[k, here])
            image = d[k, here] * mid - u[k, here] * around - scaled
            i_out[k, start - LOW : start - LOW + size] = image
            p_out[k, start - LOW : start - LOW + size] = mid
            rz = rz + eight(r[k, here] * mid)
            pq = pq + eight(mid * image)
        return rz, pq

    zero = jnp.zeros((8, u.shape[2]), F32)
    rz, pq = lax.fori_loop(3, layers - 3, third, (zero, zero))
    sums[0] = rz
    sums[1] = pq
    full = slice(HALO, LOW + rows + HALO)
    for side in range(2):
        order = (0, 1, 2, 3) if side == 0 else tuple(layers - 1 - k for k in range(4))
        for k in range(4):
            e_u[side, k, full] = u[order[k], full]
        for k in range(3):
            e_r[side, k, full] = r[order[k], full]
        for k in range(2):
            e_v[side, k, full] = v[order[k + 1], full]
            e_d[side, k, full] = d[order[k + 1], full]
            e_p[side, k, full] = p[order[k + 2], full]
        e_i[side, 0, full] = inv[order[1], full]


def inner(cond, resid, y_even, y_odd):
    layers, rows, lanes = cond.shape
    grown = rows + 4 * HALO
    field = pltpu.VMEM((layers, grown, lanes), F32)

    def edge(count):
        return shape(2, count, grown, lanes)

    outs = (
        shape(layers, rows, lanes), shape(layers, rows, lanes),
        edge(4), edge(3), edge(2), edge(1), edge(2), edge(2), shape(2, 8, lanes),
    )
    return pl.pallas_call(
        inner_kernel,
        out_shape=outs,
        in_specs=[ANY, ANY, VMEM, VMEM],
        out_specs=(VMEM,) * len(outs),
        scratch_shapes=[field] * 8
        + [pltpu.VMEM((4, grown, lanes), F32), pltpu.SemaphoreType.DMA((2,))],
        compiler_params=params(),
        name="inner",
    )(cond, resid, y_even, y_odd)


def outer_kernel(
    p_in, i_in, e_u, e_r, e_v, e_i, e_d, e_p, sums, x_even, x_odd, t_even, t_odd,
    p_out, i_out, total_out,
    u, r, v, w, p, q, d, t, masks,
):
    layers, rows = p_in.shape[0], p_in.shape[1]
    odd, has_low, has_high = place("gx")
    fill_rows(masks, rows)
    own = slice(LOW, LOW + rows)
    zero = jnp.zeros((8, u.shape[2]), F32)
    rz, pq = sums[0], sums[1]
    chunks = row_chunks(rows)
    for side in range(2):
        has = (has_low, has_high)[side]
        pick = jnp.logical_xor(odd, side == 1)
        twice = 1.0 + has

        def arrived(first, second):
            return jnp.where(pick, first, second) * has

        near, far = (1, 0) if side == 0 else (0, 1)
        for slot, source in ((0, far), (1, near)):
            u[slot, own] = arrived(x_even[source], x_odd[source])
        r[own] = arrived(x_even[2], x_odd[2])
        t[own] = arrived(t_even[0:rows], t_odd[0:rows])
        corner = arrived(t_even[rows : rows + 8], t_odd[rows : rows + 8])
        low, high = slice(HALO, LOW), slice(LOW + rows, LOW + rows + HALO)
        row = lax.broadcasted_iota(jnp.int32, zero.shape, 0)

        def one(k):
            return jnp.broadcast_to(corner[k : k + 1], zero.shape)

        u[1, low] = jnp.where(row == 7, one(0), jnp.where(row == 6, one(1), 0.0))
        u[0, low] = jnp.where(row == 7, one(2), 0.0)
        r[low] = jnp.where(row == 7, one(3), 0.0)
        u[1, high] = jnp.where(row == 0, one(4), jnp.where(row == 1, one(5), 0.0))
        u[0, high] = jnp.where(row == 0, one(6), 0.0)
        r[high] = jnp.where(row == 0, one(7), 0.0)
        t[low] = zero
        t[high] = zero

        for start, size in chunks:
            here = slice(start, start + size)
            down, up = slice(start - 1, start + size - 1), slice(start + 1, start + size + 1)
            inside = masks[0, here]
            mid, edge = u[1, here], e_u[side, 0, here]
            total = 6.0 * mid + u[0, here] + edge + u[1, down] + u[1, up] + z_sum(mid)
            inverse = has * inside / jnp.maximum(total, TINY)
            value = 2.0 * r[here] * inverse
            d[1, here] = inverse
            v[0, here] = value
            w[0, here] = mid * value
            total = 6.0 * edge + mid + e_u[side, 1, here]
            total = total + e_u[side, 0, down] + e_u[side, 0, up] + z_sum(edge)
            inverse = inside / jnp.maximum(total, TINY)
            value = 2.0 * e_r[side, 0, here] * inverse
            d[0, here] = total
            d[2, here] = inverse
            v[1, here] = value
            w[1, here] = edge * value

        for start, size in chunks:
            here = slice(start, start + size)
            down, up = slice(start - 1, start + size - 1), slice(start + 1, start + size + 1)
            plain = is_plain(start, size, rows)

            def finish(mid, total, south, north, inverse, slot, twice):
                if plain:
                    value = twice * inverse * (total + south + north)
                else:
                    total = total + masks[2, here] * south + masks[3, here] * north
                    value = twice * masks[1, here] * inverse * total
                p[slot, here] = value
                q[slot, here] = mid * value

            mid = u[1, here]
            total = 2.0 * r[here] + t[here]
            total = total + mid * (v[1, here] + z_sum(v[0, here]))
            total = total + w[1, here] + z_sum(w[0, here])
            south = mid * v[0, down] + w[0, down]
            north = mid * v[0, up] + w[0, up]
            finish(mid, total, south, north, d[1, here], 0, twice)

            mid, next_u = e_u[side, 0, here], e_u[side, 1, here]
            next_v = e_v[side, 0, here]
            total = 2.0 * e_r[side, 0, here]
            total = total + mid * (v[0, here] + next_v + z_sum(v[1, here]))
            total = total + w[0, here] + next_u * next_v + z_sum(w[1, here])
            south = mid * v[1, down] + w[1, down]
            north = mid * v[1, up] + w[1, up]
            finish(mid, total, south, north, d[2, here], 1, twice)

            inner_v = e_v[side, 1, here]
            total = 2.0 * e_r[side, 1, here]
            total = total + next_u * (v[1, here] + z_sum(next_v))
            total = total + w[1, here] + z_sum(next_u * next_v)
            total = total + (next_u * inner_v + e_u[side, 2, here] * inner_v) / twice
            south = (next_u + e_u[side, 1, down]) * e_v[side, 0, down]
            north = (next_u + e_u[side, 1, up]) * e_v[side, 0, up]
            finish(next_u, total, south, north, e_i[side, 0, here], 2, twice)

        for start, size in own_chunks(rows):
            here = slice(start, start + size)
            down, up = slice(start - 1, start + size - 1), slice(start + 1, start + size + 1)
            out_rows = slice(start - LOW, start - LOW + size)
            for k in range(3):
                layer = k if side == 0 else layers - 1 - k
                mid_u = e_u[side, k, here]
                if k < 2:
                    mid = p[k + 1, here]
                    near_y = p[k + 1, down] + p[k + 1, up]
                    near_q = q[k + 1, down] + q[k + 1, up]
                    mid_q = q[k + 1, here]
                    before_p, before_q = p[k, here], q[k, here]
                    if k == 0:
                        after_p, after_q = p[2, here], q[2, here]
                    else:
                        after_p = e_p[side, 0, here]
                        after_q = e_u[side, 2, here] * after_p
                else:
                    mid = e_p[side, 0, here]
                    mid_q = mid_u * mid
                    low_p, high_p = e_p[side, 0, down], e_p[side, 0, up]
                    near_y = low_p + high_p
                    near_q = e_u[side, 2, down] * low_p + e_u[side, 2, up] * high_p
                    before_p, before_q = p[2, here], q[2, here]
                    after_p = e_p[side, 1, here]
                    after_q = None
                around = before_p + after_p + near_y + z_sum(mid)
                if after_q is None:
                    after_q = e_u[side, 3, here] * after_p
                scaled = before_q + after_q + near_q + z_sum(mid_q)
                total = d[0, here] if k == 0 else e_d[side, k - 1, here]
                image = total * mid - mid_u * around - scaled
                p_out[layer, out_rows] = mid
                i_out[layer, out_rows] = image
                rz = rz + eight(e_r[side, k, here] * mid)
                pq = pq + eight(mid * image)
    total_out[0:1] = jnp.broadcast_to(jnp.sum(rz, keepdims=True), (1, zero.shape[1]))
    total_out[1:2] = jnp.broadcast_to(jnp.sum(pq, keepdims=True), (1, zero.shape[1]))


def outer(found, x_even, x_odd, t_even, t_odd):
    p_in = found[0]
    layers, rows, lanes = p_in.shape
    grown = rows + 4 * HALO

    def field(*lead):
        return pltpu.VMEM((*lead, grown, lanes), F32)

    return pl.pallas_call(
        outer_kernel,
        out_shape=(shape(layers, rows, lanes), shape(layers, rows, lanes), shape(2, lanes)),
        in_specs=[VMEM] * 13,
        out_specs=(VMEM, VMEM, VMEM),
        scratch_shapes=[
            field(2), field(), field(2), field(2), field(3), field(3), field(3), field(), field(4),
        ],
        input_output_aliases={0: 0, 1: 1},
        compiler_params=params(),
        name="outer",
    )(*found, x_even, x_odd, t_even, t_odd)


def power_of_two(count):
    return count & (count - 1) == 0


def sum_everywhere(value):
    count_x, count_y = lax.axis_size("gx"), lax.axis_size("gy")
    if not (power_of_two(count_x) and power_of_two(count_y)):
        return lax.psum(value, ("gx", "gy"))
    low = 1 if count_y > 1 else 0
    steps = [(0, 1 << bit | low) for bit in range(count_y.bit_length() - 1)]
    steps += [(1 << bit, low) for bit in range(count_x.bit_length() - 1)]
    for step_x, step_y in steps:
        pairs = [
            (x * count_y + y, (x ^ step_x) * count_y + (y ^ step_y))
            for x in range(count_x)
            for y in range(count_y)
        ]
        value = value + lax.ppermute(value, ("gx", "gy"), pairs)
    return value


def on_device(right_side, conductivity):
    x_even, x_odd, y_even, y_odd = pack(conductivity, right_side)
    x_even = swap_even(x_even, "gx")
    y_even = swap_even(y_even, "gy")
    y_odd = swap_odd(y_odd, "gy")
    x_odd = swap_odd(x_odd, "gx")
    t_even, t_odd = edge_terms(conductivity, right_side, y_even, y_odd)
    t_even = swap_even(t_even, "gx")
    t_odd = swap_odd(t_odd, "gx")
    found = inner(conductivity, right_side, y_even, y_odd)
    precond, image, sums = outer(found, x_even, x_odd, t_even, t_odd)
    sums = sum_everywhere(sums)
    half_alpha = sums[0, 0] / sums[1, 0]
    return (2.0 * half_alpha) * precond, right_side - half_alpha * image


def solution(mesh):
    in_specs = (P("gx", "gy", None), P("gx", "gy", None))
    out_specs = (P("gx", "gy", None), P("gx", "gy", None))
    return jax.shard_map(
        on_device, mesh=mesh, in_specs=in_specs, out_specs=out_specs, check_vma=False
    )
```

```python
import jax
import jax.numpy as jnp
from jax import lax
from jax.experimental import pallas as pl
from jax.experimental.pallas import tpu as pltpu
from jax.sharding import PartitionSpec as P

F32 = jnp.float32
HALO = 8
LOW = 2 * HALO
TINY = 1e-30
HBM = pl.BlockSpec(memory_space=pltpu.HBM)
VMEM = pl.BlockSpec(memory_space=pltpu.VMEM)


def params(mebibytes):
    return pltpu.CompilerParams(vmem_limit_bytes=mebibytes << 20)


def shape(*dims):
    return jax.ShapeDtypeStruct(dims, F32)


def ordered(first_pair_partner, count):
    return [(i, first_pair_partner(i) % count) for i in range(count)]


def swap_even(value, axis):
    count = lax.axis_size(axis)
    return lax.ppermute(value, axis, ordered(lambda i: i ^ 1, count))


def swap_odd(value, axis):
    count = lax.axis_size(axis)
    return lax.ppermute(value, axis, ordered(lambda i: ((i + 1) ^ 1) - 1, count))


def place(axis):
    index, count = lax.axis_index(axis), lax.axis_size(axis)
    odd = lax.rem(index, 2) == 1
    has_low = (index > 0).astype(F32)
    has_high = (index < count - 1).astype(F32)
    return odd, has_low, has_high


def z_sum(value):
    lane = lax.broadcasted_iota(jnp.int32, value.shape, 1)
    last = value.shape[1] - 1
    below = jnp.where(lane > 0, pltpu.roll(value, 1, 1), 0.0)
    above = jnp.where(lane < last, pltpu.roll(value, last, 1), 0.0)
    return below + above


def pack_kernel(cond, resid, x_even, y_even, y_odd, u, r, sem):
    layers, rows, _ = cond.shape
    own = pl.ds(LOW, rows)
    high = 1 - lax.rem(lax.axis_index("gx"), 2)
    two = pl.ds(high * (layers - 2), 2)
    one = pl.ds(high * (layers - 1), 1)
    copies = [
        (cond.at[two], x_even.at[pl.ds(0, 2)]),
        (resid.at[one], x_even.at[pl.ds(2, 1)]),
    ]
    odd = lax.rem(lax.axis_index("gy"), 2)
    for out, high in ((y_even, 1 - odd), (y_odd, odd)):
        tile = pl.ds(pl.multiple_of(high * (rows - HALO), HALO), HALO)
        copies.append((cond.at[:, tile], out.at[:, pl.ds(0, HALO)]))
        copies.append((resid.at[:, tile], out.at[:, pl.ds(HALO, HALO)]))
    copies += [(cond, u.at[:, own]), (resid, r.at[:, own])]
    started = [
        pltpu.make_async_copy(source, target, sem.at[i])
        for i, (source, target) in enumerate(copies)
    ]
    for copy in started:
        copy.start()
    for copy in started:
        copy.wait()


def pack(cond, resid):
    layers, rows, lanes = cond.shape
    y_out = shape(layers, 2 * HALO, lanes)
    grown = shape(layers, rows + 4 * HALO, lanes)
    return pl.pallas_call(
        pack_kernel,
        out_shape=(shape(3, rows, lanes), y_out, y_out, grown, grown),
        in_specs=[HBM, HBM],
        out_specs=(VMEM,) * 5,
        scratch_shapes=[pltpu.SemaphoreType.DMA((8,))],
        compiler_params=params(1),
        name="pack",
    )(
        pltpu.with_memory_space_constraint(cond, pltpu.HBM),
        pltpu.with_memory_space_constraint(resid, pltpu.HBM),
    )


def y_tiles(y_even, y_odd, layer, part):
    odd, has_low, has_high = place("gy")
    rows = pl.ds(part * HALO, HALO)
    first, second = y_even[layer, rows], y_odd[layer, rows]
    south = jnp.where(odd, first, second) * has_low
    north = jnp.where(odd, second, first) * has_high
    return south, north


def edge_kernel(u, r, y_even, y_odd, t_even, x_odd, grown):
    layers, rows = u.shape[0], u.shape[1] - 4 * HALO
    odd = place("gx")[0]
    end = HALO + rows
    own = slice(LOW, LOW + rows)
    sends = []
    for side in range(2):
        edge, mid, far = ((0, 1, 2), (layers - 1, layers - 2, layers - 3))[side]
        south, north = y_tiles(y_even, y_odd, mid, 0)
        middle = u[mid, own]
        grown[side, 0:HALO] = south
        grown[side, HALO:end] = middle
        grown[side, end : end + HALO] = north
        total = 6.0 * middle + u[edge, own] + u[far, own] + z_sum(middle)
        total = total + grown[side, HALO - 1 : end - 1] + grown[side, HALO + 1 : end + 1]
        term = (u[edge, own] + middle) * (2.0 * r[mid, own] / total)
        edge_south, edge_north = y_tiles(y_even, y_odd, edge, 0)
        r_south, r_north = y_tiles(y_even, y_odd, edge, 1)
        corner = jnp.concatenate(
            [
                edge_south[HALO - 1 : HALO],
                edge_south[HALO - 2 : HALO - 1],
                south[HALO - 1 : HALO],
                r_south[HALO - 1 : HALO],
                edge_north[0:1],
                edge_north[1:2],
                north[0:1],
                r_north[0:1],
            ],
            axis=0,
        )
        sends.append((term, corner))
    (t_low, c_low), (t_high, c_high) = sends
    t_even[0:rows] = jnp.where(odd, t_low, t_high)
    t_even[rows : rows + 8] = jnp.where(odd, c_low, c_high)
    x_odd[0:rows] = jnp.where(odd, u[layers - 2, own], u[0, own])
    x_odd[rows : 2 * rows] = jnp.where(odd, u[layers - 1, own], u[1, own])
    x_odd[2 * rows : 3 * rows] = jnp.where(odd, r[layers - 1, own], r[0, own])
    x_odd[3 * rows : 4 * rows] = jnp.where(odd, t_high, t_low)
    x_odd[4 * rows : 4 * rows + 8] = jnp.where(odd, c_high, c_low)


def edge_terms(u, r, y_even, y_odd):
    rows, lanes = u.shape[1] - 4 * HALO, u.shape[2]
    return pl.pallas_call(
        edge_kernel,
        out_shape=(shape(rows + 8, lanes), shape(4 * rows + 8, lanes)),
        in_specs=[VMEM] * 4,
        out_specs=(VMEM, VMEM),
        scratch_shapes=[pltpu.VMEM((2, rows + 2 * HALO, lanes), F32)],
        compiler_params=params(2),
        name="edge_terms",
    )(u, r, y_even, y_odd)


def row_chunks(rows):
    total = rows + 2 * HALO
    step = total // 3 if total % 24 == 0 else total
    return [(HALO + i * step, step) for i in range(total // step)]


def own_chunks(rows):
    step = 32 if rows % 32 == 0 else rows
    return [(LOW + i * step, step) for i in range(rows // step)]


def fill_rows(masks, rows):
    _, has_low, has_high = place("gy")
    row = lax.broadcasted_iota(jnp.int32, masks.shape[1:], 0) - LOW
    inside = jnp.where(row < 0, has_low, jnp.where(row >= rows, has_high, 1.0))
    near_low, near_high = row < 2, row >= rows - 2
    count = jnp.where(near_low, 1.0 + has_low, jnp.where(near_high, 1.0 + has_high, 1.0))
    masks[0] = inside
    masks[1] = count
    masks[2] = jnp.where(row == rows - 2, 1.0 / (1.0 + has_high), 1.0)
    masks[3] = jnp.where(row == 1, 1.0 / (1.0 + has_low), 1.0)


def is_plain(start, size, rows):
    return start >= LOW + 2 and start + size <= LOW + rows - 2


def eight(value):
    return jnp.sum(value.reshape(value.shape[0] // 8, 8, value.shape[1]), axis=0)


def inner_kernel(
    u_in, r_in, y_even, y_odd,
    u, r, p_out, i_out, e_v, e_i, e_d, e_p, sums,
    inv, v, w, d, p, q, masks,
):
    layers, rows = p_out.shape[0], p_out.shape[1]
    fill_rows(masks, rows)

    def halo(k, carry):
        for part, target in enumerate((u, r)):
            south, north = y_tiles(y_even, y_odd, k, part)
            target[k, HALO:LOW] = south
            target[k, LOW + rows : LOW + rows + HALO] = north
        return carry

    lax.fori_loop(0, layers, halo, 0)
    chunks = row_chunks(rows)

    def first(k, carry):
        for start, size in chunks:
            here = slice(start, start + size)
            down, up = slice(start - 1, start + size - 1), slice(start + 1, start + size + 1)
            mid = u[k, here]
            total = 6.0 * mid + u[k - 1, here] + u[k + 1, here]
            total = total + u[k, down] + u[k, up] + z_sum(mid)
            inverse = 1.0 / jnp.maximum(total, TINY)
            if not is_plain(start, size, rows):
                inverse = inverse * masks[0, here]
            value = 2.0 * r[k, here] * inverse
            d[k, here] = total
            inv[k, here] = inverse
            v[k, here] = value
            w[k, here] = mid * value
        return carry

    lax.fori_loop(1, layers - 1, first, 0)

    def second(k, carry):
        for start, size in chunks:
            here = slice(start, start + size)
            down, up = slice(start - 1, start + size - 1), slice(start + 1, start + size + 1)
            mid = u[k, here]
            total = 2.0 * r[k, here]
            total = total + mid * (v[k - 1, here] + v[k + 1, here] + z_sum(v[k, here]))
            total = total + (w[k - 1, here] + w[k + 1, here] + z_sum(w[k, here]))
            south = mid * v[k, down] + w[k, down]
            north = mid * v[k, up] + w[k, up]
            if is_plain(start, size, rows):
                value = inv[k, here] * (total + south + north)
            else:
                total = total + masks[2, here] * south + masks[3, here] * north
                value = masks[1, here] * inv[k, here] * total
            p[k, here] = value
            q[k, here] = mid * value
        return carry

    lax.fori_loop(2, layers - 2, second, 0)

    def third(k, carry):
        rz, pq = carry
        for start, size in own_chunks(rows):
            here = slice(start, start + size)
            down, up = slice(start - 1, start + size - 1), slice(start + 1, start + size + 1)
            mid = p[k, here]
            around = p[k - 1, here] + p[k + 1, here] + p[k, down] + p[k, up] + z_sum(mid)
            scaled = q[k - 1, here] + q[k + 1, here] + q[k, down] + q[k, up]
            scaled = scaled + z_sum(q[k, here])
            image = d[k, here] * mid - u[k, here] * around - scaled
            i_out[k, start - LOW : start - LOW + size] = image
            p_out[k, start - LOW : start - LOW + size] = mid
            rz = rz + eight(r[k, here] * mid)
            pq = pq + eight(mid * image)
        return rz, pq

    zero = jnp.zeros((8, u.shape[2]), F32)
    rz, pq = lax.fori_loop(3, layers - 3, third, (zero, zero))
    sums[0] = rz
    sums[1] = pq
    full = slice(HALO, LOW + rows + HALO)
    for side in range(2):
        order = (0, 1, 2, 3) if side == 0 else tuple(layers - 1 - k for k in range(4))
        for k in range(2):
            e_v[side, k, full] = v[order[k + 1], full]
            e_d[side, k, full] = d[order[k + 1], full]
            e_p[side, k, full] = p[order[k + 2], full]
        e_i[side, 0, full] = inv[order[1], full]


def inner(u, r, y_even, y_odd):
    layers, grown, lanes = u.shape
    rows = grown - 4 * HALO
    field = pltpu.VMEM((layers, grown, lanes), F32)

    def edge(count):
        return shape(2, count, grown, lanes)

    own, ext = shape(layers, rows, lanes), shape(layers, grown, lanes)
    outs = (ext, ext, own, own, edge(2), edge(1), edge(2), edge(2), shape(2, 8, lanes))
    return pl.pallas_call(
        inner_kernel,
        out_shape=outs,
        in_specs=[VMEM] * 4,
        out_specs=(VMEM,) * len(outs),
        scratch_shapes=[field] * 6 + [pltpu.VMEM((4, grown, lanes), F32)],
        input_output_aliases={0: 0, 1: 1},
        compiler_params=params(12),
        cost_estimate=pl.CostEstimate(flops=4_000_000_000, transcendentals=0, bytes_accessed=1),
        name="inner",
    )(u, r, y_even, y_odd)


def outer_kernel(
    b_u, b_r, p_in, i_in, e_v, e_i, e_d, e_p, sums, x_even, t_even, x_odd,
    p_out, i_out, total_out,
    u, r, v, w, p, q, d, t, masks,
):
    layers, rows = p_in.shape[0], p_in.shape[1]
    odd, has_low, has_high = place("gx")
    fill_rows(masks, rows)
    own = slice(LOW, LOW + rows)
    zero = jnp.zeros((8, u.shape[2]), F32)
    rz, pq = sums[0], sums[1]
    chunks = row_chunks(rows)
    for side in range(2):
        at = tuple(k if side == 0 else layers - 1 - k for k in range(4))
        has = (has_low, has_high)[side]
        pick = jnp.logical_xor(odd, side == 1)
        twice = 1.0 + has

        def arrived(first, second):
            return jnp.where(pick, first, second) * has

        near, far = (1, 0) if side == 0 else (0, 1)
        for slot, source in ((0, far), (1, near)):
            u[slot, own] = arrived(x_even[source], x_odd[source * rows : (source + 1) * rows])
        r[own] = arrived(x_even[2], x_odd[2 * rows : 3 * rows])
        t[own] = arrived(t_even[0:rows], x_odd[3 * rows : 4 * rows])
        corner = arrived(t_even[rows : rows + 8], x_odd[4 * rows : 4 * rows + 8])
        low, high = slice(HALO, LOW), slice(LOW + rows, LOW + rows + HALO)
        row = lax.broadcasted_iota(jnp.int32, zero.shape, 0)

        def one(k):
            return jnp.broadcast_to(corner[k : k + 1], zero.shape)

        u[1, low] = jnp.where(row == 7, one(0), jnp.where(row == 6, one(1), 0.0))
        u[0, low] = jnp.where(row == 7, one(2), 0.0)
        r[low] = jnp.where(row == 7, one(3), 0.0)
        u[1, high] = jnp.where(row == 0, one(4), jnp.where(row == 1, one(5), 0.0))
        u[0, high] = jnp.where(row == 0, one(6), 0.0)
        r[high] = jnp.where(row == 0, one(7), 0.0)
        t[low] = zero
        t[high] = zero

        for start, size in chunks:
            here = slice(start, start + size)
            down, up = slice(start - 1, start + size - 1), slice(start + 1, start + size + 1)
            inside = masks[0, here]
            mid, edge = u[1, here], b_u[at[0], here]
            total = 6.0 * mid + u[0, here] + edge + u[1, down] + u[1, up] + z_sum(mid)
            inverse = has * inside / jnp.maximum(total, TINY)
            value = 2.0 * r[here] * inverse
            d[1, here] = inverse
            v[0, here] = value
            w[0, here] = mid * value
            total = 6.0 * edge + mid + b_u[at[1], here]
            total = total + b_u[at[0], down] + b_u[at[0], up] + z_sum(edge)
            inverse = inside / jnp.maximum(total, TINY)
            value = 2.0 * b_r[at[0], here] * inverse
            d[0, here] = total
            d[2, here] = inverse
            v[1, here] = value
            w[1, here] = edge * value

        for start, size in chunks:
            here = slice(start, start + size)
            down, up = slice(start - 1, start + size - 1), slice(start + 1, start + size + 1)
            plain = is_plain(start, size, rows)

            def finish(mid, total, south, north, inverse, slot, twice):
                if plain:
                    value = twice * inverse * (total + south + north)
                else:
                    total = total + masks[2, here] * south + masks[3, here] * north
                    value = twice * masks[1, here] * inverse * total
                p[slot, here] = value
                q[slot, here] = mid * value

            mid = u[1, here]
            total = 2.0 * r[here] + t[here]
            total = total + mid * (v[1, here] + z_sum(v[0, here]))
            total = total + w[1, here] + z_sum(w[0, here])
            south = mid * v[0, down] + w[0, down]
            north = mid * v[0, up] + w[0, up]
            finish(mid, total, south, north, d[1, here], 0, twice)

            mid, next_u = b_u[at[0], here], b_u[at[1], here]
            next_v = e_v[side, 0, here]
            total = 2.0 * b_r[at[0], here]
            total = total + mid * (v[0, here] + next_v + z_sum(v[1, here]))
            total = total + w[0, here] + next_u * next_v + z_sum(w[1, here])
            south = mid * v[1, down] + w[1, down]
            north = mid * v[1, up] + w[1, up]
            finish(mid, total, south, north, d[2, here], 1, twice)

            inner_v = e_v[side, 1, here]
            total = 2.0 * b_r[at[1], here]
            total = total + next_u * (v[1, here] + z_sum(next_v))
            total = total + w[1, here] + z_sum(next_u * next_v)
            total = total + (next_u * inner_v + b_u[at[2], here] * inner_v) / twice
            south = (next_u + b_u[at[1], down]) * e_v[side, 0, down]
            north = (next_u + b_u[at[1], up]) * e_v[side, 0, up]
            finish(next_u, total, south, north, e_i[side, 0, here], 2, twice)

        for start, size in own_chunks(rows):
            here = slice(start, start + size)
            down, up = slice(start - 1, start + size - 1), slice(start + 1, start + size + 1)
            out_rows = slice(start - LOW, start - LOW + size)
            for k in range(3):
                mid_u = b_u[at[k], here]
                if k < 2:
                    mid = p[k + 1, here]
                    near_y = p[k + 1, down] + p[k + 1, up]
                    near_q = q[k + 1, down] + q[k + 1, up]
                    mid_q = q[k + 1, here]
                    before_p, before_q = p[k, here], q[k, here]
                    if k == 0:
                        after_p, after_q = p[2, here], q[2, here]
                    else:
                        after_p = e_p[side, 0, here]
                        after_q = b_u[at[2], here] * after_p
                else:
                    mid = e_p[side, 0, here]
                    mid_q = mid_u * mid
                    low_p, high_p = e_p[side, 0, down], e_p[side, 0, up]
                    near_y = low_p + high_p
                    near_q = b_u[at[2], down] * low_p + b_u[at[2], up] * high_p
                    before_p, before_q = p[2, here], q[2, here]
                    after_p = e_p[side, 1, here]
                    after_q = None
                around = before_p + after_p + near_y + z_sum(mid)
                if after_q is None:
                    after_q = b_u[at[3], here] * after_p
                scaled = before_q + after_q + near_q + z_sum(mid_q)
                total = d[0, here] if k == 0 else e_d[side, k - 1, here]
                image = total * mid - mid_u * around - scaled
                p_out[at[k], out_rows] = mid
                i_out[at[k], out_rows] = image
                rz = rz + eight(b_r[at[k], here] * mid)
                pq = pq + eight(mid * image)
    total_out[0:1] = jnp.broadcast_to(jnp.sum(rz, keepdims=True), (1, zero.shape[1]))
    total_out[1:2] = jnp.broadcast_to(jnp.sum(pq, keepdims=True), (1, zero.shape[1]))


def outer(found, x_even, t_even, x_odd):
    p_in = found[2]
    layers, rows, lanes = p_in.shape
    grown = rows + 4 * HALO

    def field(*lead):
        return pltpu.VMEM((*lead, grown, lanes), F32)

    return pl.pallas_call(
        outer_kernel,
        out_shape=(shape(layers, rows, lanes), shape(layers, rows, lanes), shape(2, lanes)),
        in_specs=[VMEM] * 12,
        out_specs=(VMEM, VMEM, VMEM),
        scratch_shapes=[
            field(2), field(), field(2), field(2), field(3), field(3), field(3), field(), field(4),
        ],
        input_output_aliases={2: 0, 3: 1},
        compiler_params=params(4),
        name="outer",
    )(*found, x_even, t_even, x_odd)


def power_of_two(count):
    return count & (count - 1) == 0


def sum_everywhere(value):
    count_x, count_y = lax.axis_size("gx"), lax.axis_size("gy")
    if not (power_of_two(count_x) and power_of_two(count_y)):
        return lax.psum(value, ("gx", "gy"))
    low = 1 if count_y > 1 else 0
    steps = [(0, 1 << bit | low) for bit in range(count_y.bit_length() - 1)]
    steps += [(1 << bit, low) for bit in range(count_x.bit_length() - 1)]
    for step_x, step_y in steps:
        pairs = [
            (x * count_y + y, (x ^ step_x) * count_y + (y ^ step_y))
            for x in range(count_x)
            for y in range(count_y)
        ]
        value = value + lax.ppermute(value, ("gx", "gy"), pairs)
    return value


def update_kernel(sums, precond, image, resid, pressure, residual, held, sem):
    half_alpha = sums[0:1] / sums[1:2]
    alpha = 2.0 * half_alpha
    layers, rows, _ = precond.shape
    own = slice(LOW, LOW + rows)
    step = 4 if layers % 4 == 0 else layers
    started = []
    for start in range(0, layers, step):
        for k in range(start, start + step):
            held[0, k] = alpha * precond[k]
            held[1, k] = resid[k, own] - half_alpha * image[k]
        part = pl.ds(start, step)
        for i, out in enumerate((pressure, residual)):
            copy = pltpu.make_async_copy(
                held.at[i, part], out.at[part], sem.at[i, start // step]
            )
            copy.start()
            started.append(copy)
    for copy in started:
        copy.wait()


def update(sums, precond, image, resid):
    out = shape(*precond.shape)
    return pl.pallas_call(
        update_kernel,
        out_shape=(out, out),
        in_specs=[VMEM] * 4,
        out_specs=(HBM, HBM),
        scratch_shapes=[
            pltpu.VMEM((2, *precond.shape), F32),
            pltpu.SemaphoreType.DMA((2, precond.shape[0])),
        ],
        compiler_params=params(4),
        name="update",
    )(sums, precond, image, resid)


def on_device(right_side, conductivity):
    x_even, y_even, y_odd, u, r = pack(conductivity, right_side)
    x_even = swap_even(x_even, "gx")
    y_even = swap_even(y_even, "gy")
    y_odd = swap_odd(y_odd, "gy")
    t_even, x_odd = edge_terms(u, r, y_even, y_odd)
    x_odd = swap_odd(x_odd, "gx")
    t_even = swap_even(t_even, "gx")
    found = inner(u, r, y_even, y_odd)
    precond, image, sums = outer(found, x_even, t_even, x_odd)
    return update(sum_everywhere(sums), precond, image, found[1])


def solution(mesh):
    in_specs = (P("gx", "gy", None), P("gx", "gy", None))
    out_specs = (P("gx", "gy", None), P("gx", "gy", None))
    return jax.shard_map(
        on_device, mesh=mesh, in_specs=in_specs, out_specs=out_specs, check_vma=False
    )
```

```python
import jax
import jax.numpy as jnp
from jax import lax
from jax.experimental import pallas as pl
from jax.experimental.pallas import tpu as pltpu
from jax.sharding import PartitionSpec as P

F32 = jnp.float32
HALO = 8
LOW = 2 * HALO
TINY = 1e-30
HBM = pl.BlockSpec(memory_space=pltpu.HBM)
VMEM = pl.BlockSpec(memory_space=pltpu.VMEM)


def params(mebibytes):
    return pltpu.CompilerParams(vmem_limit_bytes=mebibytes << 20)


def shape(*dims):
    return jax.ShapeDtypeStruct(dims, F32)


def swap(value, partner):
    count_x, count_y = lax.axis_size("gx"), lax.axis_size("gy")
    pairs = []
    for x in range(count_x):
        for y in range(count_y):
            to_x, to_y = partner(x, y)
            pairs.append((x * count_y + y, to_x * count_y + to_y))
    return lax.ppermute(value, ("gx", "gy"), pairs)


def swap_x(value, odd):
    count = lax.axis_size("gx")

    def partner(x, y):
        to = ((x + odd) ^ 1) - odd
        return (to, y) if 0 <= to < count else (x, y ^ 1)

    return swap(value, partner)


def swap_y(value, odd):
    count = lax.axis_size("gy")
    return swap(value, lambda x, y: (x, (((y + odd) ^ 1) - odd) % count))


def place(axis):
    index, count = lax.axis_index(axis), lax.axis_size(axis)
    odd = lax.rem(index, 2) == 1
    has_low = (index > 0).astype(F32)
    has_high = (index < count - 1).astype(F32)
    return odd, has_low, has_high


def z_sum(value):
    lane = lax.broadcasted_iota(jnp.int32, value.shape, 1)
    last = value.shape[1] - 1
    below = jnp.where(lane > 0, pltpu.roll(value, 1, 1), 0.0)
    above = jnp.where(lane < last, pltpu.roll(value, last, 1), 0.0)
    return below + above


def pack_kernel(cond, resid, x_even, x_odd, y_even, y_odd, tiles, sem):
    layers, rows, lanes = cond.shape
    odd = lax.rem(lax.axis_index("gx"), 2)
    x_copies, y_copies = [], []
    for out, high in ((x_even, 1 - odd), (x_odd, odd)):
        two = pl.ds(high * (layers - 2), 2)
        one = pl.ds(high * (layers - 1), 1)
        x_copies.append((cond.at[two], out.at[pl.ds(0, 2)]))
        x_copies.append((resid.at[one], out.at[pl.ds(2, 1)]))
    for side, start in enumerate((0, rows - HALO)):
        for part, source in enumerate((cond, resid)):
            y_copies.append((source.at[:, pl.ds(start, HALO)], tiles.at[side, part]))
    started = [
        pltpu.make_async_copy(source, target, sem.at[i])
        for i, (source, target) in enumerate(y_copies + x_copies)
    ]
    for copy in started:
        copy.start()
    for copy in started[:4]:
        copy.wait()
    odd = lax.rem(lax.axis_index("gy"), 2) == 1
    first = lax.broadcasted_iota(jnp.int32, (HALO, lanes), 0) < 3
    for k in range(layers):
        low = jnp.where(first, tiles[0, 0, k], pltpu.roll(tiles[0, 1, k], 3, 0))
        high = jnp.where(
            first, pltpu.roll(tiles[1, 0, k], 3, 0), pltpu.roll(tiles[1, 1, k], 5, 0)
        )
        y_even[k] = jnp.where(odd, low, high)
        y_odd[k] = jnp.where(odd, high, low)
    for copy in started[4:]:
        copy.wait()


def pack(cond, resid):
    layers, rows, lanes = cond.shape
    x_out, y_out = shape(3, rows, lanes), shape(layers, HALO, lanes)
    return pl.pallas_call(
        pack_kernel,
        out_shape=(x_out, x_out, y_out, y_out),
        in_specs=[HBM, HBM],
        out_specs=(VMEM,) * 4,
        scratch_shapes=[
            pltpu.VMEM((2, 2, layers, HALO, lanes), F32),
            pltpu.SemaphoreType.DMA((8,)),
        ],
        compiler_params=params(2),
        name="pack",
    )(
        pltpu.with_memory_space_constraint(cond, pltpu.HBM),
        pltpu.with_memory_space_constraint(resid, pltpu.HBM),
    )


def load_kernel(cond, resid, after, u, r, sem):
    own = pl.ds(LOW, cond.shape[1])
    copies = [
        pltpu.make_async_copy(source, target.at[:, own], sem.at[i])
        for i, (source, target) in enumerate(((cond, u), (resid, r)))
    ]
    for copy in copies:
        copy.start()
    for copy in copies:
        copy.wait()


def load(cond, resid, after):
    layers, rows, lanes = cond.shape
    grown = shape(layers, rows + 4 * HALO, lanes)
    return pl.pallas_call(
        load_kernel,
        out_shape=(grown, grown),
        in_specs=[HBM, HBM, VMEM],
        out_specs=(VMEM, VMEM),
        scratch_shapes=[pltpu.SemaphoreType.DMA((2,))],
        compiler_params=params(1),
        cost_estimate=pl.CostEstimate(
            flops=1_000_000_000, transcendentals=0, bytes_accessed=4 * cond.size
        ),
        name="load",
    )(
        pltpu.with_memory_space_constraint(cond, pltpu.HBM),
        pltpu.with_memory_space_constraint(resid, pltpu.HBM),
        after,
    )


def y_tiles(y_even, y_odd, layer, part):
    odd, has_low, has_high = place("gy")
    first, second = y_even[layer], y_odd[layer]
    row = lax.broadcasted_iota(jnp.int32, first.shape, 0)
    width = 3 - part
    south = pltpu.roll(jnp.where(odd, first, second), (5, 3)[part], 0)
    north = jnp.where(odd, second, first)
    if part:
        north = pltpu.roll(north, 5, 0)
    south = jnp.where(row >= HALO - width, south, 0.0) * has_low
    north = jnp.where(row < width, north, 0.0) * has_high
    return south, north


def edge_kernel(u, r, y_even, y_odd, t_even, t_odd, grown):
    layers, rows = u.shape[0], u.shape[1] - 4 * HALO
    odd = place("gx")[0]
    end = HALO + rows
    own = slice(LOW, LOW + rows)
    sends = []
    for side in range(2):
        edge, mid, far = ((0, 1, 2), (layers - 1, layers - 2, layers - 3))[side]
        south, north = y_tiles(y_even, y_odd, mid, 0)
        middle = u[mid, own]
        grown[side, 0:HALO] = south
        grown[side, HALO:end] = middle
        grown[side, end : end + HALO] = north
        total = 6.0 * middle + u[edge, own] + u[far, own] + z_sum(middle)
        total = total + grown[side, HALO - 1 : end - 1] + grown[side, HALO + 1 : end + 1]
        term = (u[edge, own] + middle) * (2.0 * r[mid, own] / total)
        edge_south, edge_north = y_tiles(y_even, y_odd, edge, 0)
        r_south, r_north = y_tiles(y_even, y_odd, edge, 1)
        corner = jnp.concatenate(
            [
                edge_south[HALO - 1 : HALO],
                edge_south[HALO - 2 : HALO - 1],
                south[HALO - 1 : HALO],
                r_south[HALO - 1 : HALO],
                edge_north[0:1],
                edge_north[1:2],
                north[0:1],
                r_north[0:1],
            ],
            axis=0,
        )
        sends.append((term, corner))
    (t_low, c_low), (t_high, c_high) = sends
    t_even[0:rows] = jnp.where(odd, t_low, t_high)
    t_even[rows : rows + 8] = jnp.where(odd, c_low, c_high)
    t_odd[0:rows] = jnp.where(odd, t_high, t_low)
    t_odd[rows : rows + 8] = jnp.where(odd, c_high, c_low)


def edge_terms(u, r, y_even, y_odd):
    rows, lanes = u.shape[1] - 4 * HALO, u.shape[2]
    return pl.pallas_call(
        edge_kernel,
        out_shape=(shape(rows + 8, lanes), shape(rows + 8, lanes)),
        in_specs=[VMEM] * 4,
        out_specs=(VMEM, VMEM),
        scratch_shapes=[pltpu.VMEM((2, rows + 2 * HALO, lanes), F32)],
        compiler_params=params(2),
        name="edge_terms",
    )(u, r, y_even, y_odd)


def row_chunks(rows):
    total = rows + 2 * HALO
    step = total // 3 if total % 24 == 0 else total
    return [(HALO + i * step, step) for i in range(total // step)]


def own_chunks(rows):
    step = 32 if rows % 32 == 0 else rows
    return [(LOW + i * step, step) for i in range(rows // step)]


def fill_rows(masks, rows):
    _, has_low, has_high = place("gy")
    row = lax.broadcasted_iota(jnp.int32, masks.shape[1:], 0) - LOW
    inside = jnp.where(row < 0, has_low, jnp.where(row >= rows, has_high, 1.0))
    near_low, near_high = row < 2, row >= rows - 2
    count = jnp.where(near_low, 1.0 + has_low, jnp.where(near_high, 1.0 + has_high, 1.0))
    masks[0] = inside
    masks[1] = count
    masks[2] = jnp.where(row == rows - 2, 1.0 / (1.0 + has_high), 1.0)
    masks[3] = jnp.where(row == 1, 1.0 / (1.0 + has_low), 1.0)


def is_plain(start, size, rows):
    return start >= LOW + 2 and start + size <= LOW + rows - 2


def eight(value):
    return jnp.sum(value.reshape(value.shape[0] // 8, 8, value.shape[1]), axis=0)


def inner_kernel(
    u_in, r_in, y_even, y_odd,
    u, r, p_out, i_out, e_v, e_i, e_d, e_p, sums,
    inv, v, w, d, p, q, masks,
):
    layers, rows = p_out.shape[0], p_out.shape[1]
    fill_rows(masks, rows)

    def halo(k, carry):
        for part, target in enumerate((u, r)):
            south, north = y_tiles(y_even, y_odd, k, part)
            target[k, HALO:LOW] = south
            target[k, LOW + rows : LOW + rows + HALO] = north
        return carry

    lax.fori_loop(0, layers, halo, 0)
    chunks = row_chunks(rows)

    def first(k, carry):
        for start, size in chunks:
            here = slice(start, start + size)
            down, up = slice(start - 1, start + size - 1), slice(start + 1, start + size + 1)
            mid = u[k, here]
            total = 6.0 * mid + u[k - 1, here] + u[k + 1, here]
            total = total + u[k, down] + u[k, up] + z_sum(mid)
            inverse = 1.0 / jnp.maximum(total, TINY)
            if not is_plain(start, size, rows):
                inverse = inverse * masks[0, here]
            value = 2.0 * r[k, here] * inverse
            d[k, here] = total
            inv[k, here] = inverse
            v[k, here] = value
            w[k, here] = mid * value
        return carry

    lax.fori_loop(1, layers - 1, first, 0)

    def second(k, carry):
        for start, size in chunks:
            here = slice(start, start + size)
            down, up = slice(start - 1, start + size - 1), slice(start + 1, start + size + 1)
            mid = u[k, here]
            total = 2.0 * r[k, here]
            total = total + mid * (v[k - 1, here] + v[k + 1, here] + z_sum(v[k, here]))
            total = total + (w[k - 1, here] + w[k + 1, here] + z_sum(w[k, here]))
            south = mid * v[k, down] + w[k, down]
            north = mid * v[k, up] + w[k, up]
            if is_plain(start, size, rows):
                value = inv[k, here] * (total + south + north)
            else:
                total = total + masks[2, here] * south + masks[3, here] * north
                value = masks[1, here] * inv[k, here] * total
            p[k, here] = value
            q[k, here] = mid * value
        return carry

    lax.fori_loop(2, layers - 2, second, 0)

    def third(k, carry):
        rz, pq = carry
        for start, size in own_chunks(rows):
            here = slice(start, start + size)
            down, up = slice(start - 1, start + size - 1), slice(start + 1, start + size + 1)
            mid = p[k, here]
            around = p[k - 1, here] + p[k + 1, here] + p[k, down] + p[k, up] + z_sum(mid)
            scaled = q[k - 1, here] + q[k + 1, here] + q[k, down] + q[k, up]
            scaled = scaled + z_sum(q[k, here])
            image = d[k, here] * mid - u[k, here] * around - scaled
            i_out[k, start - LOW : start - LOW + size] = image
            p_out[k, start - LOW : start - LOW + size] = mid
            rz = rz + eight(r[k, here] * mid)
            pq = pq + eight(mid * image)
        return rz, pq

    zero = jnp.zeros((8, u.shape[2]), F32)
    rz, pq = lax.fori_loop(3, layers - 3, third, (zero, zero))
    sums[0] = rz
    sums[1] = pq
    full = slice(HALO, LOW + rows + HALO)
    for side in range(2):
        order = (0, 1, 2, 3) if side == 0 else tuple(layers - 1 - k for k in range(4))
        for k in range(2):
            e_v[side, k, full] = v[order[k + 1], full]
            e_d[side, k, full] = d[order[k + 1], full]
            e_p[side, k, full] = p[order[k + 2], full]
        e_i[side, 0, full] = inv[order[1], full]


def inner(u, r, y_even, y_odd):
    layers, grown, lanes = u.shape
    rows = grown - 4 * HALO
    field = pltpu.VMEM((layers, grown, lanes), F32)

    def edge(count):
        return shape(2, count, grown, lanes)

    own, ext = shape(layers, rows, lanes), shape(layers, grown, lanes)
    outs = (ext, ext, own, own, edge(2), edge(1), edge(2), edge(2), shape(2, 8, lanes))
    return pl.pallas_call(
        inner_kernel,
        out_shape=outs,
        in_specs=[VMEM] * 4,
        out_specs=(VMEM,) * len(outs),
        scratch_shapes=[field] * 6 + [pltpu.VMEM((4, grown, lanes), F32)],
        input_output_aliases={0: 0, 1: 1},
        compiler_params=params(12),
        cost_estimate=pl.CostEstimate(flops=4_000_000_000, transcendentals=0, bytes_accessed=1),
        name="inner",
    )(u, r, y_even, y_odd)


def outer_kernel(
    b_u, b_r, p_in, i_in, e_v, e_i, e_d, e_p, sums, x_even, x_odd, t_even, t_odd,
    p_out, i_out, total_out,
    u, r, v, w, p, q, d, t, masks,
):
    layers, rows = p_in.shape[0], p_in.shape[1]
    odd, has_low, has_high = place("gx")
    fill_rows(masks, rows)
    own = slice(LOW, LOW + rows)
    zero = jnp.zeros((8, u.shape[2]), F32)
    rz, pq = sums[0], sums[1]
    chunks = row_chunks(rows)
    for side in range(2):
        at = tuple(k if side == 0 else layers - 1 - k for k in range(4))
        has = (has_low, has_high)[side]
        pick = jnp.logical_xor(odd, side == 1)
        twice = 1.0 + has

        def arrived(first, second):
            return jnp.where(pick, first, second) * has

        near, far = (1, 0) if side == 0 else (0, 1)
        for slot, source in ((0, far), (1, near)):
            u[slot, own] = arrived(x_even[source], x_odd[source])
        r[own] = arrived(x_even[2], x_odd[2])
        t[own] = arrived(t_even[0:rows], t_odd[0:rows])
        corner = arrived(t_even[rows : rows + 8], t_odd[rows : rows + 8])
        low, high = slice(HALO, LOW), slice(LOW + rows, LOW + rows + HALO)
        row = lax.broadcasted_iota(jnp.int32, zero.shape, 0)

        def one(k):
            return jnp.broadcast_to(corner[k : k + 1], zero.shape)

        u[1, low] = jnp.where(row == 7, one(0), jnp.where(row == 6, one(1), 0.0))
        u[0, low] = jnp.where(row == 7, one(2), 0.0)
        r[low] = jnp.where(row == 7, one(3), 0.0)
        u[1, high] = jnp.where(row == 0, one(4), jnp.where(row == 1, one(5), 0.0))
        u[0, high] = jnp.where(row == 0, one(6), 0.0)
        r[high] = jnp.where(row == 0, one(7), 0.0)
        t[low] = zero
        t[high] = zero

        for start, size in chunks:
            here = slice(start, start + size)
            down, up = slice(start - 1, start + size - 1), slice(start + 1, start + size + 1)
            inside = masks[0, here]
            mid, edge = u[1, here], b_u[at[0], here]
            total = 6.0 * mid + u[0, here] + edge + u[1, down] + u[1, up] + z_sum(mid)
            inverse = has * inside / jnp.maximum(total, TINY)
            value = 2.0 * r[here] * inverse
            d[1, here] = inverse
            v[0, here] = value
            w[0, here] = mid * value
            total = 6.0 * edge + mid + b_u[at[1], here]
            total = total + b_u[at[0], down] + b_u[at[0], up] + z_sum(edge)
            inverse = inside / jnp.maximum(total, TINY)
            value = 2.0 * b_r[at[0], here] * inverse
            d[0, here] = total
            d[2, here] = inverse
            v[1, here] = value
            w[1, here] = edge * value

        for start, size in chunks:
            here = slice(start, start + size)
            down, up = slice(start - 1, start + size - 1), slice(start + 1, start + size + 1)
            plain = is_plain(start, size, rows)

            def finish(mid, total, south, north, inverse, slot, twice):
                if plain:
                    value = twice * inverse * (total + south + north)
                else:
                    total = total + masks[2, here] * south + masks[3, here] * north
                    value = twice * masks[1, here] * inverse * total
                p[slot, here] = value
                q[slot, here] = mid * value

            mid = u[1, here]
            total = 2.0 * r[here] + t[here]
            total = total + mid * (v[1, here] + z_sum(v[0, here]))
            total = total + w[1, here] + z_sum(w[0, here])
            south = mid * v[0, down] + w[0, down]
            north = mid * v[0, up] + w[0, up]
            finish(mid, total, south, north, d[1, here], 0, twice)

            mid, next_u = b_u[at[0], here], b_u[at[1], here]
            next_v = e_v[side, 0, here]
            total = 2.0 * b_r[at[0], here]
            total = total + mid * (v[0, here] + next_v + z_sum(v[1, here]))
            total = total + w[0, here] + next_u * next_v + z_sum(w[1, here])
            south = mid * v[1, down] + w[1, down]
            north = mid * v[1, up] + w[1, up]
            finish(mid, total, south, north, d[2, here], 1, twice)

            inner_v = e_v[side, 1, here]
            total = 2.0 * b_r[at[1], here]
            total = total + next_u * (v[1, here] + z_sum(next_v))
            total = total + w[1, here] + z_sum(next_u * next_v)
            total = total + (next_u * inner_v + b_u[at[2], here] * inner_v) / twice
            south = (next_u + b_u[at[1], down]) * e_v[side, 0, down]
            north = (next_u + b_u[at[1], up]) * e_v[side, 0, up]
            finish(next_u, total, south, north, e_i[side, 0, here], 2, twice)

        for start, size in own_chunks(rows):
            here = slice(start, start + size)
            down, up = slice(start - 1, start + size - 1), slice(start + 1, start + size + 1)
            out_rows = slice(start - LOW, start - LOW + size)
            for k in range(3):
                mid_u = b_u[at[k], here]
                if k < 2:
                    mid = p[k + 1, here]
                    near_y = p[k + 1, down] + p[k + 1, up]
                    near_q = q[k + 1, down] + q[k + 1, up]
                    mid_q = q[k + 1, here]
                    before_p, before_q = p[k, here], q[k, here]
                    if k == 0:
                        after_p, after_q = p[2, here], q[2, here]
                    else:
                        after_p = e_p[side, 0, here]
                        after_q = b_u[at[2], here] * after_p
                else:
                    mid = e_p[side, 0, here]
                    mid_q = mid_u * mid
                    low_p, high_p = e_p[side, 0, down], e_p[side, 0, up]
                    near_y = low_p + high_p
                    near_q = b_u[at[2], down] * low_p + b_u[at[2], up] * high_p
                    before_p, before_q = p[2, here], q[2, here]
                    after_p = e_p[side, 1, here]
                    after_q = None
                around = before_p + after_p + near_y + z_sum(mid)
                if after_q is None:
                    after_q = b_u[at[3], here] * after_p
                scaled = before_q + after_q + near_q + z_sum(mid_q)
                total = d[0, here] if k == 0 else e_d[side, k - 1, here]
                image = total * mid - mid_u * around - scaled
                p_out[at[k], out_rows] = mid
                i_out[at[k], out_rows] = image
                rz = rz + eight(b_r[at[k], here] * mid)
                pq = pq + eight(mid * image)
    total_out[0:1] = jnp.broadcast_to(jnp.sum(rz, keepdims=True), (1, zero.shape[1]))
    total_out[1:2] = jnp.broadcast_to(jnp.sum(pq, keepdims=True), (1, zero.shape[1]))


def outer(found, x_even, x_odd, t_even, t_odd):
    p_in = found[2]
    layers, rows, lanes = p_in.shape
    grown = rows + 4 * HALO

    def field(*lead):
        return pltpu.VMEM((*lead, grown, lanes), F32)

    return pl.pallas_call(
        outer_kernel,
        out_shape=(shape(layers, rows, lanes), shape(layers, rows, lanes), shape(2, lanes)),
        in_specs=[VMEM] * 13,
        out_specs=(VMEM, VMEM, VMEM),
        scratch_shapes=[
            field(2), field(), field(2), field(2), field(3), field(3), field(3), field(), field(4),
        ],
        input_output_aliases={2: 0, 3: 1},
        compiler_params=params(4),
        name="outer",
    )(*found, x_even, x_odd, t_even, t_odd)


def power_of_two(count):
    return count & (count - 1) == 0


def sum_everywhere(value):
    count_x, count_y = lax.axis_size("gx"), lax.axis_size("gy")
    if not (power_of_two(count_x) and power_of_two(count_y)):
        return lax.psum(value, ("gx", "gy"))
    low = 1 if count_y > 1 else 0
    steps = [(0, 1 << bit | low) for bit in range(count_y.bit_length() - 1)]
    steps += [(1 << bit, low) for bit in range(count_x.bit_length() - 1)]
    for step_x, step_y in steps:
        value = value + swap(value, lambda x, y: (x ^ step_x, y ^ step_y))
    return value


def update_kernel(sums, precond, image, resid, pressure, residual, held, sem):
    half_alpha = sums[0:1] / sums[1:2]
    alpha = 2.0 * half_alpha
    layers, rows, _ = precond.shape
    own = slice(LOW, LOW + rows)
    step = 4 if layers % 4 == 0 else layers
    started = []
    for start in range(0, layers, step):
        for k in range(start, start + step):
            held[0, k] = alpha * precond[k]
            held[1, k] = resid[k, own] - half_alpha * image[k]
        part = pl.ds(start, step)
        for i, out in enumerate((pressure, residual)):
            copy = pltpu.make_async_copy(
                held.at[i, part], out.at[part], sem.at[i, start // step]
            )
            copy.start()
            started.append(copy)
    for copy in started:
        copy.wait()


def update(sums, precond, image, resid):
    out = shape(*precond.shape)
    return pl.pallas_call(
        update_kernel,
        out_shape=(out, out),
        in_specs=[VMEM] * 4,
        out_specs=(HBM, HBM),
        scratch_shapes=[
            pltpu.VMEM((2, *precond.shape), F32),
            pltpu.SemaphoreType.DMA((2, precond.shape[0])),
        ],
        compiler_params=params(4),
        name="update",
    )(sums, precond, image, resid)


def on_device(right_side, conductivity):
    x_even, x_odd, y_even, y_odd = pack(conductivity, right_side)
    u, r = load(conductivity, right_side, y_even)
    y_even, y_odd = swap_y(y_even, 0), swap_y(y_odd, 1)
    x_even, x_odd = swap_x(x_even, 0), swap_x(x_odd, 1)
    t_even, t_odd = edge_terms(u, r, y_even, y_odd)
    t_even, t_odd = swap_x(t_even, 0), swap_x(t_odd, 1)
    found = inner(u, r, y_even, y_odd)
    precond, image, sums = outer(found, x_even, x_odd, t_even, t_odd)
    return update(sum_everywhere(sums), precond, image, found[1])


def solution(mesh):
    in_specs = (P("gx", "gy", None), P("gx", "gy", None))
    out_specs = (P("gx", "gy", None), P("gx", "gy", None))
    return jax.shard_map(
        on_device, mesh=mesh, in_specs=in_specs, out_specs=out_specs, check_vma=False
    )
```

```python
import jax
import jax.numpy as jnp
from jax import lax
from jax.experimental import pallas as pl
from jax.experimental.pallas import tpu as pltpu
from jax.sharding import PartitionSpec as P

F32 = jnp.float32
HALO = 8
LOW = 2 * HALO
TINY = 1e-30
HBM = pl.BlockSpec(memory_space=pltpu.HBM)
VMEM = pl.BlockSpec(memory_space=pltpu.VMEM)


def params(mebibytes):
    return pltpu.CompilerParams(vmem_limit_bytes=mebibytes << 20)


def shape(*dims):
    return jax.ShapeDtypeStruct(dims, F32)


def swap(value, partner):
    count_x, count_y = lax.axis_size("gx"), lax.axis_size("gy")
    pairs = []
    for x in range(count_x):
        for y in range(count_y):
            to_x, to_y = partner(x, y)
            pairs.append((x * count_y + y, to_x * count_y + to_y))
    return lax.ppermute(value, ("gx", "gy"), pairs)


def swap_x(value, odd):
    count = lax.axis_size("gx")

    def partner(x, y):
        to = ((x + odd) ^ 1) - odd
        return (to, y) if 0 <= to < count else (x, y ^ 1)

    return swap(value, partner)


def swap_y(value, odd):
    count = lax.axis_size("gy")
    return swap(value, lambda x, y: (x, (((y + odd) ^ 1) - odd) % count))


def place(axis):
    index, count = lax.axis_index(axis), lax.axis_size(axis)
    odd = lax.rem(index, 2) == 1
    has_low = (index > 0).astype(F32)
    has_high = (index < count - 1).astype(F32)
    return odd, has_low, has_high


def z_sum(value):
    lane = lax.broadcasted_iota(jnp.int32, value.shape, 1)
    last = value.shape[1] - 1
    below = jnp.where(lane > 0, pltpu.roll(value, 1, 1), 0.0)
    above = jnp.where(lane < last, pltpu.roll(value, last, 1), 0.0)
    return below + above


def pack_kernel(cond, resid, x_even, x_odd, y_even, y_odd, tiles, sem):
    layers, rows, lanes = cond.shape
    odd = lax.rem(lax.axis_index("gx"), 2)
    x_copies, y_copies = [], []
    for out, high in ((x_even, 1 - odd), (x_odd, odd)):
        two = pl.ds(high * (layers - 2), 2)
        one = pl.ds(high * (layers - 1), 1)
        x_copies.append((cond.at[two], out.at[pl.ds(0, 2)]))
        x_copies.append((resid.at[one], out.at[pl.ds(2, 1)]))
    for side, start in enumerate((0, rows - HALO)):
        for part, source in enumerate((cond, resid)):
            y_copies.append((source.at[:, pl.ds(start, HALO)], tiles.at[side, part]))
    started = [
        pltpu.make_async_copy(source, target, sem.at[i])
        for i, (source, target) in enumerate(y_copies + x_copies)
    ]
    for copy in started:
        copy.start()
    for copy in started[:4]:
        copy.wait()
    odd = lax.rem(lax.axis_index("gy"), 2) == 1
    first = lax.broadcasted_iota(jnp.int32, (HALO, lanes), 0) < 3
    for k in range(layers):
        low = jnp.where(first, tiles[0, 0, k], pltpu.roll(tiles[0, 1, k], 3, 0))
        high = jnp.where(
            first, pltpu.roll(tiles[1, 0, k], 3, 0), pltpu.roll(tiles[1, 1, k], 5, 0)
        )
        y_even[k] = jnp.where(odd, low, high)
        y_odd[k] = jnp.where(odd, high, low)
    for copy in started[4:]:
        copy.wait()


def pack(cond, resid):
    layers, rows, lanes = cond.shape
    x_out, y_out = shape(3, rows, lanes), shape(layers, HALO, lanes)
    return pl.pallas_call(
        pack_kernel,
        out_shape=(x_out, x_out, y_out, y_out),
        in_specs=[HBM, HBM],
        out_specs=(VMEM,) * 4,
        scratch_shapes=[
            pltpu.VMEM((2, 2, layers, HALO, lanes), F32),
            pltpu.SemaphoreType.DMA((8,)),
        ],
        compiler_params=params(2),
        name="pack",
    )(
        pltpu.with_memory_space_constraint(cond, pltpu.HBM),
        pltpu.with_memory_space_constraint(resid, pltpu.HBM),
    )


def load_kernel(cond, resid, after, u, r, sem):
    own = pl.ds(LOW, cond.shape[1])
    copies = [
        pltpu.make_async_copy(source, target.at[:, own], sem.at[i])
        for i, (source, target) in enumerate(((cond, u), (resid, r)))
    ]
    for copy in copies:
        copy.start()
    for copy in copies:
        copy.wait()


def load(cond, resid, after):
    layers, rows, lanes = cond.shape
    grown = shape(layers, rows + 4 * HALO, lanes)
    return pl.pallas_call(
        load_kernel,
        out_shape=(grown, grown),
        in_specs=[HBM, HBM, VMEM],
        out_specs=(VMEM, VMEM),
        scratch_shapes=[pltpu.SemaphoreType.DMA((2,))],
        compiler_params=params(1),
        cost_estimate=pl.CostEstimate(
            flops=1_000_000_000, transcendentals=0, bytes_accessed=4 * cond.size
        ),
        name="load",
    )(
        pltpu.with_memory_space_constraint(cond, pltpu.HBM),
        pltpu.with_memory_space_constraint(resid, pltpu.HBM),
        after,
    )


def y_tiles(y_even, y_odd, layer, part):
    odd, has_low, has_high = place("gy")
    first, second = y_even[layer], y_odd[layer]
    row = lax.broadcasted_iota(jnp.int32, first.shape, 0)
    width = 3 - part
    south = pltpu.roll(jnp.where(odd, first, second), (5, 3)[part], 0)
    north = jnp.where(odd, second, first)
    if part:
        north = pltpu.roll(north, 5, 0)
    south = jnp.where(row >= HALO - width, south, 0.0) * has_low
    north = jnp.where(row < width, north, 0.0) * has_high
    return south, north


def edge_kernel(u, r, y_even, y_odd, t_even, t_odd, grown):
    layers, rows = u.shape[0], u.shape[1] - 4 * HALO
    odd = place("gx")[0]
    end = HALO + rows
    own = slice(LOW, LOW + rows)
    sends = []
    for side in range(2):
        edge, mid, far = ((0, 1, 2), (layers - 1, layers - 2, layers - 3))[side]
        south, north = y_tiles(y_even, y_odd, mid, 0)
        middle = u[mid, own]
        grown[side, 0:HALO] = south
        grown[side, HALO:end] = middle
        grown[side, end : end + HALO] = north
        total = 6.0 * middle + u[edge, own] + u[far, own] + z_sum(middle)
        total = total + grown[side, HALO - 1 : end - 1] + grown[side, HALO + 1 : end + 1]
        term = (u[edge, own] + middle) * (2.0 * r[mid, own] / total)
        edge_south, edge_north = y_tiles(y_even, y_odd, edge, 0)
        r_south, r_north = y_tiles(y_even, y_odd, edge, 1)
        corner = jnp.concatenate(
            [
                edge_south[HALO - 1 : HALO],
                edge_south[HALO - 2 : HALO - 1],
                south[HALO - 1 : HALO],
                r_south[HALO - 1 : HALO],
                edge_north[0:1],
                edge_north[1:2],
                north[0:1],
                r_north[0:1],
            ],
            axis=0,
        )
        sends.append((term, corner))
    (t_low, c_low), (t_high, c_high) = sends
    t_even[0:rows] = jnp.where(odd, t_low, t_high)
    t_even[rows : rows + 8] = jnp.where(odd, c_low, c_high)
    t_odd[0:rows] = jnp.where(odd, t_high, t_low)
    t_odd[rows : rows + 8] = jnp.where(odd, c_high, c_low)


def edge_terms(u, r, y_even, y_odd):
    rows, lanes = u.shape[1] - 4 * HALO, u.shape[2]
    return pl.pallas_call(
        edge_kernel,
        out_shape=(shape(rows + 8, lanes), shape(rows + 8, lanes)),
        in_specs=[VMEM] * 4,
        out_specs=(VMEM, VMEM),
        scratch_shapes=[pltpu.VMEM((2, rows + 2 * HALO, lanes), F32)],
        compiler_params=params(2),
        name="edge_terms",
    )(u, r, y_even, y_odd)


def row_chunks(rows):
    total = rows + 2 * HALO
    step = total // 3 if total % 24 == 0 else total
    return [(HALO + i * step, step) for i in range(total // step)]


def own_chunks(rows):
    step = 32 if rows % 32 == 0 else rows
    return [(LOW + i * step, step) for i in range(rows // step)]


def fill_rows(masks, rows):
    _, has_low, has_high = place("gy")
    row = lax.broadcasted_iota(jnp.int32, masks.shape[1:], 0) - LOW
    inside = jnp.where(row < 0, has_low, jnp.where(row >= rows, has_high, 1.0))
    near_low, near_high = row < 2, row >= rows - 2
    count = jnp.where(near_low, 1.0 + has_low, jnp.where(near_high, 1.0 + has_high, 1.0))
    masks[0] = inside
    masks[1] = count
    masks[2] = jnp.where(row == rows - 2, 1.0 / (1.0 + has_high), 1.0)
    masks[3] = jnp.where(row == 1, 1.0 / (1.0 + has_low), 1.0)


def is_plain(start, size, rows):
    return start >= LOW + 2 and start + size <= LOW + rows - 2


def eight(value):
    return jnp.sum(value.reshape(value.shape[0] // 8, 8, value.shape[1]), axis=0)


def inner_kernel(
    u_in, r_in, y_even, y_odd,
    u, r, p_out, i_out, e_v, e_i, e_d, e_p, sums,
    inv, v, w, d, p, q, masks,
):
    layers, rows = p_out.shape[0], p_out.shape[1]
    fill_rows(masks, rows)

    def halo(k, carry):
        for part, target in enumerate((u, r)):
            south, north = y_tiles(y_even, y_odd, k, part)
            target[k, HALO:LOW] = south
            target[k, LOW + rows : LOW + rows + HALO] = north
        return carry

    lax.fori_loop(0, layers, halo, 0)
    chunks = row_chunks(rows)

    def first(k, carry):
        for start, size in chunks:
            here = slice(start, start + size)
            down, up = slice(start - 1, start + size - 1), slice(start + 1, start + size + 1)
            mid = u[k, here]
            total = 6.0 * mid + u[k - 1, here] + u[k + 1, here]
            total = total + u[k, down] + u[k, up] + z_sum(mid)
            inverse = 1.0 / jnp.maximum(total, TINY)
            if not is_plain(start, size, rows):
                inverse = inverse * masks[0, here]
            value = 2.0 * r[k, here] * inverse
            d[k, here] = total
            inv[k, here] = inverse
            v[k, here] = value
            w[k, here] = mid * value
        return carry

    lax.fori_loop(1, layers - 1, first, 0)

    def second(k, carry):
        for start, size in chunks:
            here = slice(start, start + size)
            down, up = slice(start - 1, start + size - 1), slice(start + 1, start + size + 1)
            mid = u[k, here]
            total = 2.0 * r[k, here]
            total = total + mid * (v[k - 1, here] + v[k + 1, here] + z_sum(v[k, here]))
            total = total + (w[k - 1, here] + w[k + 1, here] + z_sum(w[k, here]))
            south = mid * v[k, down] + w[k, down]
            north = mid * v[k, up] + w[k, up]
            if is_plain(start, size, rows):
                value = inv[k, here] * (total + south + north)
            else:
                total = total + masks[2, here] * south + masks[3, here] * north
                value = masks[1, here] * inv[k, here] * total
            p[k, here] = value
            q[k, here] = mid * value
        return carry

    lax.fori_loop(2, layers - 2, second, 0)

    def third(k, carry):
        rz, pq = carry
        for start, size in own_chunks(rows):
            here = slice(start, start + size)
            down, up = slice(start - 1, start + size - 1), slice(start + 1, start + size + 1)
            mid = p[k, here]
            around = p[k - 1, here] + p[k + 1, here] + p[k, down] + p[k, up] + z_sum(mid)
            scaled = q[k - 1, here] + q[k + 1, here] + q[k, down] + q[k, up]
            scaled = scaled + z_sum(q[k, here])
            image = d[k, here] * mid - u[k, here] * around - scaled
            i_out[k, start - LOW : start - LOW + size] = image
            p_out[k, start - LOW : start - LOW + size] = mid
            rz = rz + eight(r[k, here] * mid)
            pq = pq + eight(mid * image)
        return rz, pq

    zero = jnp.zeros((8, u.shape[2]), F32)
    rz, pq = lax.fori_loop(3, layers - 3, third, (zero, zero))
    sums[0] = rz
    sums[1] = pq
    full = slice(HALO, LOW + rows + HALO)
    for side in range(2):
        order = (0, 1, 2, 3) if side == 0 else tuple(layers - 1 - k for k in range(4))
        for k in range(2):
            e_v[side, k, full] = v[order[k + 1], full]
            e_d[side, k, full] = d[order[k + 1], full]
            e_p[side, k, full] = p[order[k + 2], full]
        e_i[side, 0, full] = inv[order[1], full]


def inner(u, r, y_even, y_odd):
    layers, grown, lanes = u.shape
    rows = grown - 4 * HALO
    field = pltpu.VMEM((layers, grown, lanes), F32)

    def edge(count):
        return shape(2, count, grown, lanes)

    own, ext = shape(layers, rows, lanes), shape(layers, grown, lanes)
    outs = (ext, ext, own, own, edge(2), edge(1), edge(2), edge(2), shape(2, 8, lanes))
    return pl.pallas_call(
        inner_kernel,
        out_shape=outs,
        in_specs=[VMEM] * 4,
        out_specs=(VMEM,) * len(outs),
        scratch_shapes=[field] * 6 + [pltpu.VMEM((4, grown, lanes), F32)],
        input_output_aliases={0: 0, 1: 1},
        compiler_params=params(12),
        cost_estimate=pl.CostEstimate(flops=4_000_000_000, transcendentals=0, bytes_accessed=1),
        name="inner",
    )(u, r, y_even, y_odd)


def outer_kernel(
    b_u, b_r, p_in, i_in, e_v, e_i, e_d, e_p, sums, x_even, x_odd, t_even, t_odd,
    p_out, i_out, total_out,
    u, r, v, w, p, q, d, t, masks,
):
    layers, rows = p_in.shape[0], p_in.shape[1]
    odd, has_low, has_high = place("gx")
    fill_rows(masks, rows)
    own = slice(LOW, LOW + rows)
    zero = jnp.zeros((8, u.shape[2]), F32)
    rz, pq = sums[0], sums[1]
    chunks = row_chunks(rows)
    for side in range(2):
        at = tuple(k if side == 0 else layers - 1 - k for k in range(4))
        has = (has_low, has_high)[side]
        pick = jnp.logical_xor(odd, side == 1)
        twice = 1.0 + has

        def arrived(first, second):
            return jnp.where(pick, first, second) * has

        near, far = (1, 0) if side == 0 else (0, 1)
        for slot, source in ((0, far), (1, near)):
            u[slot, own] = arrived(x_even[source], x_odd[source])
        r[own] = arrived(x_even[2], x_odd[2])
        t[own] = arrived(t_even[0:rows], t_odd[0:rows])
        corner = arrived(t_even[rows : rows + 8], t_odd[rows : rows + 8])
        low, high = slice(HALO, LOW), slice(LOW + rows, LOW + rows + HALO)
        row = lax.broadcasted_iota(jnp.int32, zero.shape, 0)

        def one(k):
            return jnp.broadcast_to(corner[k : k + 1], zero.shape)

        u[1, low] = jnp.where(row == 7, one(0), jnp.where(row == 6, one(1), 0.0))
        u[0, low] = jnp.where(row == 7, one(2), 0.0)
        r[low] = jnp.where(row == 7, one(3), 0.0)
        u[1, high] = jnp.where(row == 0, one(4), jnp.where(row == 1, one(5), 0.0))
        u[0, high] = jnp.where(row == 0, one(6), 0.0)
        r[high] = jnp.where(row == 0, one(7), 0.0)
        t[low] = zero
        t[high] = zero

        for start, size in chunks:
            here = slice(start, start + size)
            down, up = slice(start - 1, start + size - 1), slice(start + 1, start + size + 1)
            inside = masks[0, here]
            mid, edge = u[1, here], b_u[at[0], here]
            total = 6.0 * mid + u[0, here] + edge + u[1, down] + u[1, up] + z_sum(mid)
            inverse = has * inside / jnp.maximum(total, TINY)
            value = 2.0 * r[here] * inverse
            d[1, here] = inverse
            v[0, here] = value
            w[0, here] = mid * value
            total = 6.0 * edge + mid + b_u[at[1], here]
            total = total + b_u[at[0], down] + b_u[at[0], up] + z_sum(edge)
            inverse = inside / jnp.maximum(total, TINY)
            value = 2.0 * b_r[at[0], here] * inverse
            d[0, here] = total
            d[2, here] = inverse
            v[1, here] = value
            w[1, here] = edge * value

        for start, size in chunks:
            here = slice(start, start + size)
            down, up = slice(start - 1, start + size - 1), slice(start + 1, start + size + 1)
            plain = is_plain(start, size, rows)

            def finish(mid, total, south, north, inverse, slot, twice):
                if plain:
                    value = twice * inverse * (total + south + north)
                else:
                    total = total + masks[2, here] * south + masks[3, here] * north
                    value = twice * masks[1, here] * inverse * total
                p[slot, here] = value
                q[slot, here] = mid * value

            mid = u[1, here]
            total = 2.0 * r[here] + t[here]
            total = total + mid * (v[1, here] + z_sum(v[0, here]))
            total = total + w[1, here] + z_sum(w[0, here])
            south = mid * v[0, down] + w[0, down]
            north = mid * v[0, up] + w[0, up]
            finish(mid, total, south, north, d[1, here], 0, twice)

            mid, next_u = b_u[at[0], here], b_u[at[1], here]
            next_v = e_v[side, 0, here]
            total = 2.0 * b_r[at[0], here]
            total = total + mid * (v[0, here] + next_v + z_sum(v[1, here]))
            total = total + w[0, here] + next_u * next_v + z_sum(w[1, here])
            south = mid * v[1, down] + w[1, down]
            north = mid * v[1, up] + w[1, up]
            finish(mid, total, south, north, d[2, here], 1, twice)

            inner_v = e_v[side, 1, here]
            total = 2.0 * b_r[at[1], here]
            total = total + next_u * (v[1, here] + z_sum(next_v))
            total = total + w[1, here] + z_sum(next_u * next_v)
            total = total + (next_u * inner_v + b_u[at[2], here] * inner_v) / twice
            south = (next_u + b_u[at[1], down]) * e_v[side, 0, down]
            north = (next_u + b_u[at[1], up]) * e_v[side, 0, up]
            finish(next_u, total, south, north, e_i[side, 0, here], 2, twice)

        for start, size in own_chunks(rows):
            here = slice(start, start + size)
            down, up = slice(start - 1, start + size - 1), slice(start + 1, start + size + 1)
            out_rows = slice(start - LOW, start - LOW + size)
            for k in range(3):
                mid_u = b_u[at[k], here]
                if k < 2:
                    mid = p[k + 1, here]
                    near_y = p[k + 1, down] + p[k + 1, up]
                    near_q = q[k + 1, down] + q[k + 1, up]
                    mid_q = q[k + 1, here]
                    before_p, before_q = p[k, here], q[k, here]
                    if k == 0:
                        after_p, after_q = p[2, here], q[2, here]
                    else:
                        after_p = e_p[side, 0, here]
                        after_q = b_u[at[2], here] * after_p
                else:
                    mid = e_p[side, 0, here]
                    mid_q = mid_u * mid
                    low_p, high_p = e_p[side, 0, down], e_p[side, 0, up]
                    near_y = low_p + high_p
                    near_q = b_u[at[2], down] * low_p + b_u[at[2], up] * high_p
                    before_p, before_q = p[2, here], q[2, here]
                    after_p = e_p[side, 1, here]
                    after_q = None
                around = before_p + after_p + near_y + z_sum(mid)
                if after_q is None:
                    after_q = b_u[at[3], here] * after_p
                scaled = before_q + after_q + near_q + z_sum(mid_q)
                total = d[0, here] if k == 0 else e_d[side, k - 1, here]
                image = total * mid - mid_u * around - scaled
                p_out[at[k], out_rows] = mid
                i_out[at[k], out_rows] = image
                rz = rz + eight(b_r[at[k], here] * mid)
                pq = pq + eight(mid * image)
    lane = lax.broadcasted_iota(jnp.int32, total_out.shape, 1)
    rz, pq = jnp.sum(rz, keepdims=True), jnp.sum(pq, keepdims=True)
    total_out[...] = jnp.where(lane < total_out.shape[1] // 2, rz, pq)


def outer(found, x_even, x_odd, t_even, t_odd):
    p_in = found[2]
    parts = lax.axis_size("gx") * lax.axis_size("gy")
    layers, rows, lanes = p_in.shape
    grown = rows + 4 * HALO

    def field(*lead):
        return pltpu.VMEM((*lead, grown, lanes), F32)

    return pl.pallas_call(
        outer_kernel,
        out_shape=(
            shape(layers, rows, lanes), shape(layers, rows, lanes), shape(parts, lanes),
        ),
        in_specs=[VMEM] * 13,
        out_specs=(VMEM, VMEM, VMEM),
        scratch_shapes=[
            field(2), field(), field(2), field(2), field(3), field(3), field(3), field(), field(4),
        ],
        input_output_aliases={2: 0, 3: 1},
        compiler_params=params(4),
        name="outer",
    )(*found, x_even, x_odd, t_even, t_odd)


def update_kernel(sums, precond, image, resid, pressure, residual, held, sem):
    total = jnp.sum(sums[...], axis=0, keepdims=True)
    half = total.shape[1] // 2
    half_alpha = total[0:1, 0:1] / total[0:1, half : half + 1]
    alpha = 2.0 * half_alpha
    layers, rows, _ = precond.shape
    own = slice(LOW, LOW + rows)
    step = 4 if layers % 4 == 0 else layers
    started = []
    for start in range(0, layers, step):
        for k in range(start, start + step):
            held[0, k] = alpha * precond[k]
            held[1, k] = resid[k, own] - half_alpha * image[k]
        part = pl.ds(start, step)
        for i, out in enumerate((pressure, residual)):
            copy = pltpu.make_async_copy(
                held.at[i, part], out.at[part], sem.at[i, start // step]
            )
            copy.start()
            started.append(copy)
    for copy in started:
        copy.wait()


def update(sums, precond, image, resid):
    out = shape(*precond.shape)
    return pl.pallas_call(
        update_kernel,
        out_shape=(out, out),
        in_specs=[VMEM] * 4,
        out_specs=(HBM, HBM),
        scratch_shapes=[
            pltpu.VMEM((2, *precond.shape), F32),
            pltpu.SemaphoreType.DMA((2, precond.shape[0])),
        ],
        compiler_params=params(4),
        name="update",
    )(sums, precond, image, resid)


def on_device(right_side, conductivity):
    x_even, x_odd, y_even, y_odd = pack(conductivity, right_side)
    u, r = load(conductivity, right_side, y_even)
    y_even, y_odd = swap_y(y_even, 0), swap_y(y_odd, 1)
    x_even, x_odd = swap_x(x_even, 0), swap_x(x_odd, 1)
    t_even, t_odd = edge_terms(u, r, y_even, y_odd)
    t_even, t_odd = swap_x(t_even, 0), swap_x(t_odd, 1)
    found = inner(u, r, y_even, y_odd)
    precond, image, sums = outer(found, x_even, x_odd, t_even, t_odd)
    sums = lax.all_to_all(sums, ("gx", "gy"), 0, 0, tiled=True)
    return update(sums, precond, image, found[1])


def solution(mesh):
    in_specs = (P("gx", "gy", None), P("gx", "gy", None))
    out_specs = (P("gx", "gy", None), P("gx", "gy", None))
    return jax.shard_map(
        on_device, mesh=mesh, in_specs=in_specs, out_specs=out_specs, check_vma=False
    )
```

```python
import jax
import jax.numpy as jnp
from jax import lax
from jax.experimental import pallas as pl
from jax.experimental.pallas import tpu as pltpu
from jax.sharding import PartitionSpec as P

F32 = jnp.float32
HALO = 8
LOW = 2 * HALO
TINY = 1e-30
HBM = pl.BlockSpec(memory_space=pltpu.HBM)
VMEM = pl.BlockSpec(memory_space=pltpu.VMEM)


def params(mebibytes):
    return pltpu.CompilerParams(vmem_limit_bytes=mebibytes << 20)


def shape(*dims):
    return jax.ShapeDtypeStruct(dims, F32)


def swap(value, partner):
    count_x, count_y = lax.axis_size("gx"), lax.axis_size("gy")
    pairs = []
    for x in range(count_x):
        for y in range(count_y):
            to_x, to_y = partner(x, y)
            pairs.append((x * count_y + y, to_x * count_y + to_y))
    return lax.ppermute(value, ("gx", "gy"), pairs)


def swap_x(value, odd):
    count = lax.axis_size("gx")

    def partner(x, y):
        to = ((x + odd) ^ 1) - odd
        return (to, y) if 0 <= to < count else (x, y ^ 1)

    return swap(value, partner)


def swap_y(value, odd):
    count = lax.axis_size("gy")
    return swap(value, lambda x, y: (x, (((y + odd) ^ 1) - odd) % count))


def place(axis):
    index, count = lax.axis_index(axis), lax.axis_size(axis)
    odd = lax.rem(index, 2) == 1
    has_low = (index > 0).astype(F32)
    has_high = (index < count - 1).astype(F32)
    return odd, has_low, has_high


def z_sum(value):
    lane = lax.broadcasted_iota(jnp.int32, value.shape, 1)
    last = value.shape[1] - 1
    below = jnp.where(lane > 0, pltpu.roll(value, 1, 1), 0.0)
    above = jnp.where(lane < last, pltpu.roll(value, last, 1), 0.0)
    return below + above


def pack_kernel(cond, resid, x_even, x_odd, y_even, y_odd, tiles, sem):
    layers, rows, lanes = cond.shape
    odd = lax.rem(lax.axis_index("gx"), 2)
    x_copies, y_copies = [], []
    for out, high in ((x_even, 1 - odd), (x_odd, odd)):
        two = pl.ds(high * (layers - 2), 2)
        one = pl.ds(high * (layers - 1), 1)
        x_copies.append((cond.at[two], out.at[pl.ds(0, 2)]))
        x_copies.append((resid.at[one], out.at[pl.ds(2, 1)]))
    for side, start in enumerate((0, rows - HALO)):
        for part, source in enumerate((cond, resid)):
            y_copies.append((source.at[:, pl.ds(start, HALO)], tiles.at[side, part]))
    started = [
        pltpu.make_async_copy(source, target, sem.at[i])
        for i, (source, target) in enumerate(y_copies + x_copies)
    ]
    for copy in started:
        copy.start()
    for copy in started[:4]:
        copy.wait()
    odd = lax.rem(lax.axis_index("gy"), 2) == 1
    first = lax.broadcasted_iota(jnp.int32, (HALO, lanes), 0) < 3
    for k in range(layers):
        low = jnp.where(first, tiles[0, 0, k], pltpu.roll(tiles[0, 1, k], 3, 0))
        high = jnp.where(
            first, pltpu.roll(tiles[1, 0, k], 3, 0), pltpu.roll(tiles[1, 1, k], 5, 0)
        )
        y_even[k] = jnp.where(odd, low, high)
        y_odd[k] = jnp.where(odd, high, low)
    for copy in started[4:]:
        copy.wait()


def pack(cond, resid):
    layers, rows, lanes = cond.shape
    x_out, y_out = shape(3, rows, lanes), shape(layers, HALO, lanes)
    return pl.pallas_call(
        pack_kernel,
        out_shape=(x_out, x_out, y_out, y_out),
        in_specs=[HBM, HBM],
        out_specs=(VMEM,) * 4,
        scratch_shapes=[
            pltpu.VMEM((2, 2, layers, HALO, lanes), F32),
            pltpu.SemaphoreType.DMA((8,)),
        ],
        compiler_params=params(2),
        name="pack",
    )(
        pltpu.with_memory_space_constraint(cond, pltpu.HBM),
        pltpu.with_memory_space_constraint(resid, pltpu.HBM),
    )


def load_kernel(cond, resid, after, u, r, sem):
    own = pl.ds(LOW, cond.shape[1])
    copies = [
        pltpu.make_async_copy(source, target.at[:, own], sem.at[i])
        for i, (source, target) in enumerate(((cond, u), (resid, r)))
    ]
    for copy in copies:
        copy.start()
    for copy in copies:
        copy.wait()


def load(cond, resid, after):
    layers, rows, lanes = cond.shape
    grown = shape(layers, rows + 4 * HALO, lanes)
    return pl.pallas_call(
        load_kernel,
        out_shape=(grown, grown),
        in_specs=[HBM, HBM, VMEM],
        out_specs=(VMEM, VMEM),
        scratch_shapes=[pltpu.SemaphoreType.DMA((2,))],
        compiler_params=params(1),
        cost_estimate=pl.CostEstimate(
            flops=1_000_000_000, transcendentals=0, bytes_accessed=4 * cond.size
        ),
        name="load",
    )(
        pltpu.with_memory_space_constraint(cond, pltpu.HBM),
        pltpu.with_memory_space_constraint(resid, pltpu.HBM),
        after,
    )


def y_tiles(y_even, y_odd, layer, part):
    odd, has_low, has_high = place("gy")
    first, second = y_even[layer], y_odd[layer]
    row = lax.broadcasted_iota(jnp.int32, first.shape, 0)
    width = 3 - part
    south = pltpu.roll(jnp.where(odd, first, second), (5, 3)[part], 0)
    north = jnp.where(odd, second, first)
    if part:
        north = pltpu.roll(north, 5, 0)
    south = jnp.where(row >= HALO - width, south, 0.0) * has_low
    north = jnp.where(row < width, north, 0.0) * has_high
    return south, north


def edge_kernel(u, r, y_even, y_odd, t_even, t_odd, grown):
    layers, rows = u.shape[0], u.shape[1] - 4 * HALO
    odd = place("gx")[0]
    end = HALO + rows
    own = slice(LOW, LOW + rows)
    sends = []
    for side in range(2):
        edge, mid, far = ((0, 1, 2), (layers - 1, layers - 2, layers - 3))[side]
        south, north = y_tiles(y_even, y_odd, mid, 0)
        middle = u[mid, own]
        grown[side, 0:HALO] = south
        grown[side, HALO:end] = middle
        grown[side, end : end + HALO] = north
        total = 6.0 * middle + u[edge, own] + u[far, own] + z_sum(middle)
        total = total + grown[side, HALO - 1 : end - 1] + grown[side, HALO + 1 : end + 1]
        term = (u[edge, own] + middle) * (2.0 * r[mid, own] / total)
        edge_south, edge_north = y_tiles(y_even, y_odd, edge, 0)
        r_south, r_north = y_tiles(y_even, y_odd, edge, 1)
        corner = jnp.concatenate(
            [
                edge_south[HALO - 1 : HALO],
                edge_south[HALO - 2 : HALO - 1],
                south[HALO - 1 : HALO],
                r_south[HALO - 1 : HALO],
                edge_north[0:1],
                edge_north[1:2],
                north[0:1],
                r_north[0:1],
            ],
            axis=0,
        )
        sends.append((term, corner))
    (t_low, c_low), (t_high, c_high) = sends
    t_even[0:rows] = jnp.where(odd, t_low, t_high)
    t_even[rows : rows + 8] = jnp.where(odd, c_low, c_high)
    t_odd[0:rows] = jnp.where(odd, t_high, t_low)
    t_odd[rows : rows + 8] = jnp.where(odd, c_high, c_low)


def edge_terms(u, r, y_even, y_odd):
    rows, lanes = u.shape[1] - 4 * HALO, u.shape[2]
    return pl.pallas_call(
        edge_kernel,
        out_shape=(shape(rows + 8, lanes), shape(rows + 8, lanes)),
        in_specs=[VMEM] * 4,
        out_specs=(VMEM, VMEM),
        scratch_shapes=[pltpu.VMEM((2, rows + 2 * HALO, lanes), F32)],
        compiler_params=params(2),
        name="edge_terms",
    )(u, r, y_even, y_odd)


def row_chunks(rows):
    total = rows + 2 * HALO
    step = total // 3 if total % 24 == 0 else total
    return [(HALO + i * step, step) for i in range(total // step)]


def own_chunks(rows):
    step = 32 if rows % 32 == 0 else rows
    return [(LOW + i * step, step) for i in range(rows // step)]


def fill_rows(masks, rows):
    _, has_low, has_high = place("gy")
    row = lax.broadcasted_iota(jnp.int32, masks.shape[1:], 0) - LOW
    inside = jnp.where(row < 0, has_low, jnp.where(row >= rows, has_high, 1.0))
    near_low, near_high = row < 2, row >= rows - 2
    count = jnp.where(near_low, 1.0 + has_low, jnp.where(near_high, 1.0 + has_high, 1.0))
    masks[0] = inside
    masks[1] = count
    masks[2] = jnp.where(row == rows - 2, 1.0 / (1.0 + has_high), 1.0)
    masks[3] = jnp.where(row == 1, 1.0 / (1.0 + has_low), 1.0)


def is_plain(start, size, rows):
    return start >= LOW + 2 and start + size <= LOW + rows - 2


def eight(value):
    return jnp.sum(value.reshape(value.shape[0] // 8, 8, value.shape[1]), axis=0)


def inner_kernel(
    u_in, r_in, y_even, y_odd,
    u, r, p_out, i_out, e_v, e_i, e_d, e_p, sums,
    inv, v, w, d, p, q, masks,
):
    layers, rows = p_out.shape[0], p_out.shape[1]
    fill_rows(masks, rows)

    def halo(k, carry):
        for part, target in enumerate((u, r)):
            south, north = y_tiles(y_even, y_odd, k, part)
            target[k, HALO:LOW] = south
            target[k, LOW + rows : LOW + rows + HALO] = north
        return carry

    lax.fori_loop(0, layers, halo, 0, unroll=16)
    chunks = row_chunks(rows)

    def first(k, carry):
        for start, size in chunks:
            here = slice(start, start + size)
            down, up = slice(start - 1, start + size - 1), slice(start + 1, start + size + 1)
            mid = u[k, here]
            total = 6.0 * mid + u[k - 1, here] + u[k + 1, here]
            total = total + u[k, down] + u[k, up] + z_sum(mid)
            inverse = 1.0 / jnp.maximum(total, TINY)
            if not is_plain(start, size, rows):
                inverse = inverse * masks[0, here]
            value = 2.0 * r[k, here] * inverse
            d[k, here] = total
            inv[k, here] = inverse
            v[k, here] = value
            w[k, here] = mid * value
        return carry

    lax.fori_loop(1, layers - 1, first, 0, unroll=14)

    def second(k, carry):
        for start, size in chunks:
            here = slice(start, start + size)
            down, up = slice(start - 1, start + size - 1), slice(start + 1, start + size + 1)
            mid = u[k, here]
            total = 2.0 * r[k, here]
            total = total + mid * (v[k - 1, here] + v[k + 1, here] + z_sum(v[k, here]))
            total = total + (w[k - 1, here] + w[k + 1, here] + z_sum(w[k, here]))
            south = mid * v[k, down] + w[k, down]
            north = mid * v[k, up] + w[k, up]
            if is_plain(start, size, rows):
                value = inv[k, here] * (total + south + north)
            else:
                total = total + masks[2, here] * south + masks[3, here] * north
                value = masks[1, here] * inv[k, here] * total
            p[k, here] = value
            q[k, here] = mid * value
        return carry

    lax.fori_loop(2, layers - 2, second, 0, unroll=12)

    def third(k, carry):
        rz, pq = carry
        for start, size in own_chunks(rows):
            here = slice(start, start + size)
            down, up = slice(start - 1, start + size - 1), slice(start + 1, start + size + 1)
            mid = p[k, here]
            around = p[k - 1, here] + p[k + 1, here] + p[k, down] + p[k, up] + z_sum(mid)
            scaled = q[k - 1, here] + q[k + 1, here] + q[k, down] + q[k, up]
            scaled = scaled + z_sum(q[k, here])
            image = d[k, here] * mid - u[k, here] * around - scaled
            i_out[k, start - LOW : start - LOW + size] = image
            p_out[k, start - LOW : start - LOW + size] = mid
            rz = rz + eight(r[k, here] * mid)
            pq = pq + eight(mid * image)
        return rz, pq

    zero = jnp.zeros((8, u.shape[2]), F32)
    rz, pq = lax.fori_loop(3, layers - 3, third, (zero, zero), unroll=10)
    sums[0] = rz
    sums[1] = pq
    full = slice(HALO, LOW + rows + HALO)
    for side in range(2):
        order = (0, 1, 2, 3) if side == 0 else tuple(layers - 1 - k for k in range(4))
        for k in range(2):
            e_v[side, k, full] = v[order[k + 1], full]
            e_d[side, k, full] = d[order[k + 1], full]
            e_p[side, k, full] = p[order[k + 2], full]
        e_i[side, 0, full] = inv[order[1], full]


def inner(u, r, y_even, y_odd):
    layers, grown, lanes = u.shape
    rows = grown - 4 * HALO
    field = pltpu.VMEM((layers, grown, lanes), F32)

    def edge(count):
        return shape(2, count, grown, lanes)

    own, ext = shape(layers, rows, lanes), shape(layers, grown, lanes)
    outs = (ext, ext, own, own, edge(2), edge(1), edge(2), edge(2), shape(2, 8, lanes))
    return pl.pallas_call(
        inner_kernel,
        out_shape=outs,
        in_specs=[VMEM] * 4,
        out_specs=(VMEM,) * len(outs),
        scratch_shapes=[field] * 6 + [pltpu.VMEM((4, grown, lanes), F32)],
        input_output_aliases={0: 0, 1: 1},
        compiler_params=params(12),
        cost_estimate=pl.CostEstimate(flops=100_000_000, transcendentals=0, bytes_accessed=1),
        name="inner",
    )(u, r, y_even, y_odd)


def outer_kernel(
    b_u, b_r, p_in, i_in, e_v, e_i, e_d, e_p, sums, x_even, x_odd, t_even, t_odd,
    p_out, i_out, total_out,
    u, r, v, w, p, q, d, t, masks,
):
    layers, rows = p_in.shape[0], p_in.shape[1]
    odd, has_low, has_high = place("gx")
    fill_rows(masks, rows)
    own = slice(LOW, LOW + rows)
    zero = jnp.zeros((8, u.shape[2]), F32)
    rz, pq = sums[0], sums[1]
    chunks = row_chunks(rows)
    for side in range(2):
        at = tuple(k if side == 0 else layers - 1 - k for k in range(4))
        has = (has_low, has_high)[side]
        pick = jnp.logical_xor(odd, side == 1)
        twice = 1.0 + has

        def arrived(first, second):
            return jnp.where(pick, first, second) * has

        near, far = (1, 0) if side == 0 else (0, 1)
        for slot, source in ((0, far), (1, near)):
            u[slot, own] = arrived(x_even[source], x_odd[source])
        r[own] = arrived(x_even[2], x_odd[2])
        t[own] = arrived(t_even[0:rows], t_odd[0:rows])
        corner = arrived(t_even[rows : rows + 8], t_odd[rows : rows + 8])
        low, high = slice(HALO, LOW), slice(LOW + rows, LOW + rows + HALO)
        row = lax.broadcasted_iota(jnp.int32, zero.shape, 0)

        def one(k):
            return jnp.broadcast_to(corner[k : k + 1], zero.shape)

        u[1, low] = jnp.where(row == 7, one(0), jnp.where(row == 6, one(1), 0.0))
        u[0, low] = jnp.where(row == 7, one(2), 0.0)
        r[low] = jnp.where(row == 7, one(3), 0.0)
        u[1, high] = jnp.where(row == 0, one(4), jnp.where(row == 1, one(5), 0.0))
        u[0, high] = jnp.where(row == 0, one(6), 0.0)
        r[high] = jnp.where(row == 0, one(7), 0.0)
        t[low] = zero
        t[high] = zero

        for start, size in chunks:
            here = slice(start, start + size)
            down, up = slice(start - 1, start + size - 1), slice(start + 1, start + size + 1)
            inside = masks[0, here]
            mid, edge = u[1, here], b_u[at[0], here]
            total = 6.0 * mid + u[0, here] + edge + u[1, down] + u[1, up] + z_sum(mid)
            inverse = has * inside / jnp.maximum(total, TINY)
            value = 2.0 * r[here] * inverse
            d[1, here] = inverse
            v[0, here] = value
            w[0, here] = mid * value
            total = 6.0 * edge + mid + b_u[at[1], here]
            total = total + b_u[at[0], down] + b_u[at[0], up] + z_sum(edge)
            inverse = inside / jnp.maximum(total, TINY)
            value = 2.0 * b_r[at[0], here] * inverse
            d[0, here] = total
            d[2, here] = inverse
            v[1, here] = value
            w[1, here] = edge * value

        for start, size in chunks:
            here = slice(start, start + size)
            down, up = slice(start - 1, start + size - 1), slice(start + 1, start + size + 1)
            plain = is_plain(start, size, rows)

            def finish(mid, total, south, north, inverse, slot, twice):
                if plain:
                    value = twice * inverse * (total + south + north)
                else:
                    total = total + masks[2, here] * south + masks[3, here] * north
                    value = twice * masks[1, here] * inverse * total
                p[slot, here] = value
                q[slot, here] = mid * value

            mid = u[1, here]
            total = 2.0 * r[here] + t[here]
            total = total + mid * (v[1, here] + z_sum(v[0, here]))
            total = total + w[1, here] + z_sum(w[0, here])
            south = mid * v[0, down] + w[0, down]
            north = mid * v[0, up] + w[0, up]
            finish(mid, total, south, north, d[1, here], 0, twice)

            mid, next_u = b_u[at[0], here], b_u[at[1], here]
            next_v = e_v[side, 0, here]
            total = 2.0 * b_r[at[0], here]
            total = total + mid * (v[0, here] + next_v + z_sum(v[1, here]))
            total = total + w[0, here] + next_u * next_v + z_sum(w[1, here])
            south = mid * v[1, down] + w[1, down]
            north = mid * v[1, up] + w[1, up]
            finish(mid, total, south, north, d[2, here], 1, twice)

            inner_v = e_v[side, 1, here]
            total = 2.0 * b_r[at[1], here]
            total = total + next_u * (v[1, here] + z_sum(next_v))
            total = total + w[1, here] + z_sum(next_u * next_v)
            total = total + (next_u * inner_v + b_u[at[2], here] * inner_v) / twice
            south = (next_u + b_u[at[1], down]) * e_v[side, 0, down]
            north = (next_u + b_u[at[1], up]) * e_v[side, 0, up]
            finish(next_u, total, south, north, e_i[side, 0, here], 2, twice)

        for start, size in own_chunks(rows):
            here = slice(start, start + size)
            down, up = slice(start - 1, start + size - 1), slice(start + 1, start + size + 1)
            out_rows = slice(start - LOW, start - LOW + size)
            for k in range(3):
                mid_u = b_u[at[k], here]
                if k < 2:
                    mid = p[k + 1, here]
                    near_y = p[k + 1, down] + p[k + 1, up]
                    near_q = q[k + 1, down] + q[k + 1, up]
                    mid_q = q[k + 1, here]
                    before_p, before_q = p[k, here], q[k, here]
                    if k == 0:
                        after_p, after_q = p[2, here], q[2, here]
                    else:
                        after_p = e_p[side, 0, here]
                        after_q = b_u[at[2], here] * after_p
                else:
                    mid = e_p[side, 0, here]
                    mid_q = mid_u * mid
                    low_p, high_p = e_p[side, 0, down], e_p[side, 0, up]
                    near_y = low_p + high_p
                    near_q = b_u[at[2], down] * low_p + b_u[at[2], up] * high_p
                    before_p, before_q = p[2, here], q[2, here]
                    after_p = e_p[side, 1, here]
                    after_q = None
                around = before_p + after_p + near_y + z_sum(mid)
                if after_q is None:
                    after_q = b_u[at[3], here] * after_p
                scaled = before_q + after_q + near_q + z_sum(mid_q)
                total = d[0, here] if k == 0 else e_d[side, k - 1, here]
                image = total * mid - mid_u * around - scaled
                p_out[at[k], out_rows] = mid
                i_out[at[k], out_rows] = image
                rz = rz + eight(b_r[at[k], here] * mid)
                pq = pq + eight(mid * image)
    lane = lax.broadcasted_iota(jnp.int32, total_out.shape, 1)
    rz, pq = jnp.sum(rz, keepdims=True), jnp.sum(pq, keepdims=True)
    total_out[...] = jnp.where(lane < total_out.shape[1] // 2, rz, pq)


def outer(found, x_even, x_odd, t_even, t_odd):
    p_in = found[2]
    parts = lax.axis_size("gx") * lax.axis_size("gy")
    layers, rows, lanes = p_in.shape
    grown = rows + 4 * HALO

    def field(*lead):
        return pltpu.VMEM((*lead, grown, lanes), F32)

    return pl.pallas_call(
        outer_kernel,
        out_shape=(
            shape(layers, rows, lanes), shape(layers, rows, lanes), shape(parts, lanes),
        ),
        in_specs=[VMEM] * 13,
        out_specs=(VMEM, VMEM, VMEM),
        scratch_shapes=[
            field(2), field(), field(2), field(2), field(3), field(3), field(3), field(), field(4),
        ],
        input_output_aliases={2: 0, 3: 1},
        compiler_params=params(4),
        name="outer",
    )(*found, x_even, x_odd, t_even, t_odd)


def update_kernel(sums, precond, image, resid, pressure, residual, held, sem):
    total = jnp.sum(sums[...], axis=0, keepdims=True)
    half = total.shape[1] // 2
    half_alpha = total[0:1, 0:1] / total[0:1, half : half + 1]
    alpha = 2.0 * half_alpha
    layers, rows, _ = precond.shape
    own = slice(LOW, LOW + rows)
    step = 4 if layers % 4 == 0 else layers
    started = []
    for start in range(0, layers, step):
        for k in range(start, start + step):
            held[0, k] = alpha * precond[k]
            held[1, k] = resid[k, own] - half_alpha * image[k]
        part = pl.ds(start, step)
        for i, out in enumerate((pressure, residual)):
            copy = pltpu.make_async_copy(
                held.at[i, part], out.at[part], sem.at[i, start // step]
            )
            copy.start()
            started.append(copy)
    for copy in started:
        copy.wait()


def update(sums, precond, image, resid):
    out = shape(*precond.shape)
    return pl.pallas_call(
        update_kernel,
        out_shape=(out, out),
        in_specs=[VMEM] * 4,
        out_specs=(HBM, HBM),
        scratch_shapes=[
            pltpu.VMEM((2, *precond.shape), F32),
            pltpu.SemaphoreType.DMA((2, precond.shape[0])),
        ],
        compiler_params=params(4),
        name="update",
    )(sums, precond, image, resid)


def on_device(right_side, conductivity):
    x_even, x_odd, y_even, y_odd = pack(conductivity, right_side)
    u, r = load(conductivity, right_side, y_even)
    y_even, y_odd = swap_y(y_even, 0), swap_y(y_odd, 1)
    x_even, x_odd = swap_x(x_even, 0), swap_x(x_odd, 1)
    t_even, t_odd = edge_terms(u, r, y_even, y_odd)
    t_even, t_odd = swap_x(t_even, 0), swap_x(t_odd, 1)
    found = inner(u, r, y_even, y_odd)
    precond, image, sums = outer(found, x_even, x_odd, t_even, t_odd)
    sums = lax.all_to_all(sums, ("gx", "gy"), 0, 0, tiled=True)
    return update(sums, precond, image, found[1])


def solution(mesh):
    in_specs = (P("gx", "gy", None), P("gx", "gy", None))
    out_specs = (P("gx", "gy", None), P("gx", "gy", None))
    return jax.shard_map(
        on_device, mesh=mesh, in_specs=in_specs, out_specs=out_specs, check_vma=False
    )
```

```python
import jax
import jax.numpy as jnp
from jax import lax
from jax.experimental import pallas as pl
from jax.experimental.pallas import tpu as pltpu
from jax.sharding import PartitionSpec as P

F32 = jnp.float32
HALO = 8
LOW = 2 * HALO
TINY = 1e-30
HBM = pl.BlockSpec(memory_space=pltpu.HBM)
VMEM = pl.BlockSpec(memory_space=pltpu.VMEM)


def params(mebibytes):
    return pltpu.CompilerParams(vmem_limit_bytes=mebibytes << 20)


def shape(*dims):
    return jax.ShapeDtypeStruct(dims, F32)


def swap(value, partner):
    count_x, count_y = lax.axis_size("gx"), lax.axis_size("gy")
    pairs = []
    for x in range(count_x):
        for y in range(count_y):
            to_x, to_y = partner(x, y)
            pairs.append((x * count_y + y, to_x * count_y + to_y))
    return lax.ppermute(value, ("gx", "gy"), pairs)


def swap_x(value, odd):
    count = lax.axis_size("gx")

    def partner(x, y):
        to = ((x + odd) ^ 1) - odd
        return (to, y) if 0 <= to < count else (x, y ^ 1)

    return swap(value, partner)


def swap_y(value, odd):
    count = lax.axis_size("gy")
    return swap(value, lambda x, y: (x, (((y + odd) ^ 1) - odd) % count))


def place(axis):
    index, count = lax.axis_index(axis), lax.axis_size(axis)
    odd = lax.rem(index, 2) == 1
    has_low = (index > 0).astype(F32)
    has_high = (index < count - 1).astype(F32)
    return odd, has_low, has_high


def z_sum(value):
    lane = lax.broadcasted_iota(jnp.int32, value.shape, 1)
    last = value.shape[1] - 1
    below = jnp.where(lane > 0, pltpu.roll(value, 1, 1), 0.0)
    above = jnp.where(lane < last, pltpu.roll(value, last, 1), 0.0)
    return below + above


def pack_kernel(cond, resid, x_even, x_odd, y_even, y_odd, tiles, sem):
    layers, rows, lanes = cond.shape
    odd = lax.rem(lax.axis_index("gx"), 2)
    x_copies, y_copies = [], []
    for out, high in ((x_even, 1 - odd), (x_odd, odd)):
        two = pl.ds(high * (layers - 2), 2)
        one = pl.ds(high * (layers - 1), 1)
        x_copies.append((cond.at[two], out.at[pl.ds(0, 2)]))
        x_copies.append((resid.at[one], out.at[pl.ds(2, 1)]))
    for side, start in enumerate((0, rows - HALO)):
        for part, source in enumerate((cond, resid)):
            y_copies.append((source.at[:, pl.ds(start, HALO)], tiles.at[side, part]))
    started = [
        pltpu.make_async_copy(source, target, sem.at[i])
        for i, (source, target) in enumerate(y_copies + x_copies)
    ]
    for copy in started:
        copy.start()
    for copy in started[:4]:
        copy.wait()
    odd = lax.rem(lax.axis_index("gy"), 2) == 1
    first = lax.broadcasted_iota(jnp.int32, (HALO, lanes), 0) < 3
    for k in range(layers):
        low = jnp.where(first, tiles[0, 0, k], pltpu.roll(tiles[0, 1, k], 3, 0))
        high = jnp.where(
            first, pltpu.roll(tiles[1, 0, k], 3, 0), pltpu.roll(tiles[1, 1, k], 5, 0)
        )
        y_even[k] = jnp.where(odd, low, high)
        y_odd[k] = jnp.where(odd, high, low)
    for copy in started[4:]:
        copy.wait()


def pack(cond, resid):
    layers, rows, lanes = cond.shape
    x_out, y_out = shape(3, rows, lanes), shape(layers, HALO, lanes)
    return pl.pallas_call(
        pack_kernel,
        out_shape=(x_out, x_out, y_out, y_out),
        in_specs=[HBM, HBM],
        out_specs=(VMEM,) * 4,
        scratch_shapes=[
            pltpu.VMEM((2, 2, layers, HALO, lanes), F32),
            pltpu.SemaphoreType.DMA((8,)),
        ],
        compiler_params=params(2),
        name="pack",
    )(
        pltpu.with_memory_space_constraint(cond, pltpu.HBM),
        pltpu.with_memory_space_constraint(resid, pltpu.HBM),
    )


def load_kernel(cond, resid, after, u, r, sem):
    own = pl.ds(LOW, cond.shape[1])
    copies = [
        pltpu.make_async_copy(source, target.at[:, own], sem.at[i])
        for i, (source, target) in enumerate(((cond, u), (resid, r)))
    ]
    for copy in copies:
        copy.start()
    for copy in copies:
        copy.wait()


def load(cond, resid, after):
    layers, rows, lanes = cond.shape
    grown = shape(layers, rows + 4 * HALO, lanes)
    return pl.pallas_call(
        load_kernel,
        out_shape=(grown, grown),
        in_specs=[HBM, HBM, VMEM],
        out_specs=(VMEM, VMEM),
        scratch_shapes=[pltpu.SemaphoreType.DMA((2,))],
        compiler_params=params(1),
        cost_estimate=pl.CostEstimate(
            flops=1_000_000_000, transcendentals=0, bytes_accessed=4 * cond.size
        ),
        name="load",
    )(
        pltpu.with_memory_space_constraint(cond, pltpu.HBM),
        pltpu.with_memory_space_constraint(resid, pltpu.HBM),
        after,
    )


def y_tiles(y_even, y_odd, layer, part):
    odd, has_low, has_high = place("gy")
    first, second = y_even[layer], y_odd[layer]
    row = lax.broadcasted_iota(jnp.int32, first.shape, 0)
    width = 3 - part
    south = pltpu.roll(jnp.where(odd, first, second), (5, 3)[part], 0)
    north = jnp.where(odd, second, first)
    if part:
        north = pltpu.roll(north, 5, 0)
    south = jnp.where(row >= HALO - width, south, 0.0) * has_low
    north = jnp.where(row < width, north, 0.0) * has_high
    return south, north


def edge_kernel(u, r, y_even, y_odd, t_even, t_odd, grown):
    layers, rows = u.shape[0], u.shape[1] - 4 * HALO
    odd = place("gx")[0]
    end = HALO + rows
    own = slice(LOW, LOW + rows)
    sends = []
    for side in range(2):
        edge, mid, far = ((0, 1, 2), (layers - 1, layers - 2, layers - 3))[side]
        south, north = y_tiles(y_even, y_odd, mid, 0)
        middle = u[mid, own]
        grown[side, 0:HALO] = south
        grown[side, HALO:end] = middle
        grown[side, end : end + HALO] = north
        total = 6.0 * middle + u[edge, own] + u[far, own] + z_sum(middle)
        total = total + grown[side, HALO - 1 : end - 1] + grown[side, HALO + 1 : end + 1]
        term = (u[edge, own] + middle) * (2.0 * r[mid, own] / total)
        edge_south, edge_north = y_tiles(y_even, y_odd, edge, 0)
        r_south, r_north = y_tiles(y_even, y_odd, edge, 1)
        corner = jnp.concatenate(
            [
                edge_south[HALO - 1 : HALO],
                edge_south[HALO - 2 : HALO - 1],
                south[HALO - 1 : HALO],
                r_south[HALO - 1 : HALO],
                edge_north[0:1],
                edge_north[1:2],
                north[0:1],
                r_north[0:1],
            ],
            axis=0,
        )
        sends.append((term, corner))
    (t_low, c_low), (t_high, c_high) = sends
    t_even[0:rows] = jnp.where(odd, t_low, t_high)
    t_even[rows : rows + 8] = jnp.where(odd, c_low, c_high)
    t_odd[0:rows] = jnp.where(odd, t_high, t_low)
    t_odd[rows : rows + 8] = jnp.where(odd, c_high, c_low)


def edge_terms(u, r, y_even, y_odd):
    rows, lanes = u.shape[1] - 4 * HALO, u.shape[2]
    return pl.pallas_call(
        edge_kernel,
        out_shape=(shape(rows + 8, lanes), shape(rows + 8, lanes)),
        in_specs=[VMEM] * 4,
        out_specs=(VMEM, VMEM),
        scratch_shapes=[pltpu.VMEM((2, rows + 2 * HALO, lanes), F32)],
        compiler_params=params(2),
        name="edge_terms",
    )(u, r, y_even, y_odd)


def row_chunks(rows):
    total = rows + 2 * HALO
    step = total // 3 if total % 24 == 0 else total
    return [(HALO + i * step, step) for i in range(total // step)]


def own_chunks(rows):
    step = 32 if rows % 32 == 0 else rows
    return [(LOW + i * step, step) for i in range(rows // step)]


def fill_rows(masks, rows):
    _, has_low, has_high = place("gy")
    row = lax.broadcasted_iota(jnp.int32, masks.shape[1:], 0) - LOW
    inside = jnp.where(row < 0, has_low, jnp.where(row >= rows, has_high, 1.0))
    near_low, near_high = row < 2, row >= rows - 2
    count = jnp.where(near_low, 1.0 + has_low, jnp.where(near_high, 1.0 + has_high, 1.0))
    masks[0] = inside
    masks[1] = count
    masks[2] = jnp.where(row == rows - 2, 1.0 / (1.0 + has_high), 1.0)
    masks[3] = jnp.where(row == 1, 1.0 / (1.0 + has_low), 1.0)


def is_plain(start, size, rows):
    return start >= LOW + 2 and start + size <= LOW + rows - 2


def eight(value):
    return jnp.sum(value.reshape(value.shape[0] // 8, 8, value.shape[1]), axis=0)


def inner_kernel(
    u_in, r_in, y_even, y_odd,
    u, r, p_out, i_out, e_v, e_i, e_d, e_p, sums,
    inv, v, w, d, p, q, masks,
):
    layers, rows = p_out.shape[0], p_out.shape[1]
    fill_rows(masks, rows)

    def halo(k, carry):
        for part, target in enumerate((u, r)):
            south, north = y_tiles(y_even, y_odd, k, part)
            target[k, HALO:LOW] = south
            target[k, LOW + rows : LOW + rows + HALO] = north
        return carry

    lax.fori_loop(0, layers, halo, 0, unroll=16)
    chunks = row_chunks(rows)

    def first(k, carry):
        for start, size in chunks:
            here = slice(start, start + size)
            down, up = slice(start - 1, start + size - 1), slice(start + 1, start + size + 1)
            mid = u[k, here]
            total = 6.0 * mid + u[k - 1, here] + u[k + 1, here]
            total = total + u[k, down] + u[k, up] + z_sum(mid)
            inverse = 1.0 / jnp.maximum(total, TINY)
            if not is_plain(start, size, rows):
                inverse = inverse * masks[0, here]
            value = 2.0 * r[k, here] * inverse
            d[k, here] = total
            inv[k, here] = inverse
            v[k, here] = value
            w[k, here] = mid * value
        return carry

    lax.fori_loop(1, layers - 1, first, 0, unroll=14)

    def second(k, carry):
        for start, size in chunks:
            here = slice(start, start + size)
            down, up = slice(start - 1, start + size - 1), slice(start + 1, start + size + 1)
            mid = u[k, here]
            total = 2.0 * r[k, here]
            total = total + mid * (v[k - 1, here] + v[k + 1, here] + z_sum(v[k, here]))
            total = total + (w[k - 1, here] + w[k + 1, here] + z_sum(w[k, here]))
            south = mid * v[k, down] + w[k, down]
            north = mid * v[k, up] + w[k, up]
            if is_plain(start, size, rows):
                value = inv[k, here] * (total + south + north)
            else:
                total = total + masks[2, here] * south + masks[3, here] * north
                value = masks[1, here] * inv[k, here] * total
            p[k, here] = value
            q[k, here] = mid * value
        return carry

    lax.fori_loop(2, layers - 2, second, 0, unroll=12)

    def third(k, carry):
        rz, pq = carry
        for start, size in own_chunks(rows):
            here = slice(start, start + size)
            down, up = slice(start - 1, start + size - 1), slice(start + 1, start + size + 1)
            mid = p[k, here]
            around = p[k - 1, here] + p[k + 1, here] + p[k, down] + p[k, up] + z_sum(mid)
            scaled = q[k - 1, here] + q[k + 1, here] + q[k, down] + q[k, up]
            scaled = scaled + z_sum(q[k, here])
            image = d[k, here] * mid - u[k, here] * around - scaled
            i_out[k, start - LOW : start - LOW + size] = image
            p_out[k, start - LOW : start - LOW + size] = mid
            rz = rz + eight(r[k, here] * mid)
            pq = pq + eight(mid * image)
        return rz, pq

    zero = jnp.zeros((8, u.shape[2]), F32)
    rz, pq = lax.fori_loop(3, layers - 3, third, (zero, zero), unroll=10)
    sums[0] = rz
    sums[1] = pq
    full = slice(HALO, LOW + rows + HALO)
    for side in range(2):
        order = (0, 1, 2, 3) if side == 0 else tuple(layers - 1 - k for k in range(4))
        for k in range(2):
            e_v[side, k, full] = v[order[k + 1], full]
            e_d[side, k, full] = d[order[k + 1], full]
            e_p[side, k, full] = p[order[k + 2], full]
        e_i[side, 0, full] = inv[order[1], full]


def inner(u, r, y_even, y_odd):
    layers, grown, lanes = u.shape
    rows = grown - 4 * HALO
    field = pltpu.VMEM((layers, grown, lanes), F32)

    def edge(count):
        return shape(2, count, grown, lanes)

    own, ext = shape(layers, rows, lanes), shape(layers, grown, lanes)
    outs = (ext, ext, own, own, edge(2), edge(1), edge(2), edge(2), shape(2, 8, lanes))
    return pl.pallas_call(
        inner_kernel,
        out_shape=outs,
        in_specs=[VMEM] * 4,
        out_specs=(VMEM,) * len(outs),
        scratch_shapes=[field] * 6 + [pltpu.VMEM((4, grown, lanes), F32)],
        input_output_aliases={0: 0, 1: 1},
        compiler_params=params(12),
        cost_estimate=pl.CostEstimate(flops=100_000_000, transcendentals=0, bytes_accessed=1),
        name="inner",
    )(u, r, y_even, y_odd)


def around_rows(start, size):
    return (
        slice(start, start + size),
        slice(start - 1, start + size - 1),
        slice(start + 1, start + size + 1),
    )


def side_layers(layers, side):
    return tuple(k if side == 0 else layers - 1 - k for k in range(4))


def side_place(side):
    odd, has_low, has_high = place("gx")
    has = (has_low, has_high)[side]
    pick = jnp.logical_xor(odd, side == 1)

    def arrived(first, second):
        return jnp.where(pick, first, second) * has

    return has, 1.0 + has, arrived


def start_fields(own, near, side, chunk):
    b_u, b_r = own[:2]
    u, r, v, w, _, _, d, inv, masks = near
    at = side_layers(b_u.shape[0], side)
    has = side_place(side)[0]
    here, down, up = around_rows(*chunk)
    inside = masks[0, here]
    mid, edge = u[side, 1, here], b_u[at[0], here]
    total = 6.0 * mid + u[side, 0, here] + edge
    total = total + u[side, 1, down] + u[side, 1, up] + z_sum(mid)
    inverse = has * inside / jnp.maximum(total, TINY)
    value = 2.0 * r[side, here] * inverse
    inv[side, 0, here] = inverse
    v[side, 0, here] = value
    w[side, 0, here] = mid * value
    total = 6.0 * edge + mid + b_u[at[1], here]
    total = total + b_u[at[0], down] + b_u[at[0], up] + z_sum(edge)
    inverse = inside / jnp.maximum(total, TINY)
    value = 2.0 * b_r[at[0], here] * inverse
    d[side, here] = total
    inv[side, 1, here] = inverse
    v[side, 1, here] = value
    w[side, 1, here] = edge * value


def precond_fields(own, near, side, chunk, rows, term):
    b_u, b_r, e_v, e_i = own[:4]
    u, r, v, w, p, q, _, inv, masks = near
    at = side_layers(b_u.shape[0], side)
    twice = side_place(side)[1]
    here, down, up = around_rows(*chunk)
    plain = is_plain(*chunk, rows)

    def finish(mid, total, south, north, inverse, slot):
        scale = twice * inverse
        if plain:
            total = total + south + north
        else:
            total = total + masks[2, here] * south + masks[3, here] * north
            scale = scale * masks[1, here]
        value = scale * total
        p[side, slot, here] = value
        q[side, slot, here] = mid * value
        return scale

    mid = u[side, 1, here]
    total = 2.0 * r[side, here]
    if term is not None:
        total = total + term
    total = total + mid * (v[side, 1, here] + z_sum(v[side, 0, here]))
    total = total + w[side, 1, here] + z_sum(w[side, 0, here])
    south = mid * v[side, 0, down] + w[side, 0, down]
    north = mid * v[side, 0, up] + w[side, 0, up]
    inv[side, 0, here] = finish(mid, total, south, north, inv[side, 0, here], 0)

    mid, next_u = b_u[at[0], here], b_u[at[1], here]
    next_v = e_v[side, 0, here]
    total = 2.0 * b_r[at[0], here]
    total = total + mid * (v[side, 0, here] + next_v + z_sum(v[side, 1, here]))
    total = total + w[side, 0, here] + next_u * next_v + z_sum(w[side, 1, here])
    south = mid * v[side, 1, down] + w[side, 1, down]
    north = mid * v[side, 1, up] + w[side, 1, up]
    finish(mid, total, south, north, inv[side, 1, here], 1)

    inner_v = e_v[side, 1, here]
    total = 2.0 * b_r[at[1], here]
    total = total + next_u * (v[side, 1, here] + z_sum(next_v))
    total = total + w[side, 1, here] + z_sum(next_u * next_v)
    total = total + (next_u + b_u[at[2], here]) * inner_v / twice
    south = (next_u + b_u[at[1], down]) * e_v[side, 0, down]
    north = (next_u + b_u[at[1], up]) * e_v[side, 0, up]
    finish(next_u, total, south, north, e_i[side, 0, here], 2)


def image_fields(own, near, side, chunk, k, p_out, i_out):
    b_u, b_r, _, _, e_d, e_p = own
    _, _, _, _, p, q, d, _, _ = near
    at = side_layers(b_u.shape[0], side)
    here, down, up = around_rows(*chunk)
    mid_u = b_u[at[k], here]
    if k < 2:
        mid, mid_q = p[side, k + 1, here], q[side, k + 1, here]
        near_y = p[side, k + 1, down] + p[side, k + 1, up]
        near_q = q[side, k + 1, down] + q[side, k + 1, up]
        before_p, before_q = p[side, k, here], q[side, k, here]
        if k == 0:
            after_p, after_q = p[side, 2, here], q[side, 2, here]
        else:
            after_p = e_p[side, 0, here]
            after_q = b_u[at[2], here] * after_p
    else:
        mid = e_p[side, 0, here]
        mid_q = mid_u * mid
        low_p, high_p = e_p[side, 0, down], e_p[side, 0, up]
        near_y = low_p + high_p
        near_q = b_u[at[2], down] * low_p + b_u[at[2], up] * high_p
        before_p, before_q = p[side, 2, here], q[side, 2, here]
        after_p = e_p[side, 1, here]
        after_q = b_u[at[3], here] * after_p
    around = before_p + after_p + near_y + z_sum(mid)
    scaled = before_q + after_q + near_q + z_sum(mid_q)
    total = d[side, here] if k == 0 else e_d[side, k - 1, here]
    image = total * mid - mid_u * around - scaled
    out = slice(chunk[0] - LOW, chunk[0] - LOW + chunk[1])
    p_out[at[k], out] = mid
    i_out[at[k], out] = image
    return eight(b_r[at[k], here] * mid), eight(mid * image)


def middle_chunks(rows):
    rest = rows - 2 * HALO
    step = rest // 2 if rest % 16 == 0 else rest
    return [(LOW + HALO + i * step, step) for i in range(rest // step)]


def outer_kernel(
    b_u, b_r, p_in, i_in, e_v, e_i, e_d, e_p, sums, x_even, x_odd,
    p_out, i_out, sums_out, *near,
):
    rows = p_in.shape[1]
    u, r, masks = near[0], near[1], near[-1]
    fill_rows(masks, rows)
    own = (b_u, b_r, e_v, e_i, e_d, e_p)
    here = slice(LOW, LOW + rows)
    rz, pq = sums[0], sums[1]
    zero = jnp.zeros(rz.shape, F32)
    for side in range(2):
        arrived = side_place(side)[2]
        for slot in range(2):
            layer = slot if side == 0 else 1 - slot
            u[side, slot, here] = arrived(x_even[layer], x_odd[layer])
        r[side, here] = arrived(x_even[2], x_odd[2])
        for rest in (slice(HALO, LOW), slice(LOW + rows, LOW + rows + HALO)):
            u[side, 0, rest] = zero
            u[side, 1, rest] = zero
            r[side, rest] = zero
        for chunk in row_chunks(rows):
            start_fields(own, near, side, chunk)
        for chunk in row_chunks(rows):
            precond_fields(own, near, side, chunk, rows, None)
        for chunk in own_chunks(rows):
            add_rz, add_pq = image_fields(own, near, side, chunk, 2, p_out, i_out)
            rz, pq = rz + add_rz, pq + add_pq
        for chunk in middle_chunks(rows):
            add_rz, add_pq = image_fields(own, near, side, chunk, 1, p_out, i_out)
            rz, pq = rz + add_rz, pq + add_pq
            rz = rz + image_fields(own, near, side, chunk, 0, p_out, i_out)[0]
    sums_out[0] = rz
    sums_out[1] = pq


def corner_kernel(
    b_u, b_r, p_in, i_in, e_v, e_i, e_d, e_p, sums, t_even, t_odd, masks, *refs,
):
    old, (p_out, i_out, total_out), fields = refs[:8], refs[8:11], refs[11:]
    near = (*fields, masks)
    rows = p_in.shape[1]
    u, r, p, inv = near[0], near[1], near[4], near[7]
    own = (b_u, b_r, e_v, e_i, e_d, e_p)
    rz, pq = sums[0], sums[1]
    zero = jnp.zeros(rz.shape, F32)
    row = lax.broadcasted_iota(jnp.int32, zero.shape, 0)
    low, high = slice(HALO, LOW), slice(LOW + rows, LOW + rows + HALO)
    for side in range(2):
        at = side_layers(b_u.shape[0], side)
        arrived = side_place(side)[2]
        corner = arrived(t_even[rows : rows + 8], t_odd[rows : rows + 8])

        def one(k):
            return jnp.broadcast_to(corner[k : k + 1], zero.shape)

        u[side, 1, low] = jnp.where(row == 7, one(0), jnp.where(row == 6, one(1), 0.0))
        u[side, 0, low] = jnp.where(row == 7, one(2), 0.0)
        r[side, low] = jnp.where(row == 7, one(3), 0.0)
        u[side, 1, high] = jnp.where(row == 0, one(4), jnp.where(row == 1, one(5), 0.0))
        u[side, 0, high] = jnp.where(row == 0, one(6), 0.0)
        r[side, high] = jnp.where(row == 0, one(7), 0.0)
        for band in range(2):
            if band == 0:
                term = [zero, arrived(t_even[0:HALO], t_odd[0:HALO])]
                chunk, tile = (HALO, 2 * HALO), (LOW, HALO)
            else:
                tail = slice(rows - HALO, rows)
                term = [arrived(t_even[tail], t_odd[tail]), zero]
                chunk = (LOW + rows - HALO, 2 * HALO)
                tile = (LOW + rows - HALO, HALO)
            start_fields(own, near, side, chunk)
            precond_fields(own, near, side, chunk, rows, jnp.concatenate(term, axis=0))
            for k in range(2):
                add_rz, add_pq = image_fields(own, near, side, tile, k, p_out, i_out)
                rz, pq = rz + add_rz, pq + add_pq
        for start, size in middle_chunks(rows):
            here = slice(start, start + size)
            out = slice(start - LOW, start - LOW + size)
            change = inv[side, 0, here] * arrived(t_even[out], t_odd[out])
            image = i_in[at[0], out] - (b_u[at[0], here] + u[side, 1, here]) * change
            i_out[at[0], out] = image
            pq = pq + eight(p[side, 1, here] * image)
    lane = lax.broadcasted_iota(jnp.int32, total_out.shape, 1)
    rz, pq = jnp.sum(rz, keepdims=True), jnp.sum(pq, keepdims=True)
    total_out[...] = jnp.where(lane < total_out.shape[1] // 2, rz, pq)


def outer(found, x_even, x_odd):
    layers, rows, lanes = found[2].shape
    grown = rows + 4 * HALO
    full = shape(layers, rows, lanes)
    sizes = ((2, 2), (2,), (2, 2), (2, 2), (2, 3), (2, 3), (2,), (2, 2), (4,))
    near = tuple(shape(*size, grown, lanes) for size in sizes)
    return pl.pallas_call(
        outer_kernel,
        out_shape=(full, full, shape(2, 8, lanes), *near),
        in_specs=[VMEM] * 11,
        out_specs=(VMEM,) * (3 + len(near)),
        input_output_aliases={2: 0, 3: 1},
        compiler_params=params(4),
        name="outer",
    )(*found, x_even, x_odd)


def corners(found, first, t_even, t_odd):
    layers, rows, lanes = found[2].shape
    parts = lax.axis_size("gx") * lax.axis_size("gy")
    p, i, sums, *near, masks = first
    u, r, _, _, e_v, e_i, e_d, e_p, _ = found
    full = shape(layers, rows, lanes)
    fields = tuple(shape(*field.shape) for field in near)
    return pl.pallas_call(
        corner_kernel,
        out_shape=(full, full, shape(parts, lanes), *fields),
        in_specs=[VMEM] * (12 + len(near)),
        out_specs=(VMEM,) * (3 + len(near)),
        input_output_aliases={2: 0, 3: 1, **{12 + k: 3 + k for k in range(len(near))}},
        compiler_params=params(4),
        name="corners",
    )(u, r, p, i, e_v, e_i, e_d, e_p, sums, t_even, t_odd, masks, *near)[:3]


def update_kernel(sums, precond, image, resid, pressure, residual, held, sem):
    total = jnp.sum(sums[...], axis=0, keepdims=True)
    half = total.shape[1] // 2
    half_alpha = total[0:1, 0:1] / total[0:1, half : half + 1]
    alpha = 2.0 * half_alpha
    layers, rows, _ = precond.shape
    own = slice(LOW, LOW + rows)
    step = 4 if layers % 4 == 0 else layers
    started = []
    for start in range(0, layers, step):
        for k in range(start, start + step):
            held[0, k] = alpha * precond[k]
            held[1, k] = resid[k, own] - half_alpha * image[k]
        part = pl.ds(start, step)
        for i, out in enumerate((pressure, residual)):
            copy = pltpu.make_async_copy(
                held.at[i, part], out.at[part], sem.at[i, start // step]
            )
            copy.start()
            started.append(copy)
    for copy in started:
        copy.wait()


def update(sums, precond, image, resid):
    out = shape(*precond.shape)
    return pl.pallas_call(
        update_kernel,
        out_shape=(out, out),
        in_specs=[VMEM] * 4,
        out_specs=(HBM, HBM),
        scratch_shapes=[
            pltpu.VMEM((2, *precond.shape), F32),
            pltpu.SemaphoreType.DMA((2, precond.shape[0])),
        ],
        compiler_params=params(4),
        name="update",
    )(sums, precond, image, resid)


def on_device(right_side, conductivity):
    x_even, x_odd, y_even, y_odd = pack(conductivity, right_side)
    u, r = load(conductivity, right_side, y_even)
    y_even, y_odd = swap_y(y_even, 0), swap_y(y_odd, 1)
    x_even, x_odd = swap_x(x_even, 0), swap_x(x_odd, 1)
    t_even, t_odd = edge_terms(u, r, y_even, y_odd)
    t_even, t_odd = swap_x(t_even, 0), swap_x(t_odd, 1)
    found = inner(u, r, y_even, y_odd)
    first = outer(found, x_even, x_odd)
    precond, image, sums = corners(found, first, t_even, t_odd)
    sums = lax.all_to_all(sums, ("gx", "gy"), 0, 0, tiled=True)
    return update(sums, precond, image, found[1])


def solution(mesh):
    in_specs = (P("gx", "gy", None), P("gx", "gy", None))
    out_specs = (P("gx", "gy", None), P("gx", "gy", None))
    return jax.shard_map(
        on_device, mesh=mesh, in_specs=in_specs, out_specs=out_specs, check_vma=False
    )
```

```python
import jax
import jax.numpy as jnp
from jax import lax
from jax.experimental import pallas as pl
from jax.experimental.pallas import tpu as pltpu
from jax.sharding import PartitionSpec as P

F32 = jnp.float32
HALO = 8
LOW = 2 * HALO
TINY = 1e-30
HBM = pl.BlockSpec(memory_space=pltpu.HBM)
VMEM = pl.BlockSpec(memory_space=pltpu.VMEM)


def params(mebibytes):
    return pltpu.CompilerParams(vmem_limit_bytes=mebibytes << 20)


def shape(*dims):
    return jax.ShapeDtypeStruct(dims, F32)


def swap(value, partner):
    count_x, count_y = lax.axis_size("gx"), lax.axis_size("gy")
    pairs = []
    for x in range(count_x):
        for y in range(count_y):
            to_x, to_y = partner(x, y)
            pairs.append((x * count_y + y, to_x * count_y + to_y))
    return lax.ppermute(value, ("gx", "gy"), pairs)


def swap_x(value, odd):
    count = lax.axis_size("gx")

    def partner(x, y):
        to = ((x + odd) ^ 1) - odd
        return (to, y) if 0 <= to < count else (x, y ^ 1)

    return swap(value, partner)


def swap_y(value, odd):
    count = lax.axis_size("gy")
    return swap(value, lambda x, y: (x, (((y + odd) ^ 1) - odd) % count))


def place(axis):
    index, count = lax.axis_index(axis), lax.axis_size(axis)
    odd = lax.rem(index, 2) == 1
    has_low = (index > 0).astype(F32)
    has_high = (index < count - 1).astype(F32)
    return odd, has_low, has_high


def z_sum(value):
    lane = lax.broadcasted_iota(jnp.int32, value.shape, 1)
    last = value.shape[1] - 1
    below = jnp.where(lane > 0, pltpu.roll(value, 1, 1), 0.0)
    above = jnp.where(lane < last, pltpu.roll(value, last, 1), 0.0)
    return below + above


def pack_kernel(cond, resid, x_even, x_odd, y_even, y_odd, tiles, sem):
    layers, rows, lanes = cond.shape
    odd = lax.rem(lax.axis_index("gx"), 2)
    x_copies, y_copies = [], []
    for out, high in ((x_even, 1 - odd), (x_odd, odd)):
        two = pl.ds(high * (layers - 2), 2)
        one = pl.ds(high * (layers - 1), 1)
        x_copies.append((cond.at[two], out.at[pl.ds(0, 2)]))
        x_copies.append((resid.at[one], out.at[pl.ds(2, 1)]))
    for side, start in enumerate((0, rows - HALO)):
        for part, source in enumerate((cond, resid)):
            y_copies.append((source.at[:, pl.ds(start, HALO)], tiles.at[side, part]))
    started = [
        pltpu.make_async_copy(source, target, sem.at[i])
        for i, (source, target) in enumerate(y_copies + x_copies)
    ]
    for copy in started:
        copy.start()
    for copy in started[:4]:
        copy.wait()
    odd = lax.rem(lax.axis_index("gy"), 2) == 1
    first = lax.broadcasted_iota(jnp.int32, (HALO, lanes), 0) < 3
    for k in range(layers):
        low = jnp.where(first, tiles[0, 0, k], pltpu.roll(tiles[0, 1, k], 3, 0))
        high = jnp.where(
            first, pltpu.roll(tiles[1, 0, k], 3, 0), pltpu.roll(tiles[1, 1, k], 5, 0)
        )
        y_even[k] = jnp.where(odd, low, high)
        y_odd[k] = jnp.where(odd, high, low)
    for copy in started[4:]:
        copy.wait()


def pack(cond, resid):
    layers, rows, lanes = cond.shape
    x_out, y_out = shape(3, rows, lanes), shape(layers, HALO, lanes)
    return pl.pallas_call(
        pack_kernel,
        out_shape=(x_out, x_out, y_out, y_out),
        in_specs=[HBM, HBM],
        out_specs=(VMEM,) * 4,
        scratch_shapes=[
            pltpu.VMEM((2, 2, layers, HALO, lanes), F32),
            pltpu.SemaphoreType.DMA((8,)),
        ],
        compiler_params=params(2),
        name="pack",
    )(
        pltpu.with_memory_space_constraint(cond, pltpu.HBM),
        pltpu.with_memory_space_constraint(resid, pltpu.HBM),
    )


def load_kernel(cond, resid, after, u, r, sem):
    own = pl.ds(LOW, cond.shape[1])
    copies = [
        pltpu.make_async_copy(source, target.at[:, own], sem.at[i])
        for i, (source, target) in enumerate(((cond, u), (resid, r)))
    ]
    for copy in copies:
        copy.start()
    for copy in copies:
        copy.wait()


def load(cond, resid, after):
    layers, rows, lanes = cond.shape
    grown = shape(layers, rows + 4 * HALO, lanes)
    return pl.pallas_call(
        load_kernel,
        out_shape=(grown, grown),
        in_specs=[HBM, HBM, VMEM],
        out_specs=(VMEM, VMEM),
        scratch_shapes=[pltpu.SemaphoreType.DMA((2,))],
        compiler_params=params(1),
        cost_estimate=pl.CostEstimate(
            flops=1_000_000_000, transcendentals=0, bytes_accessed=4 * cond.size
        ),
        name="load",
    )(
        pltpu.with_memory_space_constraint(cond, pltpu.HBM),
        pltpu.with_memory_space_constraint(resid, pltpu.HBM),
        after,
    )


def y_tiles(y_even, y_odd, layer, part):
    odd, has_low, has_high = place("gy")
    first, second = y_even[layer], y_odd[layer]
    row = lax.broadcasted_iota(jnp.int32, first.shape, 0)
    width = 3 - part
    south = pltpu.roll(jnp.where(odd, first, second), (5, 3)[part], 0)
    north = jnp.where(odd, second, first)
    if part:
        north = pltpu.roll(north, 5, 0)
    south = jnp.where(row >= HALO - width, south, 0.0) * has_low
    north = jnp.where(row < width, north, 0.0) * has_high
    return south, north


def row_chunks(rows):
    total = rows + 2 * HALO
    step = total // 3 if total % 24 == 0 else total
    return [(HALO + i * step, step) for i in range(total // step)]


def own_chunks(rows):
    step = 32 if rows % 32 == 0 else rows
    return [(LOW + i * step, step) for i in range(rows // step)]


def fill_rows(masks, rows):
    _, has_low, has_high = place("gy")
    row = lax.broadcasted_iota(jnp.int32, masks.shape[1:], 0) - LOW
    inside = jnp.where(row < 0, has_low, jnp.where(row >= rows, has_high, 1.0))
    near_low, near_high = row < 2, row >= rows - 2
    count = jnp.where(near_low, 1.0 + has_low, jnp.where(near_high, 1.0 + has_high, 1.0))
    masks[0] = inside
    masks[1] = count
    masks[2] = jnp.where(row == rows - 2, 1.0 / (1.0 + has_high), 1.0)
    masks[3] = jnp.where(row == 1, 1.0 / (1.0 + has_low), 1.0)


def is_plain(start, size, rows):
    return start >= LOW + 2 and start + size <= LOW + rows - 2


def eight(value):
    return jnp.sum(value.reshape(value.shape[0] // 8, 8, value.shape[1]), axis=0)


def fields_kernel(
    u_in, r_in, y_even, y_odd, u, r, inv, v, w, d, masks, t_even, t_odd
):
    layers, rows = u.shape[0], u.shape[1] - 4 * HALO
    fill_rows(masks, rows)
    for k in range(layers):
        for part, target in enumerate((u, r)):
            south, north = y_tiles(y_even, y_odd, k, part)
            target[k, HALO:LOW] = south
            target[k, LOW + rows : LOW + rows + HALO] = north
    for k in range(1, layers - 1):
        for start, size in row_chunks(rows):
            here, down, up = around_rows(start, size)
            mid = u[k, here]
            total = 6.0 * mid + u[k - 1, here] + u[k + 1, here]
            total = total + u[k, down] + u[k, up] + z_sum(mid)
            inverse = 1.0 / jnp.maximum(total, TINY)
            if not is_plain(start, size, rows):
                inverse = inverse * masks[0, here]
            value = 2.0 * r[k, here] * inverse
            d[k, here] = total
            inv[k, here] = inverse
            v[k, here] = value
            w[k, here] = mid * value
    odd = place("gx")[0]
    own, north = slice(LOW, LOW + rows), LOW + rows
    sends = []
    for side in range(2):
        edge, mid = ((0, 1), (layers - 1, layers - 2))[side]
        lines = (
            u[edge, LOW - 1 : LOW],
            u[edge, LOW - 2 : LOW - 1],
            u[mid, LOW - 1 : LOW],
            r[edge, LOW - 1 : LOW],
            u[edge, north : north + 1],
            u[edge, north + 1 : north + 2],
            u[mid, north : north + 1],
            r[edge, north : north + 1],
        )
        term = (u[edge, own] + u[mid, own]) * v[mid, own]
        sends.append((term, jnp.concatenate(lines, axis=0)))
    (t_low, c_low), (t_high, c_high) = sends
    t_even[0:rows] = jnp.where(odd, t_low, t_high)
    t_even[rows : rows + 8] = jnp.where(odd, c_low, c_high)
    t_odd[0:rows] = jnp.where(odd, t_high, t_low)
    t_odd[rows : rows + 8] = jnp.where(odd, c_high, c_low)


def fields(u, r, y_even, y_odd):
    layers, grown, lanes = u.shape
    ext, term = shape(*u.shape), shape(grown - 4 * HALO + 8, lanes)
    outs = (ext,) * 6 + (shape(4, grown, lanes), term, term)
    return pl.pallas_call(
        fields_kernel,
        out_shape=outs,
        in_specs=[VMEM] * 4,
        out_specs=(VMEM,) * len(outs),
        input_output_aliases={0: 0, 1: 1},
        compiler_params=params(4),
        name="fields",
    )(u, r, y_even, y_odd)


def inner_kernel(
    u, r, inv, v, w, d, masks, p_out, i_out, p, sums, ready, scales, partial, q
):
    layers, rows = p_out.shape[0], p_out.shape[1]
    for k in range(2, layers - 2):
        for start, size in row_chunks(rows):
            here, down, up = around_rows(start, size)
            mid = u[k, here]
            total = 2.0 * r[k, here]
            total = total + mid * (v[k - 1, here] + v[k + 1, here] + z_sum(v[k, here]))
            total = total + (w[k - 1, here] + w[k + 1, here] + z_sum(w[k, here]))
            south = mid * v[k, down] + w[k, down]
            north = mid * v[k, up] + w[k, up]
            if is_plain(start, size, rows):
                value = inv[k, here] * (total + south + north)
            else:
                total = total + masks[2, here] * south + masks[3, here] * north
                value = masks[1, here] * inv[k, here] * total
            p[k, here] = value
            q[k, here] = mid * value
    rz = pq = jnp.zeros((8, u.shape[2]), F32)
    for k in range(3, layers - 3):
        for start, size in own_chunks(rows):
            here, down, up = around_rows(start, size)
            mid = p[k, here]
            around = p[k - 1, here] + p[k + 1, here] + p[k, down] + p[k, up] + z_sum(mid)
            scaled = q[k - 1, here] + q[k + 1, here] + q[k, down] + q[k, up]
            scaled = scaled + z_sum(q[k, here])
            image = d[k, here] * mid - u[k, here] * around - scaled
            i_out[k, start - LOW : start - LOW + size] = image
            p_out[k, start - LOW : start - LOW + size] = mid
            rz = rz + eight(r[k, here] * mid)
            pq = pq + eight(mid * image)
    for side in range(2):
        at = side_layers(layers, side)
        twice = side_place(side)[1]
        for start, size in row_chunks(rows):
            here, down, up = around_rows(start, size)
            mid, value, scale = u[at[1], here], v[at[1], here], twice * inv[at[1], here]
            total = 2.0 * r[at[1], here] + mid * z_sum(value) + z_sum(w[at[1], here])
            total = total + (mid + u[at[2], here]) * v[at[2], here] / twice
            south = mid * v[at[1], down] + w[at[1], down]
            north = mid * v[at[1], up] + w[at[1], up]
            if is_plain(start, size, rows):
                total = total + south + north
            else:
                total = total + masks[2, here] * south + masks[3, here] * north
                scale = scale * masks[1, here]
            ready[side, here] = total
            scales[side, here] = scale
            edge = u[at[0], here]
            total = 6.0 * edge + mid + u[at[0], down] + u[at[0], up] + z_sum(edge)
            partial[side, here] = total
        for start, size in own_chunks(rows):
            here, down, up = around_rows(start, size)
            mid = p[at[2], here]
            around = p[at[3], here] + p[at[2], down] + p[at[2], up] + z_sum(mid)
            scaled = q[at[3], here] + q[at[2], down] + q[at[2], up] + z_sum(q[at[2], here])
            image = d[at[2], here] * mid - u[at[2], here] * around - scaled
            i_out[at[2], start - LOW : start - LOW + size] = image
            p_out[at[2], start - LOW : start - LOW + size] = mid
            rz = rz + eight(r[at[2], here] * mid)
    sums[0] = rz
    sums[1] = pq


def inner(*found):
    layers, grown, lanes = found[0].shape
    own = shape(layers, grown - 4 * HALO, lanes)
    face = shape(2, grown, lanes)
    outs = (own, own, shape(layers, grown, lanes), shape(2, 8, lanes), face, face, face)
    return pl.pallas_call(
        inner_kernel,
        out_shape=outs,
        in_specs=[VMEM] * 7,
        out_specs=(VMEM,) * len(outs),
        scratch_shapes=[pltpu.VMEM((layers, grown, lanes), F32)],
        compiler_params=params(4),
        cost_estimate=pl.CostEstimate(
            flops=100_000_000, transcendentals=0, bytes_accessed=1
        ),
        name="inner",
    )(*found)


def around_rows(start, size):
    return (
        slice(start, start + size),
        slice(start - 1, start + size - 1),
        slice(start + 1, start + size + 1),
    )


def side_layers(layers, side):
    return tuple(k if side == 0 else layers - 1 - k for k in range(4))


def side_place(side):
    odd, has_low, has_high = place("gx")
    has = (has_low, has_high)[side]
    pick = jnp.logical_xor(odd, side == 1)

    def arrived(first, second):
        return jnp.where(pick, first, second) * has

    return has, 1.0 + has, arrived


def start_fields(own, near, side, chunk):
    b_u, b_r, partial = own[0], own[1], own[-1]
    u, r, v, w, _, _, d, inv, masks = near
    at = side_layers(b_u.shape[0], side)
    has = side_place(side)[0]
    here, down, up = around_rows(*chunk)
    inside = masks[0, here]
    mid, edge = u[side, 1, here], b_u[at[0], here]
    total = 6.0 * mid + u[side, 0, here] + edge
    total = total + u[side, 1, down] + u[side, 1, up] + z_sum(mid)
    inverse = has * inside / jnp.maximum(total, TINY)
    value = 2.0 * r[side, here] * inverse
    inv[side, 0, here] = inverse
    v[side, 0, here] = value
    w[side, 0, here] = mid * value
    total = partial[side, here] + mid
    inverse = inside / jnp.maximum(total, TINY)
    value = 2.0 * b_r[at[0], here] * inverse
    d[side, here] = total
    inv[side, 1, here] = inverse
    v[side, 1, here] = value
    w[side, 1, here] = edge * value


def precond_fields(own, near, side, chunk, rows, term):
    b_u, b_r, e_v, _, _, _, ready, scales, _ = own
    u, r, v, w, p, q, _, inv, masks = near
    at = side_layers(b_u.shape[0], side)
    twice = side_place(side)[1]
    here, down, up = around_rows(*chunk)
    plain = is_plain(*chunk, rows)

    def finish(mid, total, south, north, inverse, slot):
        scale = twice * inverse
        if plain:
            total = total + south + north
        else:
            total = total + masks[2, here] * south + masks[3, here] * north
            scale = scale * masks[1, here]
        value = scale * total
        p[side, slot, here] = value
        q[side, slot, here] = mid * value
        return scale

    mid = u[side, 1, here]
    total = 2.0 * r[side, here]
    if term is not None:
        total = total + term
    total = total + mid * (v[side, 1, here] + z_sum(v[side, 0, here]))
    total = total + w[side, 1, here] + z_sum(w[side, 0, here])
    south = mid * v[side, 0, down] + w[side, 0, down]
    north = mid * v[side, 0, up] + w[side, 0, up]
    inv[side, 0, here] = finish(mid, total, south, north, inv[side, 0, here], 0)

    mid, next_u = b_u[at[0], here], b_u[at[1], here]
    next_v = e_v[at[1], here]
    total = 2.0 * b_r[at[0], here]
    total = total + mid * (v[side, 0, here] + next_v + z_sum(v[side, 1, here]))
    total = total + w[side, 0, here] + next_u * next_v + z_sum(w[side, 1, here])
    south = mid * v[side, 1, down] + w[side, 1, down]
    north = mid * v[side, 1, up] + w[side, 1, up]
    finish(mid, total, south, north, inv[side, 1, here], 1)

    total = ready[side, here] + next_u * v[side, 1, here] + w[side, 1, here]
    value = scales[side, here] * total
    p[side, 2, here] = value
    q[side, 2, here] = next_u * value


def image_fields(own, near, side, chunk, k, p_out, i_out):
    b_u, b_r, _, _, e_d, e_p = own[:6]
    _, _, _, _, p, q, d, _, _ = near
    at = side_layers(b_u.shape[0], side)
    here, down, up = around_rows(*chunk)
    mid_u = b_u[at[k], here]
    mid, mid_q = p[side, k + 1, here], q[side, k + 1, here]
    near_y = p[side, k + 1, down] + p[side, k + 1, up]
    near_q = q[side, k + 1, down] + q[side, k + 1, up]
    before_p, before_q = p[side, k, here], q[side, k, here]
    if k == 0:
        after_p, after_q = p[side, 2, here], q[side, 2, here]
    else:
        after_p = e_p[at[2], here]
        after_q = b_u[at[2], here] * after_p
    around = before_p + after_p + near_y + z_sum(mid)
    scaled = before_q + after_q + near_q + z_sum(mid_q)
    total = d[side, here] if k == 0 else e_d[at[k], here]
    image = total * mid - mid_u * around - scaled
    out = slice(chunk[0] - LOW, chunk[0] - LOW + chunk[1])
    p_out[at[k], out] = mid
    i_out[at[k], out] = image
    return eight(b_r[at[k], here] * mid), eight(mid * image)


def middle_chunks(rows):
    rest = rows - 2 * HALO
    step = rest // 2 if rest % 16 == 0 else rest
    return [(LOW + HALO + i * step, step) for i in range(rest // step)]


def outer_kernel(
    b_u, b_r, p_in, i_in, e_v, e_i, e_d, e_p, ready, scales, partial, sums, masks,
    x_even, x_odd,
    p_out, i_out, sums_out, *near,
):
    rows = p_in.shape[1]
    near = (*near, masks)
    u, r = near[0], near[1]
    own = (b_u, b_r, e_v, e_i, e_d, e_p, ready, scales, partial)
    whole = slice(LOW, LOW + rows)
    rz, pq = sums[0], sums[1]
    zero = jnp.zeros(rz.shape, F32)
    for side in range(2):
        at = side_layers(b_u.shape[0], side)
        arrived = side_place(side)[2]
        for slot in range(2):
            layer = slot if side == 0 else 1 - slot
            u[side, slot, whole] = arrived(x_even[layer], x_odd[layer])
        r[side, whole] = arrived(x_even[2], x_odd[2])
        for rest in (slice(HALO, LOW), slice(LOW + rows, LOW + rows + HALO)):
            u[side, 0, rest] = zero
            u[side, 1, rest] = zero
            r[side, rest] = zero
        for chunk in row_chunks(rows):
            start_fields(own, near, side, chunk)
        for chunk in row_chunks(rows):
            precond_fields(own, near, side, chunk, rows, None)
        for start, size in own_chunks(rows):
            here, out = slice(start, start + size), slice(start - LOW, start - LOW + size)
            change = (b_u[at[2], here] + b_u[at[1], here]) * near[4][side, 2, here]
            image = i_in[at[2], out] - change
            i_out[at[2], out] = image
            pq = pq + eight(e_p[at[2], here] * image)
        for chunk in middle_chunks(rows):
            add_rz, add_pq = image_fields(own, near, side, chunk, 1, p_out, i_out)
            rz, pq = rz + add_rz, pq + add_pq
            rz = rz + image_fields(own, near, side, chunk, 0, p_out, i_out)[0]
    sums_out[0] = rz
    sums_out[1] = pq


def corner_kernel(
    b_u, b_r, p_in, i_in, e_v, e_i, e_d, e_p, ready, scales, partial, sums, t_even, t_odd,
    masks, *refs,
):
    old, (p_out, i_out, total_out), fields = refs[:8], refs[8:11], refs[11:]
    near = (*fields, masks)
    rows = p_in.shape[1]
    u, r, p, inv = near[0], near[1], near[4], near[7]
    own = (b_u, b_r, e_v, e_i, e_d, e_p, ready, scales, partial)
    rz, pq = sums[0], sums[1]
    zero = jnp.zeros(rz.shape, F32)
    row = lax.broadcasted_iota(jnp.int32, zero.shape, 0)
    low, high = slice(HALO, LOW), slice(LOW + rows, LOW + rows + HALO)
    for side in range(2):
        at = side_layers(b_u.shape[0], side)
        arrived = side_place(side)[2]
        corner = arrived(t_even[rows : rows + 8], t_odd[rows : rows + 8])

        def one(k):
            return jnp.broadcast_to(corner[k : k + 1], zero.shape)

        u[side, 1, low] = jnp.where(row == 7, one(0), jnp.where(row == 6, one(1), 0.0))
        u[side, 0, low] = jnp.where(row == 7, one(2), 0.0)
        r[side, low] = jnp.where(row == 7, one(3), 0.0)
        u[side, 1, high] = jnp.where(row == 0, one(4), jnp.where(row == 1, one(5), 0.0))
        u[side, 0, high] = jnp.where(row == 0, one(6), 0.0)
        r[side, high] = jnp.where(row == 0, one(7), 0.0)
        for band in range(2):
            if band == 0:
                term = [zero, arrived(t_even[0:HALO], t_odd[0:HALO])]
                chunk, tile = (HALO, 2 * HALO), (LOW, HALO)
            else:
                tail = slice(rows - HALO, rows)
                term = [arrived(t_even[tail], t_odd[tail]), zero]
                chunk = (LOW + rows - HALO, 2 * HALO)
                tile = (LOW + rows - HALO, HALO)
            start_fields(own, near, side, chunk)
            precond_fields(own, near, side, chunk, rows, jnp.concatenate(term, axis=0))
            for k in range(2):
                add_rz, add_pq = image_fields(own, near, side, tile, k, p_out, i_out)
                rz, pq = rz + add_rz, pq + add_pq
        for start, size in middle_chunks(rows):
            here = slice(start, start + size)
            out = slice(start - LOW, start - LOW + size)
            change = inv[side, 0, here] * arrived(t_even[out], t_odd[out])
            image = i_in[at[0], out] - (b_u[at[0], here] + u[side, 1, here]) * change
            i_out[at[0], out] = image
            pq = pq + eight(p[side, 1, here] * image)
    lane = lax.broadcasted_iota(jnp.int32, total_out.shape, 1)
    rz, pq = jnp.sum(rz, keepdims=True), jnp.sum(pq, keepdims=True)
    total_out[...] = jnp.where(lane < total_out.shape[1] // 2, rz, pq)


def outer(found, masks, x_even, x_odd):
    layers, rows, lanes = found[2].shape
    grown = rows + 4 * HALO
    full = shape(layers, rows, lanes)
    sizes = ((2, 2), (2,), (2, 2), (2, 2), (2, 3), (2, 3), (2,), (2, 2))
    near = tuple(shape(*size, grown, lanes) for size in sizes)
    return pl.pallas_call(
        outer_kernel,
        out_shape=(full, full, shape(2, 8, lanes), *near),
        in_specs=[VMEM] * 15,
        out_specs=(VMEM,) * (3 + len(near)),
        input_output_aliases={2: 0, 3: 1},
        compiler_params=params(4),
        name="outer",
    )(*found, masks, x_even, x_odd)


def corners(found, first, masks, t_even, t_odd):
    layers, rows, lanes = found[2].shape
    parts = lax.axis_size("gx") * lax.axis_size("gy")
    p, i, sums, *near = first
    u, r, _, _, *inside, _ = found
    full = shape(layers, rows, lanes)
    again = tuple(shape(*field.shape) for field in near)
    return pl.pallas_call(
        corner_kernel,
        out_shape=(full, full, shape(parts, lanes), *again),
        in_specs=[VMEM] * (15 + len(near)),
        out_specs=(VMEM,) * (3 + len(near)),
        input_output_aliases={2: 0, 3: 1, **{15 + k: 3 + k for k in range(len(near))}},
        compiler_params=params(4),
        name="corners",
    )(u, r, p, i, *inside, sums, t_even, t_odd, masks, *near)[:3]


def update_kernel(sums, precond, image, resid, pressure, residual, held, sem):
    total = jnp.sum(sums[...], axis=0, keepdims=True)
    half = total.shape[1] // 2
    half_alpha = total[0:1, 0:1] / total[0:1, half : half + 1]
    alpha = 2.0 * half_alpha
    layers, rows, _ = precond.shape
    own = slice(LOW, LOW + rows)
    step = 4 if layers % 4 == 0 else layers
    started = []
    for start in range(0, layers, step):
        for k in range(start, start + step):
            held[0, k] = alpha * precond[k]
            held[1, k] = resid[k, own] - half_alpha * image[k]
        part = pl.ds(start, step)
        for i, out in enumerate((pressure, residual)):
            copy = pltpu.make_async_copy(
                held.at[i, part], out.at[part], sem.at[i, start // step]
            )
            copy.start()
            started.append(copy)
    for copy in started:
        copy.wait()


def update(sums, precond, image, resid):
    out = shape(*precond.shape)
    return pl.pallas_call(
        update_kernel,
        out_shape=(out, out),
        in_specs=[VMEM] * 4,
        out_specs=(HBM, HBM),
        scratch_shapes=[
            pltpu.VMEM((2, *precond.shape), F32),
            pltpu.SemaphoreType.DMA((2, precond.shape[0])),
        ],
        compiler_params=params(4),
        name="update",
    )(sums, precond, image, resid)


def on_device(right_side, conductivity):
    x_even, x_odd, y_even, y_odd = pack(conductivity, right_side)
    u, r = load(conductivity, right_side, y_even)
    y_even, y_odd = swap_y(y_even, 0), swap_y(y_odd, 1)
    x_even, x_odd = swap_x(x_even, 0), swap_x(x_odd, 1)
    *found, t_even, t_odd = fields(u, r, y_even, y_odd)
    t_even, t_odd = swap_x(t_even, 0), swap_x(t_odd, 1)
    u, r, inv, v, _, d, masks = found
    p_inner, i_inner, p, sums, *faces = inner(*found)
    found = (u, r, p_inner, i_inner, v, inv, d, p, *faces, sums)
    first = outer(found, masks, x_even, x_odd)
    precond, image, sums = corners(found, first, masks, t_even, t_odd)
    sums = lax.all_to_all(sums, ("gx", "gy"), 0, 0, tiled=True)
    return update(sums, precond, image, r)


def solution(mesh):
    in_specs = (P("gx", "gy", None), P("gx", "gy", None))
    out_specs = (P("gx", "gy", None), P("gx", "gy", None))
    return jax.shard_map(
        on_device, mesh=mesh, in_specs=in_specs, out_specs=out_specs, check_vma=False
    )
```

```python
import jax
import jax.numpy as jnp
from jax import lax
from jax.experimental import pallas as pl
from jax.experimental.pallas import tpu as pltpu
from jax.sharding import PartitionSpec as P

F32 = jnp.float32
HALO = 8
LOW = 2 * HALO
TINY = 1e-30
HBM = pl.BlockSpec(memory_space=pltpu.HBM)
VMEM = pl.BlockSpec(memory_space=pltpu.VMEM)


def params(mebibytes):
    return pltpu.CompilerParams(vmem_limit_bytes=mebibytes << 20)


def shape(*dims):
    return jax.ShapeDtypeStruct(dims, F32)


def swap(value, partner):
    count_x, count_y = lax.axis_size("gx"), lax.axis_size("gy")
    pairs = []
    for x in range(count_x):
        for y in range(count_y):
            to_x, to_y = partner(x, y)
            pairs.append((x * count_y + y, to_x * count_y + to_y))
    return lax.ppermute(value, ("gx", "gy"), pairs)


def swap_x(value, odd):
    count = lax.axis_size("gx")

    def partner(x, y):
        to = ((x + odd) ^ 1) - odd
        return (to, y) if 0 <= to < count else (x, y ^ 1)

    return swap(value, partner)


def swap_y(value, odd):
    count = lax.axis_size("gy")
    return swap(value, lambda x, y: (x, (((y + odd) ^ 1) - odd) % count))


def place(axis):
    index, count = lax.axis_index(axis), lax.axis_size(axis)
    odd = lax.rem(index, 2) == 1
    has_low = (index > 0).astype(F32)
    has_high = (index < count - 1).astype(F32)
    return odd, has_low, has_high


def z_sum(value):
    lane = lax.broadcasted_iota(jnp.int32, value.shape, 1)
    last = value.shape[1] - 1
    below = jnp.where(lane > 0, pltpu.roll(value, 1, 1), 0.0)
    above = jnp.where(lane < last, pltpu.roll(value, last, 1), 0.0)
    return below + above


def pack_kernel(cond, resid, x_even, x_odd, y_even, y_odd, tiles, sem):
    layers, rows, lanes = cond.shape
    odd = lax.rem(lax.axis_index("gx"), 2)
    x_copies, y_copies = [], []
    for out, high in ((x_even, 1 - odd), (x_odd, odd)):
        two = pl.ds(high * (layers - 2), 2)
        one = pl.ds(high * (layers - 1), 1)
        x_copies.append((cond.at[two], out.at[pl.ds(0, 2)]))
        x_copies.append((resid.at[one], out.at[pl.ds(2, 1)]))
    for side, start in enumerate((0, rows - HALO)):
        for part, source in enumerate((cond, resid)):
            y_copies.append((source.at[:, pl.ds(start, HALO)], tiles.at[side, part]))
    started = [
        pltpu.make_async_copy(source, target, sem.at[i])
        for i, (source, target) in enumerate(y_copies + x_copies)
    ]
    for copy in started:
        copy.start()
    for copy in started[:4]:
        copy.wait()
    odd = lax.rem(lax.axis_index("gy"), 2) == 1
    first = lax.broadcasted_iota(jnp.int32, (HALO, lanes), 0) < 3
    for k in range(layers):
        low = jnp.where(first, tiles[0, 0, k], pltpu.roll(tiles[0, 1, k], 3, 0))
        high = jnp.where(
            first, pltpu.roll(tiles[1, 0, k], 3, 0), pltpu.roll(tiles[1, 1, k], 5, 0)
        )
        y_even[k] = jnp.where(odd, low, high)
        y_odd[k] = jnp.where(odd, high, low)
    for copy in started[4:]:
        copy.wait()


def pack(cond, resid):
    layers, rows, lanes = cond.shape
    x_out, y_out = shape(3, rows, lanes), shape(layers, HALO, lanes)
    return pl.pallas_call(
        pack_kernel,
        out_shape=(x_out, x_out, y_out, y_out),
        in_specs=[HBM, HBM],
        out_specs=(VMEM,) * 4,
        scratch_shapes=[
            pltpu.VMEM((2, 2, layers, HALO, lanes), F32),
            pltpu.SemaphoreType.DMA((8,)),
        ],
        compiler_params=params(2),
        name="pack",
    )(
        pltpu.with_memory_space_constraint(cond, pltpu.HBM),
        pltpu.with_memory_space_constraint(resid, pltpu.HBM),
    )


def load_kernel(cond, resid, after, u, r, sem):
    own = pl.ds(LOW, cond.shape[1])
    copies = [
        pltpu.make_async_copy(source, target.at[:, own], sem.at[i])
        for i, (source, target) in enumerate(((cond, u), (resid, r)))
    ]
    for copy in copies:
        copy.start()
    for copy in copies:
        copy.wait()


def load(cond, resid, after):
    layers, rows, lanes = cond.shape
    grown = shape(layers, rows + 4 * HALO, lanes)
    return pl.pallas_call(
        load_kernel,
        out_shape=(grown, grown),
        in_specs=[HBM, HBM, VMEM],
        out_specs=(VMEM, VMEM),
        scratch_shapes=[pltpu.SemaphoreType.DMA((2,))],
        compiler_params=params(1),
        cost_estimate=pl.CostEstimate(
            flops=1_000_000_000, transcendentals=0, bytes_accessed=4 * cond.size
        ),
        name="load",
    )(
        pltpu.with_memory_space_constraint(cond, pltpu.HBM),
        pltpu.with_memory_space_constraint(resid, pltpu.HBM),
        after,
    )


def y_tiles(y_even, y_odd, layer, part):
    odd, has_low, has_high = place("gy")
    first, second = y_even[layer], y_odd[layer]
    row = lax.broadcasted_iota(jnp.int32, first.shape, 0)
    width = 3 - part
    south = pltpu.roll(jnp.where(odd, first, second), (5, 3)[part], 0)
    north = jnp.where(odd, second, first)
    if part:
        north = pltpu.roll(north, 5, 0)
    south = jnp.where(row >= HALO - width, south, 0.0) * has_low
    north = jnp.where(row < width, north, 0.0) * has_high
    return south, north


def row_chunks(rows):
    total = rows + 2 * HALO
    step = total // 3 if total % 24 == 0 else total
    return [(HALO + i * step, step) for i in range(total // step)]


def own_chunks(rows):
    step = 32 if rows % 32 == 0 else rows
    return [(LOW + i * step, step) for i in range(rows // step)]


def fill_rows(masks, rows):
    _, has_low, has_high = place("gy")
    row = lax.broadcasted_iota(jnp.int32, masks.shape[1:], 0) - LOW
    inside = jnp.where(row < 0, has_low, jnp.where(row >= rows, has_high, 1.0))
    near_low, near_high = row < 2, row >= rows - 2
    count = jnp.where(near_low, 1.0 + has_low, jnp.where(near_high, 1.0 + has_high, 1.0))
    masks[0] = inside
    masks[1] = count
    masks[2] = jnp.where(row == rows - 2, 1.0 / (1.0 + has_high), 1.0)
    masks[3] = jnp.where(row == 1, 1.0 / (1.0 + has_low), 1.0)


def is_plain(start, size, rows):
    return start >= LOW + 2 and start + size <= LOW + rows - 2


def eight(value):
    return jnp.sum(value.reshape(value.shape[0] // 8, 8, value.shape[1]), axis=0)


def fields_kernel(
    u_in, r_in, y_even, y_odd, u, r, inv, v, w, d, masks, t_even, t_odd
):
    layers, rows = u.shape[0], u.shape[1] - 4 * HALO
    fill_rows(masks, rows)
    for k in range(layers):
        for part, target in enumerate((u, r)):
            south, north = y_tiles(y_even, y_odd, k, part)
            target[k, HALO:LOW] = south
            target[k, LOW + rows : LOW + rows + HALO] = north
    for k in range(1, layers - 1):
        for start, size in row_chunks(rows):
            here, down, up = around_rows(start, size)
            mid = u[k, here]
            total = 6.0 * mid + u[k - 1, here] + u[k + 1, here]
            total = total + u[k, down] + u[k, up] + z_sum(mid)
            inverse = 1.0 / jnp.maximum(total, TINY)
            if not is_plain(start, size, rows):
                inverse = inverse * masks[0, here]
            value = 2.0 * r[k, here] * inverse
            d[k, here] = total
            inv[k, here] = inverse
            v[k, here] = value
            w[k, here] = mid * value
    odd = place("gx")[0]
    own, north = slice(LOW, LOW + rows), LOW + rows
    sends = []
    for side in range(2):
        edge, mid = ((0, 1), (layers - 1, layers - 2))[side]
        lines = (
            u[edge, LOW - 1 : LOW],
            u[edge, LOW - 2 : LOW - 1],
            u[mid, LOW - 1 : LOW],
            r[edge, LOW - 1 : LOW],
            u[edge, north : north + 1],
            u[edge, north + 1 : north + 2],
            u[mid, north : north + 1],
            r[edge, north : north + 1],
        )
        term = (u[edge, own] + u[mid, own]) * v[mid, own]
        sends.append((term, jnp.concatenate(lines, axis=0)))
    (t_low, c_low), (t_high, c_high) = sends
    t_even[0:rows] = jnp.where(odd, t_low, t_high)
    t_even[rows : rows + 8] = jnp.where(odd, c_low, c_high)
    t_odd[0:rows] = jnp.where(odd, t_high, t_low)
    t_odd[rows : rows + 8] = jnp.where(odd, c_high, c_low)


def fields(u, r, y_even, y_odd):
    layers, grown, lanes = u.shape
    ext, term = shape(*u.shape), shape(grown - 4 * HALO + 8, lanes)
    outs = (ext,) * 6 + (shape(4, grown, lanes), term, term)
    return pl.pallas_call(
        fields_kernel,
        out_shape=outs,
        in_specs=[VMEM] * 4,
        out_specs=(VMEM,) * len(outs),
        input_output_aliases={0: 0, 1: 1},
        compiler_params=params(4),
        name="fields",
    )(u, r, y_even, y_odd)


def inner_kernel(
    u, r, inv, v, w, d, masks, p_out, i_out, p, sums, ready, scales, partial, q
):
    layers, rows = p_out.shape[0], p_out.shape[1]
    for k in range(2, layers - 2):
        for start, size in row_chunks(rows):
            here, down, up = around_rows(start, size)
            mid = u[k, here]
            total = 2.0 * r[k, here]
            total = total + mid * (v[k - 1, here] + v[k + 1, here] + z_sum(v[k, here]))
            total = total + (w[k - 1, here] + w[k + 1, here] + z_sum(w[k, here]))
            south = mid * v[k, down] + w[k, down]
            north = mid * v[k, up] + w[k, up]
            if is_plain(start, size, rows):
                value = inv[k, here] * (total + south + north)
            else:
                total = total + masks[2, here] * south + masks[3, here] * north
                value = masks[1, here] * inv[k, here] * total
            p[k, here] = value
            q[k, here] = mid * value
    rz = pq = jnp.zeros((8, u.shape[2]), F32)
    for k in range(3, layers - 3):
        for start, size in own_chunks(rows):
            here, down, up = around_rows(start, size)
            mid = p[k, here]
            around = p[k - 1, here] + p[k + 1, here] + p[k, down] + p[k, up] + z_sum(mid)
            scaled = q[k - 1, here] + q[k + 1, here] + q[k, down] + q[k, up]
            scaled = scaled + z_sum(q[k, here])
            image = d[k, here] * mid - u[k, here] * around - scaled
            i_out[k, start - LOW : start - LOW + size] = image
            p_out[k, start - LOW : start - LOW + size] = mid
            rz = rz + eight(r[k, here] * mid)
            pq = pq + eight(mid * image)
    for side in range(2):
        at = side_layers(layers, side)
        twice = side_place(side)[1]
        for start, size in row_chunks(rows):
            here, down, up = around_rows(start, size)
            mid, value, scale = u[at[1], here], v[at[1], here], twice * inv[at[1], here]
            total = 2.0 * r[at[1], here] + mid * z_sum(value) + z_sum(w[at[1], here])
            total = total + (mid + u[at[2], here]) * v[at[2], here] / twice
            south = mid * v[at[1], down] + w[at[1], down]
            north = mid * v[at[1], up] + w[at[1], up]
            if is_plain(start, size, rows):
                total = total + south + north
            else:
                total = total + masks[2, here] * south + masks[3, here] * north
                scale = scale * masks[1, here]
            ready[side, here] = total
            scales[side, here] = scale
            edge = u[at[0], here]
            total = 6.0 * edge + mid + u[at[0], down] + u[at[0], up] + z_sum(edge)
            partial[side, here] = total
        for start, size in own_chunks(rows):
            here, down, up = around_rows(start, size)
            mid = p[at[2], here]
            around = p[at[3], here] + p[at[2], down] + p[at[2], up] + z_sum(mid)
            scaled = q[at[3], here] + q[at[2], down] + q[at[2], up] + z_sum(q[at[2], here])
            image = d[at[2], here] * mid - u[at[2], here] * around - scaled
            i_out[at[2], start - LOW : start - LOW + size] = image
            p_out[at[2], start - LOW : start - LOW + size] = mid
            rz = rz + eight(r[at[2], here] * mid)
    sums[0] = rz
    sums[1] = pq


def inner(*found):
    layers, grown, lanes = found[0].shape
    own = shape(layers, grown - 4 * HALO, lanes)
    face = shape(2, grown, lanes)
    outs = (own, own, shape(layers, grown, lanes), shape(2, 8, lanes), face, face, face)
    return pl.pallas_call(
        inner_kernel,
        out_shape=outs,
        in_specs=[VMEM] * 7,
        out_specs=(VMEM,) * len(outs),
        scratch_shapes=[pltpu.VMEM((layers, grown, lanes), F32)],
        compiler_params=params(4),
        cost_estimate=pl.CostEstimate(
            flops=100_000_000, transcendentals=0, bytes_accessed=1
        ),
        name="inner",
    )(*found)


def around_rows(start, size):
    return (
        slice(start, start + size),
        slice(start - 1, start + size - 1),
        slice(start + 1, start + size + 1),
    )


def side_layers(layers, side):
    return tuple(k if side == 0 else layers - 1 - k for k in range(4))


def side_place(side):
    odd, has_low, has_high = place("gx")
    has = (has_low, has_high)[side]
    pick = jnp.logical_xor(odd, side == 1)

    def arrived(first, second):
        return jnp.where(pick, first, second) * has

    return has, 1.0 + has, arrived


def start_fields(own, near, side, chunk):
    b_u, b_r, partial = own[0], own[1], own[-1]
    u, r, v, w, _, _, d, inv, masks = near
    at = side_layers(b_u.shape[0], side)
    has = side_place(side)[0]
    here, down, up = around_rows(*chunk)
    inside = masks[0, here]
    mid, edge = u[side, 1, here], b_u[at[0], here]
    total = 6.0 * mid + u[side, 0, here] + edge
    total = total + u[side, 1, down] + u[side, 1, up] + z_sum(mid)
    inverse = has * inside / jnp.maximum(total, TINY)
    value = 2.0 * r[side, here] * inverse
    inv[side, 0, here] = inverse
    v[side, 0, here] = value
    w[side, 0, here] = mid * value
    total = partial[side, here] + mid
    inverse = inside / jnp.maximum(total, TINY)
    value = 2.0 * b_r[at[0], here] * inverse
    d[side, here] = total
    inv[side, 1, here] = inverse
    v[side, 1, here] = value
    w[side, 1, here] = edge * value


def precond_fields(own, near, side, chunk, rows, term):
    b_u, b_r, e_v, _, _, _, ready, scales, _ = own
    u, r, v, w, p, q, _, inv, masks = near
    at = side_layers(b_u.shape[0], side)
    twice = side_place(side)[1]
    here, down, up = around_rows(*chunk)
    plain = is_plain(*chunk, rows)

    def finish(mid, total, south, north, inverse, slot):
        scale = twice * inverse
        if plain:
            total = total + south + north
        else:
            total = total + masks[2, here] * south + masks[3, here] * north
            scale = scale * masks[1, here]
        value = scale * total
        p[side, slot, here] = value
        q[side, slot, here] = mid * value
        return scale

    mid = u[side, 1, here]
    total = 2.0 * r[side, here]
    if term is not None:
        total = total + term
    total = total + mid * (v[side, 1, here] + z_sum(v[side, 0, here]))
    total = total + w[side, 1, here] + z_sum(w[side, 0, here])
    south = mid * v[side, 0, down] + w[side, 0, down]
    north = mid * v[side, 0, up] + w[side, 0, up]
    inv[side, 0, here] = finish(mid, total, south, north, inv[side, 0, here], 0)

    mid, next_u = b_u[at[0], here], b_u[at[1], here]
    next_v = e_v[at[1], here]
    total = 2.0 * b_r[at[0], here]
    total = total + mid * (v[side, 0, here] + next_v + z_sum(v[side, 1, here]))
    total = total + w[side, 0, here] + next_u * next_v + z_sum(w[side, 1, here])
    south = mid * v[side, 1, down] + w[side, 1, down]
    north = mid * v[side, 1, up] + w[side, 1, up]
    finish(mid, total, south, north, inv[side, 1, here], 1)

    total = ready[side, here] + next_u * v[side, 1, here] + w[side, 1, here]
    value = scales[side, here] * total
    p[side, 2, here] = value
    q[side, 2, here] = next_u * value


def image_fields(own, near, side, chunk, k, p_out, i_out):
    b_u, b_r, _, _, e_d, e_p = own[:6]
    _, _, _, _, p, q, d, _, _ = near
    at = side_layers(b_u.shape[0], side)
    here, down, up = around_rows(*chunk)
    mid_u = b_u[at[k], here]
    mid, mid_q = p[side, k + 1, here], q[side, k + 1, here]
    near_y = p[side, k + 1, down] + p[side, k + 1, up]
    near_q = q[side, k + 1, down] + q[side, k + 1, up]
    before_p, before_q = p[side, k, here], q[side, k, here]
    if k == 0:
        after_p, after_q = p[side, 2, here], q[side, 2, here]
    else:
        after_p = e_p[at[2], here]
        after_q = b_u[at[2], here] * after_p
    around = before_p + after_p + near_y + z_sum(mid)
    scaled = before_q + after_q + near_q + z_sum(mid_q)
    total = d[side, here] if k == 0 else e_d[at[k], here]
    image = total * mid - mid_u * around - scaled
    out = slice(chunk[0] - LOW, chunk[0] - LOW + chunk[1])
    p_out[at[k], out] = mid
    i_out[at[k], out] = image
    return eight(b_r[at[k], here] * mid), eight(mid * image)


def middle_chunks(rows):
    rest = rows - 2 * HALO
    step = rest // 2 if rest % 16 == 0 else rest
    return [(LOW + HALO + i * step, step) for i in range(rest // step)]


def outer_kernel(
    b_u, b_r, p_in, i_in, e_v, e_i, e_d, e_p, ready, scales, partial, sums, masks,
    x_even, x_odd,
    p_out, i_out, sums_out, *near,
):
    rows = p_in.shape[1]
    near = (*near, masks)
    u, r = near[0], near[1]
    own = (b_u, b_r, e_v, e_i, e_d, e_p, ready, scales, partial)
    whole = slice(LOW, LOW + rows)
    rz, pq = sums[0], sums[1]
    zero = jnp.zeros(rz.shape, F32)
    for side in range(2):
        at = side_layers(b_u.shape[0], side)
        arrived = side_place(side)[2]
        for slot in range(2):
            layer = slot if side == 0 else 1 - slot
            u[side, slot, whole] = arrived(x_even[layer], x_odd[layer])
        r[side, whole] = arrived(x_even[2], x_odd[2])
        for rest in (slice(HALO, LOW), slice(LOW + rows, LOW + rows + HALO)):
            u[side, 0, rest] = zero
            u[side, 1, rest] = zero
            r[side, rest] = zero
        for chunk in row_chunks(rows):
            start_fields(own, near, side, chunk)
        for chunk in row_chunks(rows):
            precond_fields(own, near, side, chunk, rows, None)
        for start, size in own_chunks(rows):
            here, out = slice(start, start + size), slice(start - LOW, start - LOW + size)
            change = (b_u[at[2], here] + b_u[at[1], here]) * near[4][side, 2, here]
            image = i_in[at[2], out] - change
            i_out[at[2], out] = image
            pq = pq + eight(e_p[at[2], here] * image)
        for chunk in middle_chunks(rows):
            add_rz, add_pq = image_fields(own, near, side, chunk, 1, p_out, i_out)
            rz, pq = rz + add_rz, pq + add_pq
            rz = rz + image_fields(own, near, side, chunk, 0, p_out, i_out)[0]
    sums_out[0] = rz
    sums_out[1] = pq


def corner_kernel(
    b_u, b_r, p_in, i_in, e_v, e_i, e_d, e_p, ready, scales, partial, sums, t_even, t_odd,
    masks, *refs,
):
    old, (p_out, i_out, total_out), fields = refs[:8], refs[8:11], refs[11:]
    near = (*fields, masks)
    rows = p_in.shape[1]
    u, r, p, inv = near[0], near[1], near[4], near[7]
    own = (b_u, b_r, e_v, e_i, e_d, e_p, ready, scales, partial)
    rz, pq = sums[0], sums[1]
    zero = jnp.zeros(rz.shape, F32)
    row = lax.broadcasted_iota(jnp.int32, zero.shape, 0)
    low, high = slice(HALO, LOW), slice(LOW + rows, LOW + rows + HALO)
    for side in range(2):
        at = side_layers(b_u.shape[0], side)
        arrived = side_place(side)[2]
        corner = arrived(t_even[rows : rows + 8], t_odd[rows : rows + 8])

        def one(k):
            return jnp.broadcast_to(corner[k : k + 1], zero.shape)

        u[side, 1, low] = jnp.where(row == 7, one(0), jnp.where(row == 6, one(1), 0.0))
        u[side, 0, low] = jnp.where(row == 7, one(2), 0.0)
        r[side, low] = jnp.where(row == 7, one(3), 0.0)
        u[side, 1, high] = jnp.where(row == 0, one(4), jnp.where(row == 1, one(5), 0.0))
        u[side, 0, high] = jnp.where(row == 0, one(6), 0.0)
        r[side, high] = jnp.where(row == 0, one(7), 0.0)
        for band in range(2):
            if band == 0:
                term = [zero, arrived(t_even[0:HALO], t_odd[0:HALO])]
                chunk, tile = (HALO, 2 * HALO), (LOW, HALO)
            else:
                tail = slice(rows - HALO, rows)
                term = [arrived(t_even[tail], t_odd[tail]), zero]
                chunk = (LOW + rows - HALO, 2 * HALO)
                tile = (LOW + rows - HALO, HALO)
            start_fields(own, near, side, chunk)
            precond_fields(own, near, side, chunk, rows, jnp.concatenate(term, axis=0))
            for k in range(2):
                add_rz, add_pq = image_fields(own, near, side, tile, k, p_out, i_out)
                rz, pq = rz + add_rz, pq + add_pq
        for start, size in middle_chunks(rows):
            here = slice(start, start + size)
            out = slice(start - LOW, start - LOW + size)
            change = inv[side, 0, here] * arrived(t_even[out], t_odd[out])
            image = i_in[at[0], out] - (b_u[at[0], here] + u[side, 1, here]) * change
            i_out[at[0], out] = image
            pq = pq + eight(p[side, 1, here] * image)
    lane = lax.broadcasted_iota(jnp.int32, total_out.shape, 1)
    rz, pq = jnp.sum(rz, keepdims=True), jnp.sum(pq, keepdims=True)
    total_out[...] = jnp.where(lane < total_out.shape[1] // 2, rz, pq)


def outer(found, masks, x_even, x_odd):
    layers, rows, lanes = found[2].shape
    grown = rows + 4 * HALO
    full = shape(layers, rows, lanes)
    sizes = ((2, 2), (2,), (2, 2), (2, 2), (2, 3), (2, 3), (2,), (2, 2))
    near = tuple(shape(*size, grown, lanes) for size in sizes)
    return pl.pallas_call(
        outer_kernel,
        out_shape=(full, full, shape(2, 8, lanes), *near),
        in_specs=[VMEM] * 15,
        out_specs=(VMEM,) * (3 + len(near)),
        input_output_aliases={2: 0, 3: 1},
        compiler_params=params(4),
        name="outer",
    )(*found, masks, x_even, x_odd)


def corners(found, first, masks, t_even, t_odd):
    layers, rows, lanes = found[2].shape
    parts = lax.axis_size("gx") * lax.axis_size("gy")
    p, i, sums, *near = first
    u, r, _, _, *inside, _ = found
    full = shape(layers, rows, lanes)
    again = tuple(shape(*field.shape) for field in near)
    return pl.pallas_call(
        corner_kernel,
        out_shape=(full, full, shape(parts, lanes), *again),
        in_specs=[VMEM] * (15 + len(near)),
        out_specs=(VMEM,) * (3 + len(near)),
        input_output_aliases={2: 0, 3: 1, **{15 + k: 3 + k for k in range(len(near))}},
        compiler_params=params(4),
        name="corners",
    )(u, r, p, i, *inside, sums, t_even, t_odd, masks, *near)[:3]


def update_kernel(sums, precond, image, resid, pressure, residual, held, sem):
    total = jnp.sum(sums[...], axis=0, keepdims=True)
    half = total.shape[1] // 2
    other = pltpu.roll(total, half, 1)
    first = lax.broadcasted_iota(jnp.int32, total.shape, 1) < half
    half_alpha = jnp.where(first, total, other) / jnp.where(first, other, total)
    alpha = 2.0 * half_alpha
    layers, rows, _ = precond.shape
    own = slice(LOW, LOW + rows)
    step = 1
    started = []
    for start in range(0, layers, step):
        for k in range(start, start + step):
            held[0, k] = alpha * precond[k]
            held[1, k] = resid[k, own] - half_alpha * image[k]
        part = pl.ds(start, step)
        for i, out in enumerate((pressure, residual)):
            copy = pltpu.make_async_copy(
                held.at[i, part], out.at[part], sem.at[i, start // step]
            )
            copy.start()
            started.append(copy)
    for copy in started:
        copy.wait()


def update(sums, precond, image, resid):
    out = shape(*precond.shape)
    return pl.pallas_call(
        update_kernel,
        out_shape=(out, out),
        in_specs=[VMEM] * 4,
        out_specs=(HBM, HBM),
        scratch_shapes=[
            pltpu.VMEM((2, *precond.shape), F32),
            pltpu.SemaphoreType.DMA((2, precond.shape[0])),
        ],
        compiler_params=params(4),
        name="update",
    )(sums, precond, image, resid)


def on_device(right_side, conductivity):
    x_even, x_odd, y_even, y_odd = pack(conductivity, right_side)
    u, r = load(conductivity, right_side, y_even)
    y_even, y_odd = swap_y(y_even, 0), swap_y(y_odd, 1)
    x_even, x_odd = swap_x(x_even, 0), swap_x(x_odd, 1)
    *found, t_even, t_odd = fields(u, r, y_even, y_odd)
    t_even, t_odd = swap_x(t_even, 0), swap_x(t_odd, 1)
    u, r, inv, v, _, d, masks = found
    p_inner, i_inner, p, sums, *faces = inner(*found)
    found = (u, r, p_inner, i_inner, v, inv, d, p, *faces, sums)
    first = outer(found, masks, x_even, x_odd)
    precond, image, sums = corners(found, first, masks, t_even, t_odd)
    sums = lax.all_to_all(sums, ("gx", "gy"), 0, 0, tiled=True)
    return update(sums, precond, image, r)


def solution(mesh):
    in_specs = (P("gx", "gy", None), P("gx", "gy", None))
    out_specs = (P("gx", "gy", None), P("gx", "gy", None))
    return jax.shard_map(
        on_device, mesh=mesh, in_specs=in_specs, out_specs=out_specs, check_vma=False
    )
```

```python
import jax
import jax.numpy as jnp
from jax import lax
from jax.experimental import pallas as pl
from jax.experimental.pallas import tpu as pltpu
from jax.sharding import PartitionSpec as P

F32 = jnp.float32
HALO = 8
LOW = 2 * HALO
TINY = 1e-30
HBM = pl.BlockSpec(memory_space=pltpu.HBM)
VMEM = pl.BlockSpec(memory_space=pltpu.VMEM)


def params(mebibytes):
    return pltpu.CompilerParams(vmem_limit_bytes=mebibytes << 20)


def shape(*dims):
    return jax.ShapeDtypeStruct(dims, F32)


def swap(value, partner):
    count_x, count_y = lax.axis_size("gx"), lax.axis_size("gy")
    pairs = []
    for x in range(count_x):
        for y in range(count_y):
            to_x, to_y = partner(x, y)
            pairs.append((x * count_y + y, to_x * count_y + to_y))
    return lax.ppermute(value, ("gx", "gy"), pairs)


def swap_x(value, odd):
    count = lax.axis_size("gx")

    def partner(x, y):
        to = ((x + odd) ^ 1) - odd
        return (to, y) if 0 <= to < count else (x, y ^ 1)

    return swap(value, partner)


def swap_y(value, odd):
    count = lax.axis_size("gy")
    return swap(value, lambda x, y: (x, (((y + odd) ^ 1) - odd) % count))


def place(axis):
    index, count = lax.axis_index(axis), lax.axis_size(axis)
    odd = lax.rem(index, 2) == 1
    has_low = (index > 0).astype(F32)
    has_high = (index < count - 1).astype(F32)
    return odd, has_low, has_high


def z_sum(value):
    lane = lax.broadcasted_iota(jnp.int32, value.shape, 1)
    last = value.shape[1] - 1
    below = jnp.where(lane > 0, pltpu.roll(value, 1, 1), 0.0)
    above = jnp.where(lane < last, pltpu.roll(value, last, 1), 0.0)
    return below + above


def pack_kernel(cond, resid, x_even, x_odd, sem):
    layers = cond.shape[0]
    odd = lax.rem(lax.axis_index("gx"), 2)
    copies = []
    for out, high in ((x_even, 1 - odd), (x_odd, odd)):
        two = pl.ds(high * (layers - 2), 2)
        one = pl.ds(high * (layers - 1), 1)
        copies.append((cond.at[two], out.at[pl.ds(0, 2)]))
        copies.append((resid.at[one], out.at[pl.ds(2, 1)]))
    started = [
        pltpu.make_async_copy(source, target, sem.at[i])
        for i, (source, target) in enumerate(copies)
    ]
    for copy in started:
        copy.start()
    for copy in started:
        copy.wait()


def pack(cond, resid):
    out = shape(3, *cond.shape[1:])
    return pl.pallas_call(
        pack_kernel,
        out_shape=(out, out),
        in_specs=[HBM, HBM],
        out_specs=(VMEM, VMEM),
        scratch_shapes=[pltpu.SemaphoreType.DMA((4,))],
        compiler_params=params(1),
        name="pack",
    )(
        pltpu.with_memory_space_constraint(cond, pltpu.HBM),
        pltpu.with_memory_space_constraint(resid, pltpu.HBM),
    )


def pack_y_kernel(cond, resid, after, y_even, y_odd, tiles, sem):
    layers, rows, lanes = cond.shape
    started = []
    for side, start in enumerate((0, rows - HALO)):
        for part, source in enumerate((cond, resid)):
            copy = pltpu.make_async_copy(
                source.at[:, pl.ds(start, HALO)], tiles.at[side, part], sem.at[2 * side + part]
            )
            copy.start()
            started.append(copy)
    for copy in started:
        copy.wait()
    odd = lax.rem(lax.axis_index("gy"), 2) == 1
    first = lax.broadcasted_iota(jnp.int32, (HALO, lanes), 0) < 3
    for k in range(layers):
        low = jnp.where(first, tiles[0, 0, k], pltpu.roll(tiles[0, 1, k], 3, 0))
        high = jnp.where(
            first, pltpu.roll(tiles[1, 0, k], 3, 0), pltpu.roll(tiles[1, 1, k], 5, 0)
        )
        y_even[k] = jnp.where(odd, low, high)
        y_odd[k] = jnp.where(odd, high, low)


def pack_y(cond, resid, after):
    layers, rows, lanes = cond.shape
    out = shape(layers, HALO, lanes)
    return pl.pallas_call(
        pack_y_kernel,
        out_shape=(out, out),
        in_specs=[HBM, HBM, VMEM],
        out_specs=(VMEM, VMEM),
        scratch_shapes=[
            pltpu.VMEM((2, 2, layers, HALO, lanes), F32),
            pltpu.SemaphoreType.DMA((4,)),
        ],
        compiler_params=params(2),
        cost_estimate=pl.CostEstimate(
            flops=1_000_000, transcendentals=0, bytes_accessed=1
        ),
        name="pack_y",
    )(
        pltpu.with_memory_space_constraint(cond, pltpu.HBM),
        pltpu.with_memory_space_constraint(resid, pltpu.HBM),
        after,
    )


def load_kernel(cond, resid, after, u, r, sem):
    own = pl.ds(LOW, cond.shape[1])
    copies = [
        pltpu.make_async_copy(source, target.at[:, own], sem.at[i])
        for i, (source, target) in enumerate(((cond, u), (resid, r)))
    ]
    for copy in copies:
        copy.start()
    for copy in copies:
        copy.wait()


def load(cond, resid, after):
    layers, rows, lanes = cond.shape
    grown = shape(layers, rows + 4 * HALO, lanes)
    return pl.pallas_call(
        load_kernel,
        out_shape=(grown, grown),
        in_specs=[HBM, HBM, VMEM],
        out_specs=(VMEM, VMEM),
        scratch_shapes=[pltpu.SemaphoreType.DMA((2,))],
        compiler_params=params(1),
        cost_estimate=pl.CostEstimate(
            flops=1_000_000_000, transcendentals=0, bytes_accessed=4 * cond.size
        ),
        name="load",
    )(
        pltpu.with_memory_space_constraint(cond, pltpu.HBM),
        pltpu.with_memory_space_constraint(resid, pltpu.HBM),
        after,
    )


def y_tiles(y_even, y_odd, layer, part):
    odd, has_low, has_high = place("gy")
    first, second = y_even[layer], y_odd[layer]
    row = lax.broadcasted_iota(jnp.int32, first.shape, 0)
    width = 3 - part
    south = pltpu.roll(jnp.where(odd, first, second), (5, 3)[part], 0)
    north = jnp.where(odd, second, first)
    if part:
        north = pltpu.roll(north, 5, 0)
    south = jnp.where(row >= HALO - width, south, 0.0) * has_low
    north = jnp.where(row < width, north, 0.0) * has_high
    return south, north


def edge_kernel(u, r, y_even, y_odd, t_even, t_odd, grown):
    layers, rows = u.shape[0], u.shape[1] - 4 * HALO
    odd = place("gx")[0]
    end = HALO + rows
    own = slice(LOW, LOW + rows)
    sends = []
    for side in range(2):
        edge, mid, far = ((0, 1, 2), (layers - 1, layers - 2, layers - 3))[side]
        south, north = y_tiles(y_even, y_odd, mid, 0)
        middle = u[mid, own]
        grown[side, 0:HALO] = south
        grown[side, HALO:end] = middle
        grown[side, end : end + HALO] = north
        total = 6.0 * middle + u[edge, own] + u[far, own] + z_sum(middle)
        total = total + grown[side, HALO - 1 : end - 1] + grown[side, HALO + 1 : end + 1]
        term = (u[edge, own] + middle) * (2.0 * r[mid, own] / total)
        edge_south, edge_north = y_tiles(y_even, y_odd, edge, 0)
        r_south, r_north = y_tiles(y_even, y_odd, edge, 1)
        corner = jnp.concatenate(
            [
                edge_south[HALO - 1 : HALO],
                edge_south[HALO - 2 : HALO - 1],
                south[HALO - 1 : HALO],
                r_south[HALO - 1 : HALO],
                edge_north[0:1],
                edge_north[1:2],
                north[0:1],
                r_north[0:1],
            ],
            axis=0,
        )
        sends.append((term, corner))
    (t_low, c_low), (t_high, c_high) = sends
    t_even[0:rows] = jnp.where(odd, t_low, t_high)
    t_even[rows : rows + 8] = jnp.where(odd, c_low, c_high)
    t_odd[0:rows] = jnp.where(odd, t_high, t_low)
    t_odd[rows : rows + 8] = jnp.where(odd, c_high, c_low)


def edge_terms(u, r, y_even, y_odd):
    rows, lanes = u.shape[1] - 4 * HALO, u.shape[2]
    return pl.pallas_call(
        edge_kernel,
        out_shape=(shape(rows + 8, lanes), shape(rows + 8, lanes)),
        in_specs=[VMEM] * 4,
        out_specs=(VMEM, VMEM),
        scratch_shapes=[pltpu.VMEM((2, rows + 2 * HALO, lanes), F32)],
        compiler_params=params(2),
        name="edge_terms",
    )(u, r, y_even, y_odd)


def row_chunks(rows):
    total = rows + 2 * HALO
    step = total // 3 if total % 24 == 0 else total
    return [(HALO + i * step, step) for i in range(total // step)]


def own_chunks(rows):
    step = 32 if rows % 32 == 0 else rows
    return [(LOW + i * step, step) for i in range(rows // step)]


def fill_rows(masks, rows):
    _, has_low, has_high = place("gy")
    row = lax.broadcasted_iota(jnp.int32, masks.shape[1:], 0) - LOW
    inside = jnp.where(row < 0, has_low, jnp.where(row >= rows, has_high, 1.0))
    near_low, near_high = row < 2, row >= rows - 2
    count = jnp.where(near_low, 1.0 + has_low, jnp.where(near_high, 1.0 + has_high, 1.0))
    masks[0] = inside
    masks[1] = count
    masks[2] = jnp.where(row == rows - 2, 1.0 / (1.0 + has_high), 1.0)
    masks[3] = jnp.where(row == 1, 1.0 / (1.0 + has_low), 1.0)


def is_plain(start, size, rows):
    return start >= LOW + 2 and start + size <= LOW + rows - 2


def eight(value):
    return jnp.sum(value.reshape(value.shape[0] // 8, 8, value.shape[1]), axis=0)


def fields_kernel(
    u_in, r_in, y_even, y_odd, u, r, inv, v, w, d, masks
):
    layers, rows = u.shape[0], u.shape[1] - 4 * HALO
    fill_rows(masks, rows)
    for k in range(layers):
        for part, target in enumerate((u, r)):
            south, north = y_tiles(y_even, y_odd, k, part)
            target[k, HALO:LOW] = south
            target[k, LOW + rows : LOW + rows + HALO] = north
    for k in range(1, layers - 1):
        for start, size in row_chunks(rows):
            here, down, up = around_rows(start, size)
            mid = u[k, here]
            total = 6.0 * mid + u[k - 1, here] + u[k + 1, here]
            total = total + u[k, down] + u[k, up] + z_sum(mid)
            inverse = 1.0 / jnp.maximum(total, TINY)
            if not is_plain(start, size, rows):
                inverse = inverse * masks[0, here]
            value = 2.0 * r[k, here] * inverse
            d[k, here] = total
            inv[k, here] = inverse
            v[k, here] = value
            w[k, here] = mid * value


def fields(u, r, y_even, y_odd):
    layers, grown, lanes = u.shape
    outs = (shape(*u.shape),) * 6 + (shape(4, grown, lanes),)
    return pl.pallas_call(
        fields_kernel,
        out_shape=outs,
        in_specs=[VMEM] * 4,
        out_specs=(VMEM,) * len(outs),
        input_output_aliases={0: 0, 1: 1},
        compiler_params=params(4),
        name="fields",
    )(u, r, y_even, y_odd)


def inner_kernel(
    u, r, inv, v, w, d, masks, p_out, i_out, p, sums, ready, scales, partial, q
):
    layers, rows = p_out.shape[0], p_out.shape[1]
    for k in range(2, layers - 2):
        for start, size in row_chunks(rows):
            here, down, up = around_rows(start, size)
            mid = u[k, here]
            total = 2.0 * r[k, here]
            total = total + mid * (v[k - 1, here] + v[k + 1, here] + z_sum(v[k, here]))
            total = total + (w[k - 1, here] + w[k + 1, here] + z_sum(w[k, here]))
            south = mid * v[k, down] + w[k, down]
            north = mid * v[k, up] + w[k, up]
            if is_plain(start, size, rows):
                value = inv[k, here] * (total + south + north)
            else:
                total = total + masks[2, here] * south + masks[3, here] * north
                value = masks[1, here] * inv[k, here] * total
            p[k, here] = value
            q[k, here] = mid * value
    rz = pq = jnp.zeros((8, u.shape[2]), F32)
    for k in range(3, layers - 3):
        for start, size in own_chunks(rows):
            here, down, up = around_rows(start, size)
            mid = p[k, here]
            around = p[k - 1, here] + p[k + 1, here] + p[k, down] + p[k, up] + z_sum(mid)
            scaled = q[k - 1, here] + q[k + 1, here] + q[k, down] + q[k, up]
            scaled = scaled + z_sum(q[k, here])
            image = d[k, here] * mid - u[k, here] * around - scaled
            i_out[k, start - LOW : start - LOW + size] = image
            p_out[k, start - LOW : start - LOW + size] = mid
            rz = rz + eight(r[k, here] * mid)
            pq = pq + eight(mid * image)
    for side in range(2):
        at = side_layers(layers, side)
        twice = side_place(side)[1]
        for start, size in row_chunks(rows):
            here, down, up = around_rows(start, size)
            mid, value, scale = u[at[1], here], v[at[1], here], twice * inv[at[1], here]
            total = 2.0 * r[at[1], here] + mid * z_sum(value) + z_sum(w[at[1], here])
            total = total + (mid + u[at[2], here]) * v[at[2], here] / twice
            south = mid * v[at[1], down] + w[at[1], down]
            north = mid * v[at[1], up] + w[at[1], up]
            if is_plain(start, size, rows):
                total = total + south + north
            else:
                total = total + masks[2, here] * south + masks[3, here] * north
                scale = scale * masks[1, here]
            ready[side, here] = total
            scales[side, here] = scale
            edge = u[at[0], here]
            total = 6.0 * edge + mid + u[at[0], down] + u[at[0], up] + z_sum(edge)
            partial[side, here] = total
        for start, size in own_chunks(rows):
            here, down, up = around_rows(start, size)
            mid = p[at[2], here]
            around = p[at[3], here] + p[at[2], down] + p[at[2], up] + z_sum(mid)
            scaled = q[at[3], here] + q[at[2], down] + q[at[2], up] + z_sum(q[at[2], here])
            image = d[at[2], here] * mid - u[at[2], here] * around - scaled
            i_out[at[2], start - LOW : start - LOW + size] = image
            p_out[at[2], start - LOW : start - LOW + size] = mid
            rz = rz + eight(r[at[2], here] * mid)
    sums[0] = rz
    sums[1] = pq


def inner(*found):
    layers, grown, lanes = found[0].shape
    own = shape(layers, grown - 4 * HALO, lanes)
    face = shape(2, grown, lanes)
    outs = (own, own, shape(layers, grown, lanes), shape(2, 8, lanes), face, face, face)
    return pl.pallas_call(
        inner_kernel,
        out_shape=outs,
        in_specs=[VMEM] * 7,
        out_specs=(VMEM,) * len(outs),
        scratch_shapes=[pltpu.VMEM((layers, grown, lanes), F32)],
        compiler_params=params(4),
        cost_estimate=pl.CostEstimate(
            flops=100_000_000, transcendentals=0, bytes_accessed=1
        ),
        name="inner",
    )(*found)


def around_rows(start, size):
    return (
        slice(start, start + size),
        slice(start - 1, start + size - 1),
        slice(start + 1, start + size + 1),
    )


def side_layers(layers, side):
    return tuple(k if side == 0 else layers - 1 - k for k in range(4))


def side_place(side):
    odd, has_low, has_high = place("gx")
    has = (has_low, has_high)[side]
    pick = jnp.logical_xor(odd, side == 1)

    def arrived(first, second):
        return jnp.where(pick, first, second) * has

    return has, 1.0 + has, arrived


def start_fields(own, near, side, chunk):
    b_u, b_r, partial = own[0], own[1], own[-1]
    u, r, v, w, _, _, d, inv, masks = near
    at = side_layers(b_u.shape[0], side)
    has = side_place(side)[0]
    here, down, up = around_rows(*chunk)
    inside = masks[0, here]
    mid, edge = u[side, 1, here], b_u[at[0], here]
    total = 6.0 * mid + u[side, 0, here] + edge
    total = total + u[side, 1, down] + u[side, 1, up] + z_sum(mid)
    inverse = has * inside / jnp.maximum(total, TINY)
    value = 2.0 * r[side, here] * inverse
    inv[side, 0, here] = inverse
    v[side, 0, here] = value
    w[side, 0, here] = mid * value
    total = partial[side, here] + mid
    inverse = inside / jnp.maximum(total, TINY)
    value = 2.0 * b_r[at[0], here] * inverse
    d[side, here] = total
    inv[side, 1, here] = inverse
    v[side, 1, here] = value
    w[side, 1, here] = edge * value


def precond_fields(own, near, side, chunk, rows, term):
    b_u, b_r, e_v, _, _, _, ready, scales, _ = own
    u, r, v, w, p, q, _, inv, masks = near
    at = side_layers(b_u.shape[0], side)
    twice = side_place(side)[1]
    here, down, up = around_rows(*chunk)
    plain = is_plain(*chunk, rows)

    def finish(mid, total, south, north, inverse, slot):
        scale = twice * inverse
        if plain:
            total = total + south + north
        else:
            total = total + masks[2, here] * south + masks[3, here] * north
            scale = scale * masks[1, here]
        value = scale * total
        p[side, slot, here] = value
        q[side, slot, here] = mid * value
        return scale

    mid = u[side, 1, here]
    total = 2.0 * r[side, here]
    if term is not None:
        total = total + term
    total = total + mid * (v[side, 1, here] + z_sum(v[side, 0, here]))
    total = total + w[side, 1, here] + z_sum(w[side, 0, here])
    south = mid * v[side, 0, down] + w[side, 0, down]
    north = mid * v[side, 0, up] + w[side, 0, up]
    inv[side, 0, here] = finish(mid, total, south, north, inv[side, 0, here], 0)

    mid, next_u = b_u[at[0], here], b_u[at[1], here]
    next_v = e_v[at[1], here]
    total = 2.0 * b_r[at[0], here]
    total = total + mid * (v[side, 0, here] + next_v + z_sum(v[side, 1, here]))
    total = total + w[side, 0, here] + next_u * next_v + z_sum(w[side, 1, here])
    south = mid * v[side, 1, down] + w[side, 1, down]
    north = mid * v[side, 1, up] + w[side, 1, up]
    finish(mid, total, south, north, inv[side, 1, here], 1)

    total = ready[side, here] + next_u * v[side, 1, here] + w[side, 1, here]
    value = scales[side, here] * total
    p[side, 2, here] = value
    q[side, 2, here] = next_u * value


def image_fields(own, near, side, chunk, k, p_out, i_out):
    b_u, b_r, _, _, e_d, e_p = own[:6]
    _, _, _, _, p, q, d, _, _ = near
    at = side_layers(b_u.shape[0], side)
    here, down, up = around_rows(*chunk)
    mid_u = b_u[at[k], here]
    mid, mid_q = p[side, k + 1, here], q[side, k + 1, here]
    near_y = p[side, k + 1, down] + p[side, k + 1, up]
    near_q = q[side, k + 1, down] + q[side, k + 1, up]
    before_p, before_q = p[side, k, here], q[side, k, here]
    if k == 0:
        after_p, after_q = p[side, 2, here], q[side, 2, here]
    else:
        after_p = e_p[at[2], here]
        after_q = b_u[at[2], here] * after_p
    around = before_p + after_p + near_y + z_sum(mid)
    scaled = before_q + after_q + near_q + z_sum(mid_q)
    total = d[side, here] if k == 0 else e_d[at[k], here]
    image = total * mid - mid_u * around - scaled
    out = slice(chunk[0] - LOW, chunk[0] - LOW + chunk[1])
    p_out[at[k], out] = mid
    i_out[at[k], out] = image
    return eight(b_r[at[k], here] * mid), eight(mid * image)


def middle_chunks(rows):
    rest = rows - 2 * HALO
    step = rest // 2 if rest % 16 == 0 else rest
    return [(LOW + HALO + i * step, step) for i in range(rest // step)]


def outer_kernel(
    b_u, b_r, p_in, i_in, e_v, e_i, e_d, e_p, ready, scales, partial, sums, masks,
    x_even, x_odd,
    p_out, i_out, sums_out, *near,
):
    rows = p_in.shape[1]
    near = (*near, masks)
    u, r = near[0], near[1]
    own = (b_u, b_r, e_v, e_i, e_d, e_p, ready, scales, partial)
    whole = slice(LOW, LOW + rows)
    rz, pq = sums[0], sums[1]
    zero = jnp.zeros(rz.shape, F32)
    for side in range(2):
        at = side_layers(b_u.shape[0], side)
        arrived = side_place(side)[2]
        for slot in range(2):
            layer = slot if side == 0 else 1 - slot
            u[side, slot, whole] = arrived(x_even[layer], x_odd[layer])
        r[side, whole] = arrived(x_even[2], x_odd[2])
        for rest in (slice(HALO, LOW), slice(LOW + rows, LOW + rows + HALO)):
            u[side, 0, rest] = zero
            u[side, 1, rest] = zero
            r[side, rest] = zero
        for chunk in row_chunks(rows):
            start_fields(own, near, side, chunk)
        for chunk in row_chunks(rows):
            precond_fields(own, near, side, chunk, rows, None)
        for start, size in own_chunks(rows):
            here, out = slice(start, start + size), slice(start - LOW, start - LOW + size)
            change = (b_u[at[2], here] + b_u[at[1], here]) * near[4][side, 2, here]
            image = i_in[at[2], out] - change
            i_out[at[2], out] = image
            pq = pq + eight(e_p[at[2], here] * image)
        for chunk in middle_chunks(rows):
            add_rz, add_pq = image_fields(own, near, side, chunk, 1, p_out, i_out)
            rz, pq = rz + add_rz, pq + add_pq
            rz = rz + image_fields(own, near, side, chunk, 0, p_out, i_out)[0]
    sums_out[0] = rz
    sums_out[1] = pq


def corner_kernel(
    b_u, b_r, p_in, i_in, e_v, e_i, e_d, e_p, ready, scales, partial, sums, t_even, t_odd,
    masks, *refs,
):
    old, (p_out, i_out, total_out), fields = refs[:8], refs[8:11], refs[11:]
    near = (*fields, masks)
    rows = p_in.shape[1]
    u, r, p, inv = near[0], near[1], near[4], near[7]
    own = (b_u, b_r, e_v, e_i, e_d, e_p, ready, scales, partial)
    rz, pq = sums[0], sums[1]
    zero = jnp.zeros(rz.shape, F32)
    row = lax.broadcasted_iota(jnp.int32, zero.shape, 0)
    low, high = slice(HALO, LOW), slice(LOW + rows, LOW + rows + HALO)
    for side in range(2):
        at = side_layers(b_u.shape[0], side)
        arrived = side_place(side)[2]
        corner = arrived(t_even[rows : rows + 8], t_odd[rows : rows + 8])

        def one(k):
            return jnp.broadcast_to(corner[k : k + 1], zero.shape)

        u[side, 1, low] = jnp.where(row == 7, one(0), jnp.where(row == 6, one(1), 0.0))
        u[side, 0, low] = jnp.where(row == 7, one(2), 0.0)
        r[side, low] = jnp.where(row == 7, one(3), 0.0)
        u[side, 1, high] = jnp.where(row == 0, one(4), jnp.where(row == 1, one(5), 0.0))
        u[side, 0, high] = jnp.where(row == 0, one(6), 0.0)
        r[side, high] = jnp.where(row == 0, one(7), 0.0)
        for band in range(2):
            if band == 0:
                term = [zero, arrived(t_even[0:HALO], t_odd[0:HALO])]
                chunk, tile = (HALO, 2 * HALO), (LOW, HALO)
            else:
                tail = slice(rows - HALO, rows)
                term = [arrived(t_even[tail], t_odd[tail]), zero]
                chunk = (LOW + rows - HALO, 2 * HALO)
                tile = (LOW + rows - HALO, HALO)
            start_fields(own, near, side, chunk)
            precond_fields(own, near, side, chunk, rows, jnp.concatenate(term, axis=0))
            for k in range(2):
                add_rz, add_pq = image_fields(own, near, side, tile, k, p_out, i_out)
                rz, pq = rz + add_rz, pq + add_pq
        for start, size in middle_chunks(rows):
            here = slice(start, start + size)
            out = slice(start - LOW, start - LOW + size)
            change = inv[side, 0, here] * arrived(t_even[out], t_odd[out])
            image = i_in[at[0], out] - (b_u[at[0], here] + u[side, 1, here]) * change
            i_out[at[0], out] = image
            pq = pq + eight(p[side, 1, here] * image)
    lane = lax.broadcasted_iota(jnp.int32, total_out.shape, 1)
    rz, pq = jnp.sum(rz, keepdims=True), jnp.sum(pq, keepdims=True)
    total_out[...] = jnp.where(lane < total_out.shape[1] // 2, rz, pq)


def outer(found, masks, x_even, x_odd):
    layers, rows, lanes = found[2].shape
    grown = rows + 4 * HALO
    full = shape(layers, rows, lanes)
    sizes = ((2, 2), (2,), (2, 2), (2, 2), (2, 3), (2, 3), (2,), (2, 2))
    near = tuple(shape(*size, grown, lanes) for size in sizes)
    return pl.pallas_call(
        outer_kernel,
        out_shape=(full, full, shape(2, 8, lanes), *near),
        in_specs=[VMEM] * 15,
        out_specs=(VMEM,) * (3 + len(near)),
        input_output_aliases={2: 0, 3: 1},
        compiler_params=params(4),
        name="outer",
    )(*found, masks, x_even, x_odd)


def corners(found, first, masks, t_even, t_odd):
    layers, rows, lanes = found[2].shape
    parts = lax.axis_size("gx") * lax.axis_size("gy")
    p, i, sums, *near = first
    u, r, _, _, *inside, _ = found
    full = shape(layers, rows, lanes)
    again = tuple(shape(*field.shape) for field in near)
    return pl.pallas_call(
        corner_kernel,
        out_shape=(full, full, shape(parts, lanes), *again),
        in_specs=[VMEM] * (15 + len(near)),
        out_specs=(VMEM,) * (3 + len(near)),
        input_output_aliases={2: 0, 3: 1, **{15 + k: 3 + k for k in range(len(near))}},
        compiler_params=params(4),
        name="corners",
    )(u, r, p, i, *inside, sums, t_even, t_odd, masks, *near)[:3]


def update_kernel(sums, precond, image, resid, pressure, residual, held, sem):
    total = jnp.sum(sums[...], axis=0, keepdims=True)
    half = total.shape[1] // 2
    other = pltpu.roll(total, half, 1)
    first = lax.broadcasted_iota(jnp.int32, total.shape, 1) < half
    half_alpha = jnp.where(first, total, other) / jnp.where(first, other, total)
    alpha = 2.0 * half_alpha
    layers, rows, _ = precond.shape
    own = slice(LOW, LOW + rows)
    step = 1
    started = []
    for start in range(0, layers, step):
        for k in range(start, start + step):
            held[0, k] = alpha * precond[k]
            held[1, k] = resid[k, own] - half_alpha * image[k]
        part = pl.ds(start, step)
        for i, out in enumerate((pressure, residual)):
            copy = pltpu.make_async_copy(
                held.at[i, part], out.at[part], sem.at[i, start // step]
            )
            copy.start()
            started.append(copy)
    for copy in started:
        copy.wait()


def update(sums, precond, image, resid):
    out = shape(*precond.shape)
    return pl.pallas_call(
        update_kernel,
        out_shape=(out, out),
        in_specs=[VMEM] * 4,
        out_specs=(HBM, HBM),
        scratch_shapes=[
            pltpu.VMEM((2, *precond.shape), F32),
            pltpu.SemaphoreType.DMA((2, precond.shape[0])),
        ],
        compiler_params=params(4),
        name="update",
    )(sums, precond, image, resid)


def on_device(right_side, conductivity):
    x_even, x_odd = pack(conductivity, right_side)
    y_even, y_odd = pack_y(conductivity, right_side, x_odd)
    u, r = load(conductivity, right_side, y_even)
    y_even, y_odd = swap_y(y_even, 0), swap_y(y_odd, 1)
    x_even, x_odd = swap_x(x_even, 0), swap_x(x_odd, 1)
    t_even, t_odd = edge_terms(u, r, y_even, y_odd)
    t_even, t_odd = swap_x(t_even, 0), swap_x(t_odd, 1)
    found = fields(u, r, y_even, y_odd)
    u, r, inv, v, _, d, masks = found
    p_inner, i_inner, p, sums, *faces = inner(*found)
    found = (u, r, p_inner, i_inner, v, inv, d, p, *faces, sums)
    first = outer(found, masks, x_even, x_odd)
    precond, image, sums = corners(found, first, masks, t_even, t_odd)
    sums = lax.all_to_all(sums, ("gx", "gy"), 0, 0, tiled=True)
    return update(sums, precond, image, r)


def solution(mesh):
    in_specs = (P("gx", "gy", None), P("gx", "gy", None))
    out_specs = (P("gx", "gy", None), P("gx", "gy", None))
    return jax.shard_map(
        on_device, mesh=mesh, in_specs=in_specs, out_specs=out_specs, check_vma=False
    )
```
